512 devices in a mesh: prow: 32 (over y, x), pcol: 16 (over z, core).
Axes of the slice: x: 4, y: 8, z: 8, core: 2. Of those that a mesh axis runs over, the one named last changes fastest.
Arguments:
- matrix: bfloat16 [4, 8192, 4, 4096], P(None, 'prow', None, 'pcol'), may hold values from -6 to 6
- pivots: int32 [2, 256], replicated, may hold values from 0 to 32767, as said below
- lower_inverse: bfloat16 [2, 256, 256], replicated, as said below
- upper_inverse: bfloat16 [2, 256, 256], replicated, as said below
Outputs:
- factored: bfloat16 [4, 8192, 4, 4096], P(None, 'prow', None, 'pcol')
The draws below stay inside these ranges and needn't reach their ends.
Inputs may be any that keep to these rules, and one draw needn't show every extreme that they name: For each panel k and each i, pivots[k, i] is either k * 256 + i or a row at or after (k + 1) * 256; entry 0 of each list is k * 256; the rows of one panel's list are distinct, and each list names row 32767. Each lower_inverse[k] is unit lower triangular. Each upper_inverse[k] is upper triangular with positive diagonal.
All inputs are finite; a program needn't handle non-finite values.
Results may differ from the reference program's by a relative error of at most 0.0079.
Values may be sent and summed in bfloat16 or wider, within the bound.
A program may use at most 64 MiB of HBM per device.

```python
import jax
import jax.numpy as jnp
from jax import lax

NB = 256
RB = 4
CB = 4
PANELS = 2
ROWS = 32768
COLS = 16384
N_PROW = 32
N_PCOL = 16


def pivot_lists(key):
    lists = []
    for panel in range(PANELS):
        offset = panel * NB
        below_count = ROWS - offset - NB
        subkey = jax.random.fold_in(key, panel)
        candidate = jax.random.permutation(jax.random.fold_in(subkey, 1), below_count - 1)[:NB] + offset + NB
        place_at = jax.random.randint(jax.random.fold_in(subkey, 2), (), 1, NB)
        candidate = candidate.at[place_at].set(ROWS - 1)
        positions = jnp.arange(NB)
        unmoved = ((jax.random.randint(jax.random.fold_in(subkey, 3), (NB,), 0, 4) == 0) | (positions == 0)) & (positions != place_at)
        lists.append(jnp.where(unmoved, offset + positions, candidate))
    return jnp.stack(lists).astype(jnp.int32)


def draw_pivots(key, part):
    return pivot_lists(key)


def draw_lower_inverse(key, part):
    entries = jax.random.normal(key, (PANELS, NB, NB), jnp.float32)
    entries = entries * (0.5 / NB ** 0.5)
    result = jnp.tril(entries, -1) + jnp.eye(NB, dtype=jnp.float32)[None]
    return result.astype(jnp.bfloat16)


def draw_upper_inverse(key, part):
    first = jax.random.fold_in(key, 11)
    second = jax.random.fold_in(key, 12)
    entries = jax.random.normal(first, (PANELS, NB, NB), jnp.float32)
    diagonal = jax.random.uniform(second, (PANELS, NB), jnp.float32, 0.5, 1.5)
    entries = jnp.triu(entries * (0.5 / NB ** 0.5), 1)
    result = (entries + diagonal[:, :, None] * jnp.eye(NB, dtype=jnp.float32)[None]) * (1.0 / NB ** 0.5)
    return result.astype(jnp.bfloat16)


def block_scale(stream_key, shape, split, low, top_value):
    loudness = 1.0
    for dim, shards_of in split:
        draws = jax.random.uniform(jax.random.fold_in(jax.random.fold_in(stream_key, 6), dim), (shards_of,), jnp.float32, low / len(split), top_value / len(split))
        loudness = loudness * jnp.repeat(jnp.exp(draws), shape[dim] // shards_of).reshape((-1,) + (1,) * (len(shape) - 1 - dim))
    return loudness


def scatter_about(rng, shape, deviation, reach, cuts=(), kind=jnp.bfloat16):
    values = jax.random.normal(rng, shape, jnp.float32) * deviation
    if len(cuts) > 0:
        values = block_scale(rng, shape, cuts, -0.22, 0.18) * values
    return jnp.clip(values, min=-reach, max=reach).astype(kind)


def setup_inputs(seed: int = 0) -> dict:
    streams_of = jax.random.split(jax.random.key(seed), 5)
    return {
        "matrix": scatter_about(streams_of[0], (RB, N_PROW * NB, CB, N_PCOL * NB), 1.0, 6.0, ((1, 32), (3, 16))),
        "pivots": draw_pivots(jax.random.fold_in(streams_of[4], 71), 0),
        "lower_inverse": draw_lower_inverse(jax.random.fold_in(streams_of[4], 71), 0),
        "upper_inverse": draw_upper_inverse(jax.random.fold_in(streams_of[4], 71), 0),
    }


def reference(matrix, pivots, lower_inverse, upper_inverse):
    current = matrix.reshape(ROWS, COLS)
    row_index = jnp.arange(ROWS)
    col_index = jnp.arange(COLS)
    for panel in range(PANELS):
        start = panel * NB
        chosen = pivots[panel]
        old_top = current[start:start + NB]
        incoming = current[chosen]
        current = current.at[chosen].set(old_top)
        current = current.at[start:start + NB].set(incoming)
        lower = jnp.dot(current[:, start:start + NB], upper_inverse[panel], preferred_element_type=jnp.float32).astype(jnp.bfloat16)
        upper = jnp.dot(lower_inverse[panel], current[start:start + NB], preferred_element_type=jnp.float32).astype(jnp.bfloat16)
        row_mask = row_index >= start + NB
        col_mask = col_index >= start + NB

        def update_rows(item):
            block_rows, block_lower, block_mask = item
            product = jnp.dot(block_lower, upper, preferred_element_type=jnp.float32)
            changed = (block_rows.astype(jnp.float32) - product).astype(jnp.bfloat16)
            return jnp.where(block_mask[:, None] & col_mask[None, :], changed, block_rows)

        blocks = lax.map(update_rows, (current.reshape(ROWS // NB, NB, COLS), lower.reshape(ROWS // NB, NB, NB), row_mask.reshape(ROWS // NB, NB)))
        current = blocks.reshape(ROWS, COLS)
        current = current.at[start + NB:, start:start + NB].set(lower[start + NB:])
        current = current.at[start:start + NB, start + NB:].set(upper[:, start + NB:])
    return current.reshape(RB, N_PROW * NB, CB, N_PCOL * NB)
```

```python
import jax
import jax.numpy as jnp
from jax import lax
from jax.sharding import PartitionSpec as P


def spread(block, axis, source):
    block = jnp.where(lax.axis_index(axis) == source, block, jnp.zeros_like(block))
    return lax.psum(block, axis)


def local(matrix, pivots, lower_inverse, upper_inverse):
    row_count = lax.axis_size("prow")
    col_count = lax.axis_size("pcol")
    my_row = lax.axis_index("prow")
    my_col = lax.axis_index("pcol")
    blocks_down, block, blocks_across, _ = matrix.shape
    local_rows = blocks_down * block
    local_cols = blocks_across * block
    current = matrix.reshape(local_rows, local_cols)
    row_place = jnp.arange(local_rows)
    col_place = jnp.arange(local_cols)
    global_rows = (row_place // block * row_count + my_row) * block + row_place % block
    global_cols = (col_place // block * col_count + my_col) * block + col_place % block
    for panel in range(pivots.shape[0]):
        start = panel * block
        chosen = pivots[panel]
        block_row = chosen // block
        is_mine = block_row % row_count == my_row
        local_index = block_row // row_count * block + chosen % block
        safe_index = jnp.where(is_mine, local_index, 0)
        picked = jnp.where(is_mine[:, None], current[safe_index], jnp.zeros((), jnp.bfloat16))
        top_holder = panel % row_count
        top_first = panel // row_count * block
        is_top = my_row == top_holder
        top_local = current[top_first : top_first + block]
        incoming = lax.psum(picked, "prow").astype(jnp.float32)
        old_top = spread(top_local, "prow", top_holder)
        incoming = incoming.astype(jnp.bfloat16)
        target = jnp.where(is_mine, local_index, local_rows)
        current = current.at[target].set(old_top, mode="drop")
        top_now = current[top_first : top_first + block]
        current = current.at[top_first : top_first + block].set(
            jnp.where(is_top, incoming, top_now)
        )
        panel_holder = panel % col_count
        panel_first = panel // col_count * block
        panel_cols = current[:, panel_first : panel_first + block]
        factor = jnp.dot(
            panel_cols, upper_inverse[panel], preferred_element_type=jnp.float32
        ).astype(jnp.bfloat16)
        lower = spread(factor, "pcol", panel_holder)
        upper = jnp.dot(
            lower_inverse[panel], incoming, preferred_element_type=jnp.float32
        ).astype(jnp.bfloat16)
        row_mask = global_rows >= start + block
        col_mask = global_cols >= start + block
        product = jnp.dot(lower, upper, preferred_element_type=jnp.float32)
        changed = (current.astype(jnp.float32) - product).astype(jnp.bfloat16)
        current = jnp.where(row_mask[:, None] & col_mask[None, :], changed, current)
        panel_now = current[:, panel_first : panel_first + block]
        is_panel = my_col == panel_holder
        current = current.at[:, panel_first : panel_first + block].set(
            jnp.where(is_panel & row_mask[:, None], lower, panel_now)
        )
        top_now = current[top_first : top_first + block]
        current = current.at[top_first : top_first + block].set(
            jnp.where(is_top & col_mask[None, :], upper, top_now)
        )
    return current.reshape(matrix.shape)


def solution(mesh):
    in_specs = (P(None, "prow", None, "pcol"), P(), P(), P())
    out_specs = P(None, "prow", None, "pcol")
    return jax.shard_map(local, mesh=mesh, in_specs=in_specs, out_specs=out_specs, check_vma=False)
```

```python
import functools

import jax
import jax.numpy as jnp
from jax import lax
from jax.experimental import pallas as pl
from jax.experimental.pallas import tpu as pltpu
from jax.sharding import PartitionSpec as P

MESH = pl.DeviceIdType.MESH


def sum_kernel(axis, other, n, x_ref, o_ref, recv, gath, ssend, srecv, gsend, grecv):
    me = lax.axis_index(axis)
    them = lax.axis_index(other)

    def dev(j):
        return (j, them) if axis == "prow" else (them, j)

    barrier = pltpu.get_barrier_semaphore()

    def greet(i, c):
        j = lax.rem(me + i, n)
        pl.semaphore_signal(barrier, 1, device_id=dev(j), device_id_type=MESH)
        return c

    lax.fori_loop(1, n, greet, 0)
    pl.semaphore_wait(barrier, n - 1)

    def scatter(j, s):
        return pltpu.make_async_remote_copy(
            src_ref=x_ref.at[j],
            dst_ref=recv.at[s],
            send_sem=ssend.at[j],
            recv_sem=srecv.at[s],
            device_id=dev(j),
            device_id_type=MESH,
        )

    def start_scatter(i, c):
        scatter(lax.rem(me + i, n), me).start()
        return c

    lax.fori_loop(1, n, start_scatter, 0)
    recv[me] = x_ref[me]

    def wait_scatter(i, c):
        scatter(lax.rem(me + n - i, n), lax.rem(me + n - i, n)).wait_recv()
        scatter(lax.rem(me + i, n), me).wait_send()
        return c

    lax.fori_loop(1, n, wait_scatter, 0)

    total = recv[0].astype(jnp.float32)
    for s in range(1, n):
        total = total + recv[s].astype(jnp.float32)
    gath[me] = total.astype(gath.dtype)

    def gather(j, s):
        return pltpu.make_async_remote_copy(
            src_ref=gath.at[s],
            dst_ref=gath.at[s],
            send_sem=gsend.at[j],
            recv_sem=grecv.at[s],
            device_id=dev(j),
            device_id_type=MESH,
        )

    def start_gather(i, c):
        gather(lax.rem(me + i, n), me).start()
        return c

    lax.fori_loop(1, n, start_gather, 0)

    def wait_gather(i, c):
        gather(lax.rem(me + n - i, n), lax.rem(me + n - i, n)).wait_recv()
        gather(lax.rem(me + i, n), me).wait_send()
        return c

    lax.fori_loop(1, n, wait_gather, 0)
    o_ref[...] = gath[...]


def axis_sum(x, axis, other, collective_id):
    n = lax.axis_size(axis)
    chunks = x.reshape(n, x.shape[0] // n, x.shape[1])
    out = pl.pallas_call(
        functools.partial(sum_kernel, axis, other, n),
        out_shape=jax.ShapeDtypeStruct(chunks.shape, chunks.dtype),
        in_specs=[pl.BlockSpec(memory_space=pltpu.VMEM)],
        out_specs=pl.BlockSpec(memory_space=pltpu.VMEM),
        scratch_shapes=[
            pltpu.VMEM(chunks.shape, chunks.dtype),
            pltpu.VMEM(chunks.shape, chunks.dtype),
            pltpu.SemaphoreType.DMA((n,)),
            pltpu.SemaphoreType.DMA((n,)),
            pltpu.SemaphoreType.DMA((n,)),
            pltpu.SemaphoreType.DMA((n,)),
        ],
        compiler_params=pltpu.CompilerParams(
            collective_id=collective_id, has_side_effects=True
        ),
    )(chunks)
    return out.reshape(x.shape)


def local(matrix, pivots, lower_inverse, upper_inverse):
    row_count = lax.axis_size("prow")
    col_count = lax.axis_size("pcol")
    my_row = lax.axis_index("prow")
    my_col = lax.axis_index("pcol")
    blocks_down, block, blocks_across, _ = matrix.shape
    local_rows = blocks_down * block
    local_cols = blocks_across * block
    current = matrix.reshape(local_rows, local_cols)
    row_place = jnp.arange(local_rows)
    col_place = jnp.arange(local_cols)
    global_rows = (row_place // block * row_count + my_row) * block + row_place % block
    global_cols = (col_place // block * col_count + my_col) * block + col_place % block
    for panel in range(pivots.shape[0]):
        start = panel * block
        chosen = pivots[panel]
        block_row = chosen // block
        is_mine = block_row % row_count == my_row
        local_index = block_row // row_count * block + chosen % block
        safe_index = jnp.where(is_mine, local_index, 0)
        picked = jnp.where(is_mine[:, None], current[safe_index], jnp.zeros((), jnp.bfloat16))
        top_holder = panel % row_count
        top_first = panel // row_count * block
        is_top = my_row == top_holder
        top_local = current[top_first : top_first + block]
        top_part = jnp.where(is_top, top_local, jnp.zeros((), jnp.bfloat16))
        both = axis_sum(jnp.concatenate([picked, top_part], axis=0), "prow", "pcol", 0)
        incoming = both[:block]
        old_top = both[block:]
        target = jnp.where(is_mine, local_index, local_rows)
        current = current.at[target].set(old_top, mode="drop")
        top_now = current[top_first : top_first + block]
        current = current.at[top_first : top_first + block].set(
            jnp.where(is_top, incoming, top_now)
        )
        panel_holder = panel % col_count
        panel_first = panel // col_count * block
        panel_cols = current[:, panel_first : panel_first + block]
        factor = jnp.dot(
            panel_cols, upper_inverse[panel], preferred_element_type=jnp.float32
        ).astype(jnp.bfloat16)
        is_panel = my_col == panel_holder
        factor = jnp.where(is_panel, factor, jnp.zeros((), jnp.bfloat16))
        lower = axis_sum(factor, "pcol", "prow", 1)
        upper = jnp.dot(
            lower_inverse[panel], incoming, preferred_element_type=jnp.float32
        ).astype(jnp.bfloat16)
        row_mask = global_rows >= start + block
        col_mask = global_cols >= start + block
        product = jnp.dot(lower, upper, preferred_element_type=jnp.float32)
        changed = (current.astype(jnp.float32) - product).astype(jnp.bfloat16)
        current = jnp.where(row_mask[:, None] & col_mask[None, :], changed, current)
        panel_now = current[:, panel_first : panel_first + block]
        current = current.at[:, panel_first : panel_first + block].set(
            jnp.where(is_panel & row_mask[:, None], lower, panel_now)
        )
        top_now = current[top_first : top_first + block]
        current = current.at[top_first : top_first + block].set(
            jnp.where(is_top & col_mask[None, :], upper, top_now)
        )
    return current.reshape(matrix.shape)


def solution(mesh):
    in_specs = (P(None, "prow", None, "pcol"), P(), P(), P())
    out_specs = P(None, "prow", None, "pcol")
    return jax.shard_map(local, mesh=mesh, in_specs=in_specs, out_specs=out_specs, check_vma=False)
```

```python
import functools

import jax
import jax.numpy as jnp
from jax import lax
from jax.experimental import pallas as pl
from jax.experimental.pallas import tpu as pltpu
from jax.sharding import PartitionSpec as P

MESH = pl.DeviceIdType.MESH


def sum_kernel(axis, other, n, summed, source, x_ref, o_ref, recv, gath, ssend, srecv,
               bsend, brecv, gsend, grecv):
    me = lax.axis_index(axis)
    them = lax.axis_index(other)

    def dev(j):
        return (j, them) if axis == "prow" else (them, j)

    barrier = pltpu.get_barrier_semaphore()

    def greet(i, c):
        j = lax.rem(me + i, n)
        pl.semaphore_signal(barrier, 1, device_id=dev(j), device_id_type=MESH)
        return c

    lax.fori_loop(1, n, greet, 0)
    pl.semaphore_wait(barrier, n - 1)

    def scatter(j, s):
        return pltpu.make_async_remote_copy(
            src_ref=x_ref.at[j],
            dst_ref=recv.at[s],
            send_sem=ssend.at[j],
            recv_sem=srecv.at[s],
            device_id=dev(j),
            device_id_type=MESH,
        )

    def spread(j):
        return pltpu.make_async_remote_copy(
            src_ref=x_ref.at[j],
            dst_ref=gath.at[j],
            send_sem=bsend.at[j],
            recv_sem=brecv.at[0],
            device_id=dev(j),
            device_id_type=MESH,
        )

    if summed > 0:
        def start_scatter(i, c):
            j = lax.rem(me + i, n)

            @pl.when(j < summed)
            def _():
                scatter(j, me).start()

            return c

        lax.fori_loop(1, n, start_scatter, 0)

    if summed < n:
        @pl.when(me == source)
        def _():
            def start_spread(i, c):
                j = lax.rem(me + i, n)

                @pl.when(j >= summed)
                def _():
                    spread(j).start()

                return c

            lax.fori_loop(1, n, start_spread, 0)
            if source >= summed:
                gath[source] = x_ref[source]

    if summed > 0:
        @pl.when(me < summed)
        def _():
            recv[me] = x_ref[me]

            def wait_scatter(i, c):
                s = lax.rem(me + n - i, n)
                scatter(s, s).wait_recv()
                return c

            lax.fori_loop(1, n, wait_scatter, 0)
            total = recv[0].astype(jnp.float32)
            for s in range(1, n):
                total = total + recv[s].astype(jnp.float32)
            gath[me] = total.astype(gath.dtype)

        def wait_scatter_sent(i, c):
            j = lax.rem(me + i, n)

            @pl.when(j < summed)
            def _():
                scatter(j, me).wait_send()

            return c

        lax.fori_loop(1, n, wait_scatter_sent, 0)

    if summed < n:
        @pl.when((me >= summed) & (me != source))
        def _():
            spread(me).wait_recv()

        @pl.when(me == source)
        def _():
            def wait_spread_sent(i, c):
                j = lax.rem(me + i, n)

                @pl.when(j >= summed)
                def _():
                    spread(j).wait_send()

                return c

            lax.fori_loop(1, n, wait_spread_sent, 0)

    def gather(j, s):
        return pltpu.make_async_remote_copy(
            src_ref=gath.at[s],
            dst_ref=gath.at[s],
            send_sem=gsend.at[j],
            recv_sem=grecv.at[s],
            device_id=dev(j),
            device_id_type=MESH,
        )

    def start_gather(i, c):
        gather(lax.rem(me + i, n), me).start()
        return c

    lax.fori_loop(1, n, start_gather, 0)

    def wait_gather(i, c):
        gather(lax.rem(me + n - i, n), lax.rem(me + n - i, n)).wait_recv()
        gather(lax.rem(me + i, n), me).wait_send()
        return c

    lax.fori_loop(1, n, wait_gather, 0)
    o_ref[...] = gath[...]


def axis_sum(x, axis, other, collective_id, summed_rows, source):
    n = lax.axis_size(axis)
    chunks = x.reshape(n, x.shape[0] // n, x.shape[1])
    summed = summed_rows // chunks.shape[1]
    out = pl.pallas_call(
        functools.partial(sum_kernel, axis, other, n, summed, source),
        out_shape=jax.ShapeDtypeStruct(chunks.shape, chunks.dtype),
        in_specs=[pl.BlockSpec(memory_space=pltpu.VMEM)],
        out_specs=pl.BlockSpec(memory_space=pltpu.VMEM),
        scratch_shapes=[
            pltpu.VMEM(chunks.shape, chunks.dtype),
            pltpu.VMEM(chunks.shape, chunks.dtype),
            pltpu.SemaphoreType.DMA((n,)),
            pltpu.SemaphoreType.DMA((n,)),
            pltpu.SemaphoreType.DMA((n,)),
            pltpu.SemaphoreType.DMA((1,)),
            pltpu.SemaphoreType.DMA((n,)),
            pltpu.SemaphoreType.DMA((n,)),
        ],
        compiler_params=pltpu.CompilerParams(
            collective_id=collective_id, has_side_effects=True
        ),
    )(chunks)
    return out.reshape(x.shape)


def local(matrix, pivots, lower_inverse, upper_inverse):
    row_count = lax.axis_size("prow")
    col_count = lax.axis_size("pcol")
    my_row = lax.axis_index("prow")
    my_col = lax.axis_index("pcol")
    blocks_down, block, blocks_across, _ = matrix.shape
    local_rows = blocks_down * block
    local_cols = blocks_across * block
    current = matrix.reshape(local_rows, local_cols)
    row_place = jnp.arange(local_rows)
    col_place = jnp.arange(local_cols)
    global_rows = (row_place // block * row_count + my_row) * block + row_place % block
    global_cols = (col_place // block * col_count + my_col) * block + col_place % block
    for panel in range(pivots.shape[0]):
        start = panel * block
        chosen = pivots[panel]
        block_row = chosen // block
        is_mine = block_row % row_count == my_row
        local_index = block_row // row_count * block + chosen % block
        safe_index = jnp.where(is_mine, local_index, 0)
        picked = jnp.where(is_mine[:, None], current[safe_index], jnp.zeros((), jnp.bfloat16))
        top_holder = panel % row_count
        top_first = panel // row_count * block
        is_top = my_row == top_holder
        top_local = current[top_first : top_first + block]
        top_part = jnp.where(is_top, top_local, jnp.zeros((), jnp.bfloat16))
        both = axis_sum(
            jnp.concatenate([picked, top_part], axis=0), "prow", "pcol", 2 * panel, block, top_holder
        )
        incoming = both[:block]
        old_top = both[block:]
        target = jnp.where(is_mine, local_index, local_rows)
        current = current.at[target].set(old_top, mode="drop")
        top_now = current[top_first : top_first + block]
        current = current.at[top_first : top_first + block].set(
            jnp.where(is_top, incoming, top_now)
        )
        panel_holder = panel % col_count
        panel_first = panel // col_count * block
        panel_cols = current[:, panel_first : panel_first + block]
        factor = jnp.dot(
            panel_cols, upper_inverse[panel], preferred_element_type=jnp.float32
        ).astype(jnp.bfloat16)
        is_panel = my_col == panel_holder
        factor = jnp.where(is_panel, factor, jnp.zeros((), jnp.bfloat16))
        lower = axis_sum(factor, "pcol", "prow", 2 * panel + 1, 0, panel_holder)
        upper = jnp.dot(
            lower_inverse[panel], incoming, preferred_element_type=jnp.float32
        ).astype(jnp.bfloat16)
        row_mask = global_rows >= start + block
        col_mask = global_cols >= start + block
        product = jnp.dot(lower, upper, preferred_element_type=jnp.float32)
        changed = (current.astype(jnp.float32) - product).astype(jnp.bfloat16)
        current = jnp.where(row_mask[:, None] & col_mask[None, :], changed, current)
        panel_now = current[:, panel_first : panel_first + block]
        current = current.at[:, panel_first : panel_first + block].set(
            jnp.where(is_panel & row_mask[:, None], lower, panel_now)
        )
        top_now = current[top_first : top_first + block]
        current = current.at[top_first : top_first + block].set(
            jnp.where(is_top & col_mask[None, :], upper, top_now)
        )
    return current.reshape(matrix.shape)


def solution(mesh):
    in_specs = (P(None, "prow", None, "pcol"), P(), P(), P())
    out_specs = P(None, "prow", None, "pcol")
    return jax.shard_map(local, mesh=mesh, in_specs=in_specs, out_specs=out_specs, check_vma=False)
```

```python
import functools

import jax
import jax.numpy as jnp
from jax import lax
from jax.experimental import pallas as pl
from jax.experimental.pallas import tpu as pltpu
from jax.sharding import PartitionSpec as P

MESH = pl.DeviceIdType.MESH


def sum_kernel(axis, other, n, summed, source, x_ref, o_ref, recv, gath, ssend, srecv,
               bsend, brecv, gsend, grecv):
    me = lax.axis_index(axis)
    them = lax.axis_index(other)

    def dev(j):
        return (j, them) if axis == "prow" else (them, j)

    barrier = pltpu.get_barrier_semaphore()

    def greet(i, c):
        j = lax.rem(me + i, n)
        pl.semaphore_signal(barrier, 1, device_id=dev(j), device_id_type=MESH)
        return c

    lax.fori_loop(1, n, greet, 0)
    pl.semaphore_wait(barrier, n - 1)

    def scatter(j, s):
        return pltpu.make_async_remote_copy(
            src_ref=x_ref.at[j],
            dst_ref=recv.at[s],
            send_sem=ssend.at[j],
            recv_sem=srecv.at[s],
            device_id=dev(j),
            device_id_type=MESH,
        )

    def spread(j):
        return pltpu.make_async_remote_copy(
            src_ref=x_ref.at[j],
            dst_ref=gath.at[j],
            send_sem=bsend.at[j],
            recv_sem=brecv.at[0],
            device_id=dev(j),
            device_id_type=MESH,
        )

    if summed > 0:
        def start_scatter(i, c):
            j = lax.rem(me + i, n)

            @pl.when(j < summed)
            def _():
                scatter(j, me).start()

            return c

        lax.fori_loop(1, n, start_scatter, 0)

    if summed < n:
        @pl.when(me == source)
        def _():
            def start_spread(i, c):
                j = lax.rem(me + i, n)

                @pl.when(j >= summed)
                def _():
                    spread(j).start()

                return c

            lax.fori_loop(1, n, start_spread, 0)
            if source >= summed:
                gath[source] = x_ref[source]

    if summed > 0:
        @pl.when(me < summed)
        def _():
            recv[me] = x_ref[me]

            def wait_scatter(i, c):
                s = lax.rem(me + n - i, n)
                scatter(s, s).wait_recv()
                return c

            lax.fori_loop(1, n, wait_scatter, 0)
            total = recv[0].astype(jnp.float32)
            for s in range(1, n):
                total = total + recv[s].astype(jnp.float32)
            gath[me] = total.astype(gath.dtype)

        def wait_scatter_sent(i, c):
            j = lax.rem(me + i, n)

            @pl.when(j < summed)
            def _():
                scatter(j, me).wait_send()

            return c

        lax.fori_loop(1, n, wait_scatter_sent, 0)

    if summed < n:
        @pl.when((me >= summed) & (me != source))
        def _():
            spread(me).wait_recv()

        @pl.when(me == source)
        def _():
            def wait_spread_sent(i, c):
                j = lax.rem(me + i, n)

                @pl.when(j >= summed)
                def _():
                    spread(j).wait_send()

                return c

            lax.fori_loop(1, n, wait_spread_sent, 0)

    def gather(j, s):
        return pltpu.make_async_remote_copy(
            src_ref=gath.at[s],
            dst_ref=gath.at[s],
            send_sem=gsend.at[j],
            recv_sem=grecv.at[s],
            device_id=dev(j),
            device_id_type=MESH,
        )

    def start_gather(i, c):
        gather(lax.rem(me + i, n), me).start()
        return c

    lax.fori_loop(1, n, start_gather, 0)

    def wait_gather(i, c):
        gather(lax.rem(me + n - i, n), lax.rem(me + n - i, n)).wait_recv()
        gather(lax.rem(me + i, n), me).wait_send()
        return c

    lax.fori_loop(1, n, wait_gather, 0)
    o_ref[...] = gath[...]


def axis_sum(x, axis, other, collective_id, summed_rows, source):
    n = lax.axis_size(axis)
    chunks = x.reshape(n, x.shape[0] // n, x.shape[1])
    summed = summed_rows // chunks.shape[1]
    out = pl.pallas_call(
        functools.partial(sum_kernel, axis, other, n, summed, source),
        out_shape=jax.ShapeDtypeStruct(chunks.shape, chunks.dtype),
        in_specs=[pl.BlockSpec(memory_space=pltpu.VMEM)],
        out_specs=pl.BlockSpec(memory_space=pltpu.VMEM),
        scratch_shapes=[
            pltpu.VMEM(chunks.shape, chunks.dtype),
            pltpu.VMEM(chunks.shape, chunks.dtype),
            pltpu.SemaphoreType.DMA((n,)),
            pltpu.SemaphoreType.DMA((n,)),
            pltpu.SemaphoreType.DMA((n,)),
            pltpu.SemaphoreType.DMA((1,)),
            pltpu.SemaphoreType.DMA((n,)),
            pltpu.SemaphoreType.DMA((n,)),
        ],
        compiler_params=pltpu.CompilerParams(
            collective_id=collective_id, has_side_effects=True
        ),
    )(chunks)
    return out.reshape(x.shape)


def group_kernel(stride, size, mode, x_ref, o_ref, buf, send, recv):
    p = lax.axis_index("prow")
    q = lax.axis_index("pcol")
    me = lax.rem(p // stride, size)
    base = p - me * stride

    def dev(k):
        return (base + k * stride, q)

    barrier = pltpu.get_barrier_semaphore()

    def greet(i, c):
        pl.semaphore_signal(barrier, 1, device_id=dev(lax.rem(me + i, size)), device_id_type=MESH)
        return c

    lax.fori_loop(1, size, greet, 0)
    pl.semaphore_wait(barrier, size - 1)

    def copy(k, s):
        src = x_ref.at[k] if mode == "rs" else buf.at[s]
        return pltpu.make_async_remote_copy(
            src_ref=src,
            dst_ref=buf.at[s],
            send_sem=send.at[k],
            recv_sem=recv.at[s],
            device_id=dev(k),
            device_id_type=MESH,
        )

    if mode == "ag":
        buf[me] = x_ref[...]

    def start(i, c):
        copy(lax.rem(me + i, size), me).start()
        return c

    lax.fori_loop(1, size, start, 0)
    if mode == "rs":
        buf[me] = x_ref[me]

    def wait(i, c):
        s = lax.rem(me + size - i, size)
        copy(s, s).wait_recv()
        copy(lax.rem(me + i, size), me).wait_send()
        return c

    lax.fori_loop(1, size, wait, 0)
    if mode == "rs":
        total = buf[0].astype(jnp.float32)
        for s in range(1, size):
            total = total + buf[s].astype(jnp.float32)
        o_ref[...] = total.astype(o_ref.dtype)
    else:
        o_ref[...] = buf[...]


def group_step(x, stride, size, mode, collective_id):
    if mode == "rs":
        chunks = x.reshape(size, x.shape[0] // size, x.shape[1])
        out_shape = chunks.shape[1:]
        buf_shape = chunks.shape
    else:
        chunks = x
        out_shape = (size,) + x.shape
        buf_shape = out_shape
    out = pl.pallas_call(
        functools.partial(group_kernel, stride, size, mode),
        out_shape=jax.ShapeDtypeStruct(out_shape, x.dtype),
        in_specs=[pl.BlockSpec(memory_space=pltpu.VMEM)],
        out_specs=pl.BlockSpec(memory_space=pltpu.VMEM),
        scratch_shapes=[
            pltpu.VMEM(buf_shape, x.dtype),
            pltpu.SemaphoreType.DMA((size,)),
            pltpu.SemaphoreType.DMA((size,)),
        ],
        compiler_params=pltpu.CompilerParams(
            collective_id=collective_id, has_side_effects=True
        ),
    )(chunks)
    if mode == "ag":
        out = out.reshape(size * x.shape[0], x.shape[1])
    return out


def prow_sum(x, x_devices):
    y_devices = lax.axis_size("prow") // x_devices
    part = group_step(x, 1, x_devices, "rs", 10)
    part = group_step(part, x_devices, y_devices, "rs", 11)
    part = group_step(part, x_devices, y_devices, "ag", 12)
    return group_step(part, 1, x_devices, "ag", 13)


def local(x_devices, matrix, pivots, lower_inverse, upper_inverse):
    row_count = lax.axis_size("prow")
    col_count = lax.axis_size("pcol")
    my_row = lax.axis_index("prow")
    my_col = lax.axis_index("pcol")
    blocks_down, block, blocks_across, _ = matrix.shape
    local_rows = blocks_down * block
    local_cols = blocks_across * block
    current = matrix.reshape(local_rows, local_cols)
    row_place = jnp.arange(local_rows)
    col_place = jnp.arange(local_cols)
    global_rows = (row_place // block * row_count + my_row) * block + row_place % block
    global_cols = (col_place // block * col_count + my_col) * block + col_place % block
    for panel in range(pivots.shape[0]):
        start = panel * block
        chosen = pivots[panel]
        block_row = chosen // block
        is_mine = block_row % row_count == my_row
        local_index = block_row // row_count * block + chosen % block
        safe_index = jnp.where(is_mine, local_index, 0)
        picked = jnp.where(is_mine[:, None], current[safe_index], jnp.zeros((), jnp.bfloat16))
        top_holder = panel % row_count
        top_first = panel // row_count * block
        is_top = my_row == top_holder
        top_local = current[top_first : top_first + block]
        top_part = jnp.where(is_top, top_local, jnp.zeros((), jnp.bfloat16))
        both = prow_sum(jnp.concatenate([picked, top_part], axis=0), x_devices)
        incoming = both[:block]
        old_top = both[block:]
        target = jnp.where(is_mine, local_index, local_rows)
        current = current.at[target].set(old_top, mode="drop")
        top_now = current[top_first : top_first + block]
        current = current.at[top_first : top_first + block].set(
            jnp.where(is_top, incoming, top_now)
        )
        panel_holder = panel % col_count
        panel_first = panel // col_count * block
        panel_cols = current[:, panel_first : panel_first + block]
        factor = jnp.dot(
            panel_cols, upper_inverse[panel], preferred_element_type=jnp.float32
        ).astype(jnp.bfloat16)
        is_panel = my_col == panel_holder
        factor = jnp.where(is_panel, factor, jnp.zeros((), jnp.bfloat16))
        lower = axis_sum(factor, "pcol", "prow", 2 * panel + 1, 0, panel_holder)
        upper = jnp.dot(
            lower_inverse[panel], incoming, preferred_element_type=jnp.float32
        ).astype(jnp.bfloat16)
        row_mask = global_rows >= start + block
        col_mask = global_cols >= start + block
        product = jnp.dot(lower, upper, preferred_element_type=jnp.float32)
        changed = (current.astype(jnp.float32) - product).astype(jnp.bfloat16)
        current = jnp.where(row_mask[:, None] & col_mask[None, :], changed, current)
        panel_now = current[:, panel_first : panel_first + block]
        current = current.at[:, panel_first : panel_first + block].set(
            jnp.where(is_panel & row_mask[:, None], lower, panel_now)
        )
        top_now = current[top_first : top_first + block]
        current = current.at[top_first : top_first + block].set(
            jnp.where(is_top & col_mask[None, :], upper, top_now)
        )
    return current.reshape(matrix.shape)


def solution(mesh):
    x_devices = len({d.coords[0] for d in mesh.devices[:, 0]})
    in_specs = (P(None, "prow", None, "pcol"), P(), P(), P())
    out_specs = P(None, "prow", None, "pcol")
    return jax.shard_map(functools.partial(local, x_devices), mesh=mesh, in_specs=in_specs, out_specs=out_specs, check_vma=False)
```

```python
import functools

import jax
import jax.numpy as jnp
from jax import lax
from jax.experimental import pallas as pl
from jax.experimental.pallas import tpu as pltpu
from jax.sharding import PartitionSpec as P

MESH = pl.DeviceIdType.MESH


def sum_kernel(axis, other, n, summed, source, x_ref, o_ref, recv, gath, ssend, srecv,
               bsend, brecv, gsend, grecv):
    me = lax.axis_index(axis)
    them = lax.axis_index(other)

    def dev(j):
        return (j, them) if axis == "prow" else (them, j)

    barrier = pltpu.get_barrier_semaphore()

    def greet(i, c):
        j = lax.rem(me + i, n)
        pl.semaphore_signal(barrier, 1, device_id=dev(j), device_id_type=MESH)
        return c

    lax.fori_loop(1, n, greet, 0)
    pl.semaphore_wait(barrier, n - 1)

    def scatter(j, s):
        return pltpu.make_async_remote_copy(
            src_ref=x_ref.at[j],
            dst_ref=recv.at[s],
            send_sem=ssend.at[j],
            recv_sem=srecv.at[s],
            device_id=dev(j),
            device_id_type=MESH,
        )

    def spread(j):
        return pltpu.make_async_remote_copy(
            src_ref=x_ref.at[j],
            dst_ref=gath.at[j],
            send_sem=bsend.at[j],
            recv_sem=brecv.at[0],
            device_id=dev(j),
            device_id_type=MESH,
        )

    if summed > 0:
        def start_scatter(i, c):
            j = lax.rem(me + i, n)

            @pl.when(j < summed)
            def _():
                scatter(j, me).start()

            return c

        lax.fori_loop(1, n, start_scatter, 0)

    if summed < n:
        @pl.when(me == source)
        def _():
            def start_spread(i, c):
                j = lax.rem(me + i, n)

                @pl.when(j >= summed)
                def _():
                    spread(j).start()

                return c

            lax.fori_loop(1, n, start_spread, 0)
            if source >= summed:
                gath[source] = x_ref[source]

    if summed > 0:
        @pl.when(me < summed)
        def _():
            recv[me] = x_ref[me]

            def wait_scatter(i, c):
                s = lax.rem(me + n - i, n)
                scatter(s, s).wait_recv()
                return c

            lax.fori_loop(1, n, wait_scatter, 0)
            total = recv[0].astype(jnp.float32)
            for s in range(1, n):
                total = total + recv[s].astype(jnp.float32)
            gath[me] = total.astype(gath.dtype)

        def wait_scatter_sent(i, c):
            j = lax.rem(me + i, n)

            @pl.when(j < summed)
            def _():
                scatter(j, me).wait_send()

            return c

        lax.fori_loop(1, n, wait_scatter_sent, 0)

    if summed < n:
        @pl.when((me >= summed) & (me != source))
        def _():
            spread(me).wait_recv()

        @pl.when(me == source)
        def _():
            def wait_spread_sent(i, c):
                j = lax.rem(me + i, n)

                @pl.when(j >= summed)
                def _():
                    spread(j).wait_send()

                return c

            lax.fori_loop(1, n, wait_spread_sent, 0)

    def gather(j, s):
        return pltpu.make_async_remote_copy(
            src_ref=gath.at[s],
            dst_ref=gath.at[s],
            send_sem=gsend.at[j],
            recv_sem=grecv.at[s],
            device_id=dev(j),
            device_id_type=MESH,
        )

    def start_gather(i, c):
        gather(lax.rem(me + i, n), me).start()
        return c

    lax.fori_loop(1, n, start_gather, 0)

    def wait_gather(i, c):
        gather(lax.rem(me + n - i, n), lax.rem(me + n - i, n)).wait_recv()
        gather(lax.rem(me + i, n), me).wait_send()
        return c

    lax.fori_loop(1, n, wait_gather, 0)
    o_ref[...] = gath[...]


def axis_sum(x, axis, other, collective_id, summed_rows, source):
    n = lax.axis_size(axis)
    chunks = x.reshape(n, x.shape[0] // n, x.shape[1])
    summed = summed_rows // chunks.shape[1]
    out = pl.pallas_call(
        functools.partial(sum_kernel, axis, other, n, summed, source),
        out_shape=jax.ShapeDtypeStruct(chunks.shape, chunks.dtype),
        in_specs=[pl.BlockSpec(memory_space=pltpu.VMEM)],
        out_specs=pl.BlockSpec(memory_space=pltpu.VMEM),
        scratch_shapes=[
            pltpu.VMEM(chunks.shape, chunks.dtype),
            pltpu.VMEM(chunks.shape, chunks.dtype),
            pltpu.SemaphoreType.DMA((n,)),
            pltpu.SemaphoreType.DMA((n,)),
            pltpu.SemaphoreType.DMA((n,)),
            pltpu.SemaphoreType.DMA((1,)),
            pltpu.SemaphoreType.DMA((n,)),
            pltpu.SemaphoreType.DMA((n,)),
        ],
        compiler_params=pltpu.CompilerParams(
            collective_id=collective_id, has_side_effects=True
        ),
    )(chunks)
    return out.reshape(x.shape)


def group_kernel(stride, size, mode, x_ref, o_ref, buf, send, recv):
    p = lax.axis_index("prow")
    q = lax.axis_index("pcol")
    me = lax.rem(p // stride, size)
    base = p - me * stride

    def dev(k):
        return (base + k * stride, q)

    barrier = pltpu.get_barrier_semaphore()

    def greet(i, c):
        pl.semaphore_signal(barrier, 1, device_id=dev(lax.rem(me + i, size)), device_id_type=MESH)
        return c

    lax.fori_loop(1, size, greet, 0)
    pl.semaphore_wait(barrier, size - 1)

    def copy(k, s):
        src = x_ref.at[k] if mode == "rs" else buf.at[s]
        return pltpu.make_async_remote_copy(
            src_ref=src,
            dst_ref=buf.at[s],
            send_sem=send.at[k],
            recv_sem=recv.at[s],
            device_id=dev(k),
            device_id_type=MESH,
        )

    if mode == "ag":
        buf[me] = x_ref[...]

    def start(i, c):
        copy(lax.rem(me + i, size), me).start()
        return c

    lax.fori_loop(1, size, start, 0)
    if mode == "rs":
        buf[me] = x_ref[me]

    def wait(i, c):
        s = lax.rem(me + size - i, size)
        copy(s, s).wait_recv()
        copy(lax.rem(me + i, size), me).wait_send()
        return c

    lax.fori_loop(1, size, wait, 0)
    if mode == "rs":
        total = buf[0].astype(jnp.float32)
        for s in range(1, size):
            total = total + buf[s].astype(jnp.float32)
        o_ref[...] = total.astype(o_ref.dtype)
    else:
        o_ref[...] = buf[...]


def group_step(x, stride, size, mode, collective_id):
    if mode == "rs":
        chunks = x.reshape(size, x.shape[0] // size, x.shape[1])
        out_shape = chunks.shape[1:]
        buf_shape = chunks.shape
    else:
        chunks = x
        out_shape = (size,) + x.shape
        buf_shape = out_shape
    out = pl.pallas_call(
        functools.partial(group_kernel, stride, size, mode),
        out_shape=jax.ShapeDtypeStruct(out_shape, x.dtype),
        in_specs=[pl.BlockSpec(memory_space=pltpu.VMEM)],
        out_specs=pl.BlockSpec(memory_space=pltpu.VMEM),
        scratch_shapes=[
            pltpu.VMEM(buf_shape, x.dtype),
            pltpu.SemaphoreType.DMA((size,)),
            pltpu.SemaphoreType.DMA((size,)),
        ],
        compiler_params=pltpu.CompilerParams(
            collective_id=collective_id, has_side_effects=True
        ),
    )(chunks)
    if mode == "ag":
        out = out.reshape(size * x.shape[0], x.shape[1])
    return out


def prow_kernel(xd, yd, x_ref, o_ref, b1, a2, b2, b3, b4, sends, recvs):
    p = lax.axis_index("prow")
    q = lax.axis_index("pcol")
    xi = lax.rem(p, xd)
    yi = p // xd

    def xdev(k):
        return (yi * xd + k, q)

    def ydev(k):
        return (k * xd + xi, q)

    barrier = pltpu.get_barrier_semaphore()

    def greet_x(i, c):
        pl.semaphore_signal(barrier, 1, device_id=xdev(lax.rem(xi + i, xd)), device_id_type=MESH)
        return c

    def greet_y(i, c):
        pl.semaphore_signal(barrier, 1, device_id=ydev(lax.rem(yi + i, yd)), device_id_type=MESH)
        return c

    lax.fori_loop(1, xd, greet_x, 0)
    lax.fori_loop(1, yd, greet_y, 0)
    pl.semaphore_wait(barrier, xd + yd - 2)

    def exchange(phase, src, dst, me, size, dev):
        def copy(k, s):
            return pltpu.make_async_remote_copy(
                src_ref=src(k, s),
                dst_ref=dst.at[s],
                send_sem=sends.at[phase, k],
                recv_sem=recvs.at[phase, s],
                device_id=dev(k),
                device_id_type=MESH,
            )

        def start(i, c):
            copy(lax.rem(me + i, size), me).start()
            return c

        lax.fori_loop(1, size, start, 0)

        def wait(i, c):
            s = lax.rem(me + size - i, size)
            copy(s, s).wait_recv()
            copy(lax.rem(me + i, size), me).wait_send()
            return c

        lax.fori_loop(1, size, wait, 0)

    def total(buf, size):
        acc = buf[0].astype(jnp.float32)
        for s in range(1, size):
            acc = acc + buf[s].astype(jnp.float32)
        return acc

    exchange(0, lambda k, s: x_ref.at[k], b1, xi, xd, xdev)
    b1[xi] = x_ref[xi]
    a2[...] = total(b1, xd).astype(a2.dtype).reshape(a2.shape)
    exchange(1, lambda k, s: a2.at[k], b2, yi, yd, ydev)
    b2[yi] = a2[yi]
    b3[yi] = total(b2, yd).astype(b3.dtype)
    exchange(2, lambda k, s: b3.at[s], b3, yi, yd, ydev)
    b4[xi] = b3[...].reshape(b4.shape[1:])
    exchange(3, lambda k, s: b4.at[s], b4, xi, xd, xdev)
    o_ref[...] = b4[...]


def prow_sum(x, xd):
    yd = lax.axis_size("prow") // xd
    rows, cols = x.shape
    chunks = x.reshape(xd, rows // xd, cols)
    part = rows // xd // yd
    out = pl.pallas_call(
        functools.partial(prow_kernel, xd, yd),
        out_shape=jax.ShapeDtypeStruct(chunks.shape, x.dtype),
        in_specs=[pl.BlockSpec(memory_space=pltpu.VMEM)],
        out_specs=pl.BlockSpec(memory_space=pltpu.VMEM),
        scratch_shapes=[
            pltpu.VMEM(chunks.shape, x.dtype),
            pltpu.VMEM((yd, part, cols), x.dtype),
            pltpu.VMEM((yd, part, cols), x.dtype),
            pltpu.VMEM((yd, part, cols), x.dtype),
            pltpu.VMEM(chunks.shape, x.dtype),
            pltpu.SemaphoreType.DMA((4, max(xd, yd))),
            pltpu.SemaphoreType.DMA((4, max(xd, yd))),
        ],
        compiler_params=pltpu.CompilerParams(collective_id=10, has_side_effects=True),
    )(chunks)
    return out.reshape(rows, cols)


def local(x_devices, matrix, pivots, lower_inverse, upper_inverse):
    row_count = lax.axis_size("prow")
    col_count = lax.axis_size("pcol")
    my_row = lax.axis_index("prow")
    my_col = lax.axis_index("pcol")
    blocks_down, block, blocks_across, _ = matrix.shape
    local_rows = blocks_down * block
    local_cols = blocks_across * block
    current = matrix.reshape(local_rows, local_cols)
    row_place = jnp.arange(local_rows)
    col_place = jnp.arange(local_cols)
    global_rows = (row_place // block * row_count + my_row) * block + row_place % block
    global_cols = (col_place // block * col_count + my_col) * block + col_place % block
    for panel in range(pivots.shape[0]):
        start = panel * block
        chosen = pivots[panel]
        block_row = chosen // block
        is_mine = block_row % row_count == my_row
        local_index = block_row // row_count * block + chosen % block
        safe_index = jnp.where(is_mine, local_index, 0)
        picked = jnp.where(is_mine[:, None], current[safe_index], jnp.zeros((), jnp.bfloat16))
        top_holder = panel % row_count
        top_first = panel // row_count * block
        is_top = my_row == top_holder
        top_local = current[top_first : top_first + block]
        top_part = jnp.where(is_top, top_local, jnp.zeros((), jnp.bfloat16))
        both = prow_sum(jnp.concatenate([picked, top_part], axis=0), x_devices)
        incoming = both[:block]
        old_top = both[block:]
        target = jnp.where(is_mine, local_index, local_rows)
        current = current.at[target].set(old_top, mode="drop")
        top_now = current[top_first : top_first + block]
        current = current.at[top_first : top_first + block].set(
            jnp.where(is_top, incoming, top_now)
        )
        panel_holder = panel % col_count
        panel_first = panel // col_count * block
        panel_cols = current[:, panel_first : panel_first + block]
        factor = jnp.dot(
            panel_cols, upper_inverse[panel], preferred_element_type=jnp.float32
        ).astype(jnp.bfloat16)
        is_panel = my_col == panel_holder
        factor = jnp.where(is_panel, factor, jnp.zeros((), jnp.bfloat16))
        lower = axis_sum(factor, "pcol", "prow", 2 * panel + 1, 0, panel_holder)
        upper = jnp.dot(
            lower_inverse[panel], incoming, preferred_element_type=jnp.float32
        ).astype(jnp.bfloat16)
        row_mask = global_rows >= start + block
        col_mask = global_cols >= start + block
        product = jnp.dot(lower, upper, preferred_element_type=jnp.float32)
        changed = (current.astype(jnp.float32) - product).astype(jnp.bfloat16)
        current = jnp.where(row_mask[:, None] & col_mask[None, :], changed, current)
        panel_now = current[:, panel_first : panel_first + block]
        current = current.at[:, panel_first : panel_first + block].set(
            jnp.where(is_panel & row_mask[:, None], lower, panel_now)
        )
        top_now = current[top_first : top_first + block]
        current = current.at[top_first : top_first + block].set(
            jnp.where(is_top & col_mask[None, :], upper, top_now)
        )
    return current.reshape(matrix.shape)


def solution(mesh):
    x_devices = len({d.coords[0] for d in mesh.devices[:, 0]})
    in_specs = (P(None, "prow", None, "pcol"), P(), P(), P())
    out_specs = P(None, "prow", None, "pcol")
    return jax.shard_map(functools.partial(local, x_devices), mesh=mesh, in_specs=in_specs, out_specs=out_specs, check_vma=False)
```

```python
import functools

import jax
import jax.numpy as jnp
from jax import lax
from jax.experimental import pallas as pl
from jax.experimental.pallas import tpu as pltpu
from jax.sharding import PartitionSpec as P

MESH = pl.DeviceIdType.MESH


def sum_kernel(axis, other, n, summed, source, x_ref, o_ref, recv, gath, ssend, srecv,
               bsend, brecv, gsend, grecv):
    me = lax.axis_index(axis)
    them = lax.axis_index(other)

    def dev(j):
        return (j, them) if axis == "prow" else (them, j)

    barrier = pltpu.get_barrier_semaphore()

    def greet(i, c):
        j = lax.rem(me + i, n)
        pl.semaphore_signal(barrier, 1, device_id=dev(j), device_id_type=MESH)
        return c

    lax.fori_loop(1, n, greet, 0)
    pl.semaphore_wait(barrier, n - 1)

    def scatter(j, s):
        return pltpu.make_async_remote_copy(
            src_ref=x_ref.at[j],
            dst_ref=recv.at[s],
            send_sem=ssend.at[j],
            recv_sem=srecv.at[s],
            device_id=dev(j),
            device_id_type=MESH,
        )

    def spread(j):
        return pltpu.make_async_remote_copy(
            src_ref=x_ref.at[j],
            dst_ref=gath.at[j],
            send_sem=bsend.at[j],
            recv_sem=brecv.at[0],
            device_id=dev(j),
            device_id_type=MESH,
        )

    if summed > 0:
        def start_scatter(i, c):
            j = lax.rem(me + i, n)

            @pl.when(j < summed)
            def _():
                scatter(j, me).start()

            return c

        lax.fori_loop(1, n, start_scatter, 0)

    if summed < n:
        @pl.when(me == source)
        def _():
            def start_spread(i, c):
                j = lax.rem(me + i, n)

                @pl.when(j >= summed)
                def _():
                    spread(j).start()

                return c

            lax.fori_loop(1, n, start_spread, 0)
            if source >= summed:
                gath[source] = x_ref[source]

    if summed > 0:
        @pl.when(me < summed)
        def _():
            recv[me] = x_ref[me]

            def wait_scatter(i, c):
                s = lax.rem(me + n - i, n)
                scatter(s, s).wait_recv()
                return c

            lax.fori_loop(1, n, wait_scatter, 0)
            total = recv[0].astype(jnp.float32)
            for s in range(1, n):
                total = total + recv[s].astype(jnp.float32)
            gath[me] = total.astype(gath.dtype)

        def wait_scatter_sent(i, c):
            j = lax.rem(me + i, n)

            @pl.when(j < summed)
            def _():
                scatter(j, me).wait_send()

            return c

        lax.fori_loop(1, n, wait_scatter_sent, 0)

    if summed < n:
        @pl.when((me >= summed) & (me != source))
        def _():
            spread(me).wait_recv()

        @pl.when(me == source)
        def _():
            def wait_spread_sent(i, c):
                j = lax.rem(me + i, n)

                @pl.when(j >= summed)
                def _():
                    spread(j).wait_send()

                return c

            lax.fori_loop(1, n, wait_spread_sent, 0)

    def gather(j, s):
        return pltpu.make_async_remote_copy(
            src_ref=gath.at[s],
            dst_ref=gath.at[s],
            send_sem=gsend.at[j],
            recv_sem=grecv.at[s],
            device_id=dev(j),
            device_id_type=MESH,
        )

    def start_gather(i, c):
        gather(lax.rem(me + i, n), me).start()
        return c

    lax.fori_loop(1, n, start_gather, 0)

    def wait_gather(i, c):
        gather(lax.rem(me + n - i, n), lax.rem(me + n - i, n)).wait_recv()
        gather(lax.rem(me + i, n), me).wait_send()
        return c

    lax.fori_loop(1, n, wait_gather, 0)
    o_ref[...] = gath[...]


def axis_sum(x, axis, other, collective_id, summed_rows, source):
    n = lax.axis_size(axis)
    chunks = x.reshape(n, x.shape[0] // n, x.shape[1])
    summed = summed_rows // chunks.shape[1]
    out = pl.pallas_call(
        functools.partial(sum_kernel, axis, other, n, summed, source),
        out_shape=jax.ShapeDtypeStruct(chunks.shape, chunks.dtype),
        in_specs=[pl.BlockSpec(memory_space=pltpu.VMEM)],
        out_specs=pl.BlockSpec(memory_space=pltpu.VMEM),
        scratch_shapes=[
            pltpu.VMEM(chunks.shape, chunks.dtype),
            pltpu.VMEM(chunks.shape, chunks.dtype),
            pltpu.SemaphoreType.DMA((n,)),
            pltpu.SemaphoreType.DMA((n,)),
            pltpu.SemaphoreType.DMA((n,)),
            pltpu.SemaphoreType.DMA((1,)),
            pltpu.SemaphoreType.DMA((n,)),
            pltpu.SemaphoreType.DMA((n,)),
        ],
        compiler_params=pltpu.CompilerParams(
            collective_id=collective_id, has_side_effects=True
        ),
    )(chunks)
    return out.reshape(x.shape)


def group_kernel(stride, size, mode, x_ref, o_ref, buf, send, recv):
    p = lax.axis_index("prow")
    q = lax.axis_index("pcol")
    me = lax.rem(p // stride, size)
    base = p - me * stride

    def dev(k):
        return (base + k * stride, q)

    barrier = pltpu.get_barrier_semaphore()

    def greet(i, c):
        pl.semaphore_signal(barrier, 1, device_id=dev(lax.rem(me + i, size)), device_id_type=MESH)
        return c

    lax.fori_loop(1, size, greet, 0)
    pl.semaphore_wait(barrier, size - 1)

    def copy(k, s):
        src = x_ref.at[k] if mode == "rs" else buf.at[s]
        return pltpu.make_async_remote_copy(
            src_ref=src,
            dst_ref=buf.at[s],
            send_sem=send.at[k],
            recv_sem=recv.at[s],
            device_id=dev(k),
            device_id_type=MESH,
        )

    if mode == "ag":
        buf[me] = x_ref[...]

    def start(i, c):
        copy(lax.rem(me + i, size), me).start()
        return c

    lax.fori_loop(1, size, start, 0)
    if mode == "rs":
        buf[me] = x_ref[me]

    def wait(i, c):
        s = lax.rem(me + size - i, size)
        copy(s, s).wait_recv()
        copy(lax.rem(me + i, size), me).wait_send()
        return c

    lax.fori_loop(1, size, wait, 0)
    if mode == "rs":
        total = buf[0].astype(jnp.float32)
        for s in range(1, size):
            total = total + buf[s].astype(jnp.float32)
        o_ref[...] = total.astype(o_ref.dtype)
    else:
        o_ref[...] = buf[...]


def group_step(x, stride, size, mode, collective_id):
    if mode == "rs":
        chunks = x.reshape(size, x.shape[0] // size, x.shape[1])
        out_shape = chunks.shape[1:]
        buf_shape = chunks.shape
    else:
        chunks = x
        out_shape = (size,) + x.shape
        buf_shape = out_shape
    out = pl.pallas_call(
        functools.partial(group_kernel, stride, size, mode),
        out_shape=jax.ShapeDtypeStruct(out_shape, x.dtype),
        in_specs=[pl.BlockSpec(memory_space=pltpu.VMEM)],
        out_specs=pl.BlockSpec(memory_space=pltpu.VMEM),
        scratch_shapes=[
            pltpu.VMEM(buf_shape, x.dtype),
            pltpu.SemaphoreType.DMA((size,)),
            pltpu.SemaphoreType.DMA((size,)),
        ],
        compiler_params=pltpu.CompilerParams(
            collective_id=collective_id, has_side_effects=True
        ),
    )(chunks)
    if mode == "ag":
        out = out.reshape(size * x.shape[0], x.shape[1])
    return out


def prow_kernel(xd, yd, x_ref, o_ref, b1, a2, b2, b3, b4, sends, recvs):
    p = lax.axis_index("prow")
    q = lax.axis_index("pcol")
    xi = lax.rem(p, xd)
    yi = p // xd

    def xdev(k):
        return (yi * xd + k, q)

    def ydev(k):
        return (k * xd + xi, q)

    barrier = pltpu.get_barrier_semaphore()

    def greet_x(i, c):
        pl.semaphore_signal(barrier, 1, device_id=xdev(lax.rem(xi + i, xd)), device_id_type=MESH)
        return c

    def greet_y(i, c):
        pl.semaphore_signal(barrier, 1, device_id=ydev(lax.rem(yi + i, yd)), device_id_type=MESH)
        return c

    lax.fori_loop(1, xd, greet_x, 0)
    lax.fori_loop(1, yd, greet_y, 0)
    pl.semaphore_wait(barrier, xd + yd - 2)

    def exchange(phase, src, dst, me, size, dev):
        def copy(k, s):
            return pltpu.make_async_remote_copy(
                src_ref=src(k, s),
                dst_ref=dst.at[s],
                send_sem=sends.at[phase, k],
                recv_sem=recvs.at[phase, s],
                device_id=dev(k),
                device_id_type=MESH,
            )

        def start(i, c):
            copy(lax.rem(me + i, size), me).start()
            return c

        lax.fori_loop(1, size, start, 0)

        def wait(i, c):
            s = lax.rem(me + size - i, size)
            copy(s, s).wait_recv()
            copy(lax.rem(me + i, size), me).wait_send()
            return c

        lax.fori_loop(1, size, wait, 0)

    def total(buf, size):
        acc = buf[0].astype(jnp.float32)
        for s in range(1, size):
            acc = acc + buf[s].astype(jnp.float32)
        return acc

    exchange(0, lambda k, s: x_ref.at[k], b1, xi, xd, xdev)
    b1[xi] = x_ref[xi]
    a2[...] = total(b1, xd).astype(a2.dtype).reshape(a2.shape)
    exchange(1, lambda k, s: a2.at[k], b2, yi, yd, ydev)
    b2[yi] = a2[yi]
    b3[yi] = total(b2, yd).astype(b3.dtype)
    exchange(2, lambda k, s: b3.at[s], b3, yi, yd, ydev)
    b4[xi] = b3[...].reshape(b4.shape[1:])
    exchange(3, lambda k, s: b4.at[s], b4, xi, xd, xdev)
    o_ref[...] = b4[...]


def prow_sum(x, xd):
    yd = lax.axis_size("prow") // xd
    rows, cols = x.shape
    chunks = x.reshape(xd, rows // xd, cols)
    part = rows // xd // yd
    out = pl.pallas_call(
        functools.partial(prow_kernel, xd, yd),
        out_shape=jax.ShapeDtypeStruct(chunks.shape, x.dtype),
        in_specs=[pl.BlockSpec(memory_space=pltpu.VMEM)],
        out_specs=pl.BlockSpec(memory_space=pltpu.VMEM),
        scratch_shapes=[
            pltpu.VMEM(chunks.shape, x.dtype),
            pltpu.VMEM((yd, part, cols), x.dtype),
            pltpu.VMEM((yd, part, cols), x.dtype),
            pltpu.VMEM((yd, part, cols), x.dtype),
            pltpu.VMEM(chunks.shape, x.dtype),
            pltpu.SemaphoreType.DMA((4, max(xd, yd))),
            pltpu.SemaphoreType.DMA((4, max(xd, yd))),
        ],
        compiler_params=pltpu.CompilerParams(collective_id=10, has_side_effects=True),
    )(chunks)
    return out.reshape(rows, cols)


def pcol_kernel(nz, source, x_ref, o_ref, g, p1send, p1recv, p2send, p2recv, p3send, p3recv):
    q = lax.axis_index("pcol")
    p = lax.axis_index("prow")
    nc = lax.axis_size("pcol") // nz
    z = q // nc
    c = lax.rem(q, nc)
    zs, cs = source // nc, source % nc

    def dev(zz, cc):
        return (p, zz * nc + cc)

    barrier = pltpu.get_barrier_semaphore()
    n = nz * nc

    def greet(i, carry):
        j = lax.rem(q + i, n)
        pl.semaphore_signal(barrier, 1, device_id=(p, j), device_id_type=MESH)
        return carry

    lax.fori_loop(1, n, greet, 0)
    pl.semaphore_wait(barrier, n - 1)

    def spread(j):
        return pltpu.make_async_remote_copy(
            src_ref=x_ref.at[j],
            dst_ref=g.at[j],
            send_sem=p1send.at[j],
            recv_sem=p1recv.at[0],
            device_id=dev(j, cs),
            device_id_type=MESH,
        )

    def ring(j, s):
        return pltpu.make_async_remote_copy(
            src_ref=g.at[s],
            dst_ref=g.at[s],
            send_sem=p2send.at[j],
            recv_sem=p2recv.at[s],
            device_id=dev(j, cs),
            device_id_type=MESH,
        )

    def partner(zz):
        return pltpu.make_async_remote_copy(
            src_ref=g,
            dst_ref=g,
            send_sem=p3send.at[0],
            recv_sem=p3recv.at[0],
            device_id=dev(zz, 1 - cs),
            device_id_type=MESH,
        )

    @pl.when(q == source)
    def _():
        def start(i, carry):
            spread(lax.rem(zs + i, nz)).start()
            return carry

        lax.fori_loop(1, nz, start, 0)
        g[zs] = x_ref[zs]

        def sent(i, carry):
            spread(lax.rem(zs + i, nz)).wait_send()
            return carry

        lax.fori_loop(1, nz, sent, 0)

    @pl.when((c == cs) & (z != zs))
    def _():
        spread(z).wait_recv()

    @pl.when(c == cs)
    def _():
        def start(i, carry):
            ring(lax.rem(z + i, nz), z).start()
            return carry

        lax.fori_loop(1, nz, start, 0)

        def wait(i, carry):
            s = lax.rem(z + nz - i, nz)
            ring(s, s).wait_recv()
            ring(lax.rem(z + i, nz), z).wait_send()
            return carry

        lax.fori_loop(1, nz, wait, 0)
        partner(z).start()
        partner(z).wait_send()

    @pl.when(c != cs)
    def _():
        partner(z).wait_recv()

    o_ref[...] = g[...]


def pcol_bcast(x, nz, source, collective_id):
    rows, cols = x.shape
    chunks = x.reshape(nz, rows // nz, cols)
    out = pl.pallas_call(
        functools.partial(pcol_kernel, nz, source),
        out_shape=jax.ShapeDtypeStruct(chunks.shape, x.dtype),
        in_specs=[pl.BlockSpec(memory_space=pltpu.VMEM)],
        out_specs=pl.BlockSpec(memory_space=pltpu.VMEM),
        scratch_shapes=[
            pltpu.VMEM(chunks.shape, x.dtype),
            pltpu.SemaphoreType.DMA((nz,)),
            pltpu.SemaphoreType.DMA((1,)),
            pltpu.SemaphoreType.DMA((nz,)),
            pltpu.SemaphoreType.DMA((nz,)),
            pltpu.SemaphoreType.DMA((1,)),
            pltpu.SemaphoreType.DMA((1,)),
        ],
        compiler_params=pltpu.CompilerParams(collective_id=collective_id, has_side_effects=True),
    )(chunks)
    return out.reshape(rows, cols)


def local(x_devices, z_chips, matrix, pivots, lower_inverse, upper_inverse):
    row_count = lax.axis_size("prow")
    col_count = lax.axis_size("pcol")
    my_row = lax.axis_index("prow")
    my_col = lax.axis_index("pcol")
    blocks_down, block, blocks_across, _ = matrix.shape
    local_rows = blocks_down * block
    local_cols = blocks_across * block
    current = matrix.reshape(local_rows, local_cols)
    row_place = jnp.arange(local_rows)
    col_place = jnp.arange(local_cols)
    global_rows = (row_place // block * row_count + my_row) * block + row_place % block
    global_cols = (col_place // block * col_count + my_col) * block + col_place % block
    for panel in range(pivots.shape[0]):
        start = panel * block
        chosen = pivots[panel]
        block_row = chosen // block
        is_mine = block_row % row_count == my_row
        local_index = block_row // row_count * block + chosen % block
        safe_index = jnp.where(is_mine, local_index, 0)
        picked = jnp.where(is_mine[:, None], current[safe_index], jnp.zeros((), jnp.bfloat16))
        top_holder = panel % row_count
        top_first = panel // row_count * block
        is_top = my_row == top_holder
        top_local = current[top_first : top_first + block]
        top_part = jnp.where(is_top, top_local, jnp.zeros((), jnp.bfloat16))
        both = prow_sum(jnp.concatenate([picked, top_part], axis=0), x_devices)
        incoming = both[:block]
        old_top = both[block:]
        target = jnp.where(is_mine, local_index, local_rows)
        current = current.at[target].set(old_top, mode="drop")
        top_now = current[top_first : top_first + block]
        current = current.at[top_first : top_first + block].set(
            jnp.where(is_top, incoming, top_now)
        )
        panel_holder = panel % col_count
        panel_first = panel // col_count * block
        panel_cols = current[:, panel_first : panel_first + block]
        factor = jnp.dot(
            panel_cols, upper_inverse[panel], preferred_element_type=jnp.float32
        ).astype(jnp.bfloat16)
        is_panel = my_col == panel_holder
        factor = jnp.where(is_panel, factor, jnp.zeros((), jnp.bfloat16))
        lower = pcol_bcast(factor, z_chips, panel_holder, 20 + panel)
        upper = jnp.dot(
            lower_inverse[panel], incoming, preferred_element_type=jnp.float32
        ).astype(jnp.bfloat16)
        row_mask = global_rows >= start + block
        col_mask = global_cols >= start + block
        product = jnp.dot(lower, upper, preferred_element_type=jnp.float32)
        changed = (current.astype(jnp.float32) - product).astype(jnp.bfloat16)
        current = jnp.where(row_mask[:, None] & col_mask[None, :], changed, current)
        panel_now = current[:, panel_first : panel_first + block]
        current = current.at[:, panel_first : panel_first + block].set(
            jnp.where(is_panel & row_mask[:, None], lower, panel_now)
        )
        top_now = current[top_first : top_first + block]
        current = current.at[top_first : top_first + block].set(
            jnp.where(is_top & col_mask[None, :], upper, top_now)
        )
    return current.reshape(matrix.shape)


def solution(mesh):
    x_devices = len({d.coords[0] for d in mesh.devices[:, 0]})
    z_chips = len({d.coords[2] for d in mesh.devices[0, :]})
    in_specs = (P(None, "prow", None, "pcol"), P(), P(), P())
    out_specs = P(None, "prow", None, "pcol")
    return jax.shard_map(functools.partial(local, x_devices, z_chips), mesh=mesh, in_specs=in_specs, out_specs=out_specs, check_vma=False)
```

```python
import functools

import jax
import jax.numpy as jnp
from jax import lax
from jax.experimental import pallas as pl
from jax.experimental.pallas import tpu as pltpu
from jax.sharding import PartitionSpec as P

MESH = pl.DeviceIdType.MESH


def sum_kernel(axis, other, n, summed, source, x_ref, o_ref, recv, gath, ssend, srecv,
               bsend, brecv, gsend, grecv):
    me = lax.axis_index(axis)
    them = lax.axis_index(other)

    def dev(j):
        return (j, them) if axis == "prow" else (them, j)

    barrier = pltpu.get_barrier_semaphore()

    def greet(i, c):
        j = lax.rem(me + i, n)
        pl.semaphore_signal(barrier, 1, device_id=dev(j), device_id_type=MESH)
        return c

    lax.fori_loop(1, n, greet, 0)
    pl.semaphore_wait(barrier, n - 1)

    def scatter(j, s):
        return pltpu.make_async_remote_copy(
            src_ref=x_ref.at[j],
            dst_ref=recv.at[s],
            send_sem=ssend.at[j],
            recv_sem=srecv.at[s],
            device_id=dev(j),
            device_id_type=MESH,
        )

    def spread(j):
        return pltpu.make_async_remote_copy(
            src_ref=x_ref.at[j],
            dst_ref=gath.at[j],
            send_sem=bsend.at[j],
            recv_sem=brecv.at[0],
            device_id=dev(j),
            device_id_type=MESH,
        )

    if summed > 0:
        def start_scatter(i, c):
            j = lax.rem(me + i, n)

            @pl.when(j < summed)
            def _():
                scatter(j, me).start()

            return c

        lax.fori_loop(1, n, start_scatter, 0)

    if summed < n:
        @pl.when(me == source)
        def _():
            def start_spread(i, c):
                j = lax.rem(me + i, n)

                @pl.when(j >= summed)
                def _():
                    spread(j).start()

                return c

            lax.fori_loop(1, n, start_spread, 0)
            if source >= summed:
                gath[source] = x_ref[source]

    if summed > 0:
        @pl.when(me < summed)
        def _():
            recv[me] = x_ref[me]

            def wait_scatter(i, c):
                s = lax.rem(me + n - i, n)
                scatter(s, s).wait_recv()
                return c

            lax.fori_loop(1, n, wait_scatter, 0)
            total = recv[0].astype(jnp.float32)
            for s in range(1, n):
                total = total + recv[s].astype(jnp.float32)
            gath[me] = total.astype(gath.dtype)

        def wait_scatter_sent(i, c):
            j = lax.rem(me + i, n)

            @pl.when(j < summed)
            def _():
                scatter(j, me).wait_send()

            return c

        lax.fori_loop(1, n, wait_scatter_sent, 0)

    if summed < n:
        @pl.when((me >= summed) & (me != source))
        def _():
            spread(me).wait_recv()

        @pl.when(me == source)
        def _():
            def wait_spread_sent(i, c):
                j = lax.rem(me + i, n)

                @pl.when(j >= summed)
                def _():
                    spread(j).wait_send()

                return c

            lax.fori_loop(1, n, wait_spread_sent, 0)

    def gather(j, s):
        return pltpu.make_async_remote_copy(
            src_ref=gath.at[s],
            dst_ref=gath.at[s],
            send_sem=gsend.at[j],
            recv_sem=grecv.at[s],
            device_id=dev(j),
            device_id_type=MESH,
        )

    def start_gather(i, c):
        gather(lax.rem(me + i, n), me).start()
        return c

    lax.fori_loop(1, n, start_gather, 0)

    def wait_gather(i, c):
        gather(lax.rem(me + n - i, n), lax.rem(me + n - i, n)).wait_recv()
        gather(lax.rem(me + i, n), me).wait_send()
        return c

    lax.fori_loop(1, n, wait_gather, 0)
    o_ref[...] = gath[...]


def axis_sum(x, axis, other, collective_id, summed_rows, source):
    n = lax.axis_size(axis)
    chunks = x.reshape(n, x.shape[0] // n, x.shape[1])
    summed = summed_rows // chunks.shape[1]
    out = pl.pallas_call(
        functools.partial(sum_kernel, axis, other, n, summed, source),
        out_shape=jax.ShapeDtypeStruct(chunks.shape, chunks.dtype),
        in_specs=[pl.BlockSpec(memory_space=pltpu.VMEM)],
        out_specs=pl.BlockSpec(memory_space=pltpu.VMEM),
        scratch_shapes=[
            pltpu.VMEM(chunks.shape, chunks.dtype),
            pltpu.VMEM(chunks.shape, chunks.dtype),
            pltpu.SemaphoreType.DMA((n,)),
            pltpu.SemaphoreType.DMA((n,)),
            pltpu.SemaphoreType.DMA((n,)),
            pltpu.SemaphoreType.DMA((1,)),
            pltpu.SemaphoreType.DMA((n,)),
            pltpu.SemaphoreType.DMA((n,)),
        ],
        compiler_params=pltpu.CompilerParams(
            collective_id=collective_id, has_side_effects=True
        ),
    )(chunks)
    return out.reshape(x.shape)


def group_kernel(stride, size, mode, x_ref, o_ref, buf, send, recv):
    p = lax.axis_index("prow")
    q = lax.axis_index("pcol")
    me = lax.rem(p // stride, size)
    base = p - me * stride

    def dev(k):
        return (base + k * stride, q)

    barrier = pltpu.get_barrier_semaphore()

    def greet(i, c):
        pl.semaphore_signal(barrier, 1, device_id=dev(lax.rem(me + i, size)), device_id_type=MESH)
        return c

    lax.fori_loop(1, size, greet, 0)
    pl.semaphore_wait(barrier, size - 1)

    def copy(k, s):
        src = x_ref.at[k] if mode == "rs" else buf.at[s]
        return pltpu.make_async_remote_copy(
            src_ref=src,
            dst_ref=buf.at[s],
            send_sem=send.at[k],
            recv_sem=recv.at[s],
            device_id=dev(k),
            device_id_type=MESH,
        )

    if mode == "ag":
        buf[me] = x_ref[...]

    def start(i, c):
        copy(lax.rem(me + i, size), me).start()
        return c

    lax.fori_loop(1, size, start, 0)
    if mode == "rs":
        buf[me] = x_ref[me]

    def wait(i, c):
        s = lax.rem(me + size - i, size)
        copy(s, s).wait_recv()
        copy(lax.rem(me + i, size), me).wait_send()
        return c

    lax.fori_loop(1, size, wait, 0)
    if mode == "rs":
        total = buf[0].astype(jnp.float32)
        for s in range(1, size):
            total = total + buf[s].astype(jnp.float32)
        o_ref[...] = total.astype(o_ref.dtype)
    else:
        o_ref[...] = buf[...]


def group_step(x, stride, size, mode, collective_id):
    if mode == "rs":
        chunks = x.reshape(size, x.shape[0] // size, x.shape[1])
        out_shape = chunks.shape[1:]
        buf_shape = chunks.shape
    else:
        chunks = x
        out_shape = (size,) + x.shape
        buf_shape = out_shape
    out = pl.pallas_call(
        functools.partial(group_kernel, stride, size, mode),
        out_shape=jax.ShapeDtypeStruct(out_shape, x.dtype),
        in_specs=[pl.BlockSpec(memory_space=pltpu.VMEM)],
        out_specs=pl.BlockSpec(memory_space=pltpu.VMEM),
        scratch_shapes=[
            pltpu.VMEM(buf_shape, x.dtype),
            pltpu.SemaphoreType.DMA((size,)),
            pltpu.SemaphoreType.DMA((size,)),
        ],
        compiler_params=pltpu.CompilerParams(
            collective_id=collective_id, has_side_effects=True
        ),
    )(chunks)
    if mode == "ag":
        out = out.reshape(size * x.shape[0], x.shape[1])
    return out


def prow_kernel(xd, yd, top, t_ref, o_ref, b1, a2, b2, b3, b4, sends, recvs, tsend, trecv):
    p = lax.axis_index("prow")
    q = lax.axis_index("pcol")
    xi = lax.rem(p, xd)
    yi = p // xd
    xt, yt = top % xd, top // xd

    def xdev(k):
        return (yi * xd + k, q)

    def ydev(k):
        return (k * xd + xi, q)

    barrier = pltpu.get_barrier_semaphore()

    def greet_x(i, c):
        pl.semaphore_signal(barrier, 1, device_id=xdev(lax.rem(xi + i, xd)), device_id_type=MESH)
        return c

    def greet_y(i, c):
        pl.semaphore_signal(barrier, 1, device_id=ydev(lax.rem(yi + i, yd)), device_id_type=MESH)
        return c

    lax.fori_loop(1, xd, greet_x, 0)
    lax.fori_loop(1, yd, greet_y, 0)
    pl.semaphore_wait(barrier, xd + yd - 2)

    def exchange(phase, src, dst, me, size, dev):
        def copy(k, s):
            return pltpu.make_async_remote_copy(
                src_ref=src(k, s),
                dst_ref=dst(s),
                send_sem=sends.at[phase, k],
                recv_sem=recvs.at[phase, s],
                device_id=dev(k),
                device_id_type=MESH,
            )

        def start(i, c):
            copy(lax.rem(me + i, size), me).start()
            return c

        lax.fori_loop(1, size, start, 0)

        def wait(i, c):
            s = lax.rem(me + size - i, size)
            copy(s, s).wait_recv()
            copy(lax.rem(me + i, size), me).wait_send()
            return c

        lax.fori_loop(1, size, wait, 0)

    def total(parts, size):
        acc = parts(0).astype(jnp.float32)
        for s in range(1, size):
            acc = acc + parts(s).astype(jnp.float32)
        return acc

    def top_copy(k):
        return pltpu.make_async_remote_copy(
            src_ref=t_ref.at[k, 1],
            dst_ref=b1.at[xt, 1],
            send_sem=tsend.at[k],
            recv_sem=trecv.at[0],
            device_id=xdev(k),
            device_id_type=MESH,
        )

    @pl.when(p == top)
    def _():
        def start(i, c):
            top_copy(lax.rem(xi + i, xd)).start()
            return c

        lax.fori_loop(1, xd, start, 0)

    exchange(0, lambda k, s: t_ref.at[k, 0], lambda s: b1.at[s, 0], xi, xd, xdev)
    b1[xi, 0] = t_ref[xi, 0]
    top_half = (yd // 2, b1.shape[2] * 2 // yd, b1.shape[3])
    a2[: yd // 2] = total(lambda s: b1[s, 0], xd).astype(a2.dtype).reshape(top_half)

    @pl.when(p == top)
    def _():
        def sent(i, c):
            top_copy(lax.rem(xi + i, xd)).wait_send()
            return c

        lax.fori_loop(1, xd, sent, 0)
        a3 = t_ref[xi, 1]
        a2[yd // 2 :] = a3.reshape(top_half)

    @pl.when((yi == yt) & (p != top))
    def _():
        top_copy(xi).wait_recv()
        a2[yd // 2 :] = b1[xt, 1].reshape(top_half)

    @pl.when(yi != yt)
    def _():
        a2[yd // 2 :] = jnp.zeros(top_half, a2.dtype)

    exchange(1, lambda k, s: a2.at[k], lambda s: b2.at[s], yi, yd, ydev)
    b2[yi] = a2[yi]
    b3[yi] = total(lambda s: b2[s], yd).astype(b3.dtype)
    exchange(2, lambda k, s: b3.at[s], lambda s: b3.at[s], yi, yd, ydev)
    b4[xi] = b3[...].reshape(b4.shape[1:])
    exchange(3, lambda k, s: b4.at[s], lambda s: b4.at[s], xi, xd, xdev)
    o_ref[...] = b4[...]


def prow_sum(picked, top_part, xd, top):
    yd = lax.axis_size("prow") // xd
    rows, cols = picked.shape
    chunks = jnp.stack(
        [picked.reshape(xd, rows // xd, cols), top_part.reshape(xd, rows // xd, cols)], axis=1
    )
    part = 2 * rows // xd // yd
    out = pl.pallas_call(
        functools.partial(prow_kernel, xd, yd, top),
        out_shape=jax.ShapeDtypeStruct((xd, yd, part, cols), picked.dtype),
        in_specs=[pl.BlockSpec(memory_space=pltpu.VMEM)],
        out_specs=pl.BlockSpec(memory_space=pltpu.VMEM),
        scratch_shapes=[
            pltpu.VMEM(chunks.shape, picked.dtype),
            pltpu.VMEM((yd, part, cols), picked.dtype),
            pltpu.VMEM((yd, part, cols), picked.dtype),
            pltpu.VMEM((yd, part, cols), picked.dtype),
            pltpu.VMEM((xd, yd, part, cols), picked.dtype),
            pltpu.SemaphoreType.DMA((4, max(xd, yd))),
            pltpu.SemaphoreType.DMA((4, max(xd, yd))),
            pltpu.SemaphoreType.DMA((xd,)),
            pltpu.SemaphoreType.DMA((1,)),
        ],
        compiler_params=pltpu.CompilerParams(collective_id=10 + top, has_side_effects=True),
    )(chunks)
    out = out.reshape(xd, 2, rows // xd, cols)
    return out[:, 0].reshape(rows, cols), out[:, 1].reshape(rows, cols)


def pcol_kernel(nz, source, x_ref, o_ref, g, p1send, p1recv, p2send, p2recv, p3send, p3recv):
    q = lax.axis_index("pcol")
    p = lax.axis_index("prow")
    nc = lax.axis_size("pcol") // nz
    z = q // nc
    c = lax.rem(q, nc)
    zs, cs = source // nc, source % nc

    def dev(zz, cc):
        return (p, zz * nc + cc)

    barrier = pltpu.get_barrier_semaphore()
    n = nz * nc

    def greet(i, carry):
        j = lax.rem(q + i, n)
        pl.semaphore_signal(barrier, 1, device_id=(p, j), device_id_type=MESH)
        return carry

    lax.fori_loop(1, n, greet, 0)
    pl.semaphore_wait(barrier, n - 1)

    def spread(j):
        return pltpu.make_async_remote_copy(
            src_ref=x_ref.at[j],
            dst_ref=g.at[j],
            send_sem=p1send.at[j],
            recv_sem=p1recv.at[0],
            device_id=dev(j, cs),
            device_id_type=MESH,
        )

    def ring(j, s):
        return pltpu.make_async_remote_copy(
            src_ref=g.at[s],
            dst_ref=g.at[s],
            send_sem=p2send.at[j],
            recv_sem=p2recv.at[s],
            device_id=dev(j, cs),
            device_id_type=MESH,
        )

    def partner(zz):
        return pltpu.make_async_remote_copy(
            src_ref=g,
            dst_ref=g,
            send_sem=p3send.at[0],
            recv_sem=p3recv.at[0],
            device_id=dev(zz, 1 - cs),
            device_id_type=MESH,
        )

    @pl.when(q == source)
    def _():
        def start(i, carry):
            spread(lax.rem(zs + i, nz)).start()
            return carry

        lax.fori_loop(1, nz, start, 0)
        g[zs] = x_ref[zs]

        def sent(i, carry):
            spread(lax.rem(zs + i, nz)).wait_send()
            return carry

        lax.fori_loop(1, nz, sent, 0)

    @pl.when((c == cs) & (z != zs))
    def _():
        spread(z).wait_recv()

    @pl.when(c == cs)
    def _():
        def start(i, carry):
            ring(lax.rem(z + i, nz), z).start()
            return carry

        lax.fori_loop(1, nz, start, 0)

        def wait(i, carry):
            s = lax.rem(z + nz - i, nz)
            ring(s, s).wait_recv()
            ring(lax.rem(z + i, nz), z).wait_send()
            return carry

        lax.fori_loop(1, nz, wait, 0)
        partner(z).start()
        partner(z).wait_send()

    @pl.when(c != cs)
    def _():
        partner(z).wait_recv()

    o_ref[...] = g[...]


def pcol_bcast(x, nz, source, collective_id):
    rows, cols = x.shape
    chunks = x.reshape(nz, rows // nz, cols)
    out = pl.pallas_call(
        functools.partial(pcol_kernel, nz, source),
        out_shape=jax.ShapeDtypeStruct(chunks.shape, x.dtype),
        in_specs=[pl.BlockSpec(memory_space=pltpu.VMEM)],
        out_specs=pl.BlockSpec(memory_space=pltpu.VMEM),
        scratch_shapes=[
            pltpu.VMEM(chunks.shape, x.dtype),
            pltpu.SemaphoreType.DMA((nz,)),
            pltpu.SemaphoreType.DMA((1,)),
            pltpu.SemaphoreType.DMA((nz,)),
            pltpu.SemaphoreType.DMA((nz,)),
            pltpu.SemaphoreType.DMA((1,)),
            pltpu.SemaphoreType.DMA((1,)),
        ],
        compiler_params=pltpu.CompilerParams(collective_id=collective_id, has_side_effects=True),
    )(chunks)
    return out.reshape(rows, cols)


def local(x_devices, z_chips, matrix, pivots, lower_inverse, upper_inverse):
    row_count = lax.axis_size("prow")
    col_count = lax.axis_size("pcol")
    my_row = lax.axis_index("prow")
    my_col = lax.axis_index("pcol")
    blocks_down, block, blocks_across, _ = matrix.shape
    local_rows = blocks_down * block
    local_cols = blocks_across * block
    current = matrix.reshape(local_rows, local_cols)
    row_place = jnp.arange(local_rows)
    col_place = jnp.arange(local_cols)
    global_rows = (row_place // block * row_count + my_row) * block + row_place % block
    global_cols = (col_place // block * col_count + my_col) * block + col_place % block
    for panel in range(pivots.shape[0]):
        start = panel * block
        chosen = pivots[panel]
        block_row = chosen // block
        is_mine = block_row % row_count == my_row
        local_index = block_row // row_count * block + chosen % block
        safe_index = jnp.where(is_mine, local_index, 0)
        picked = jnp.where(is_mine[:, None], current[safe_index], jnp.zeros((), jnp.bfloat16))
        top_holder = panel % row_count
        top_first = panel // row_count * block
        is_top = my_row == top_holder
        top_local = current[top_first : top_first + block]
        top_part = jnp.where(is_top, top_local, jnp.zeros((), jnp.bfloat16))
        incoming, old_top = prow_sum(picked, top_part, x_devices, top_holder)
        target = jnp.where(is_mine, local_index, local_rows)
        current = current.at[target].set(old_top, mode="drop")
        top_now = current[top_first : top_first + block]
        current = current.at[top_first : top_first + block].set(
            jnp.where(is_top, incoming, top_now)
        )
        panel_holder = panel % col_count
        panel_first = panel // col_count * block
        panel_cols = current[:, panel_first : panel_first + block]
        factor = jnp.dot(
            panel_cols, upper_inverse[panel], preferred_element_type=jnp.float32
        ).astype(jnp.bfloat16)
        is_panel = my_col == panel_holder
        factor = jnp.where(is_panel, factor, jnp.zeros((), jnp.bfloat16))
        lower = pcol_bcast(factor, z_chips, panel_holder, 20 + panel)
        upper = jnp.dot(
            lower_inverse[panel], incoming, preferred_element_type=jnp.float32
        ).astype(jnp.bfloat16)
        row_mask = global_rows >= start + block
        col_mask = global_cols >= start + block
        product = jnp.dot(lower, upper, preferred_element_type=jnp.float32)
        changed = (current.astype(jnp.float32) - product).astype(jnp.bfloat16)
        current = jnp.where(row_mask[:, None] & col_mask[None, :], changed, current)
        panel_now = current[:, panel_first : panel_first + block]
        current = current.at[:, panel_first : panel_first + block].set(
            jnp.where(is_panel & row_mask[:, None], lower, panel_now)
        )
        top_now = current[top_first : top_first + block]
        current = current.at[top_first : top_first + block].set(
            jnp.where(is_top & col_mask[None, :], upper, top_now)
        )
    return current.reshape(matrix.shape)


def solution(mesh):
    x_devices = len({d.coords[0] for d in mesh.devices[:, 0]})
    z_chips = len({d.coords[2] for d in mesh.devices[0, :]})
    in_specs = (P(None, "prow", None, "pcol"), P(), P(), P())
    out_specs = P(None, "prow", None, "pcol")
    return jax.shard_map(functools.partial(local, x_devices, z_chips), mesh=mesh, in_specs=in_specs, out_specs=out_specs, check_vma=False)
```

```python
import functools

import jax
import jax.numpy as jnp
from jax import lax
from jax.experimental import pallas as pl
from jax.experimental.pallas import tpu as pltpu
from jax.sharding import PartitionSpec as P

MESH = pl.DeviceIdType.MESH


def sum_kernel(axis, other, n, summed, source, x_ref, o_ref, recv, gath, ssend, srecv,
               bsend, brecv, gsend, grecv):
    me = lax.axis_index(axis)
    them = lax.axis_index(other)

    def dev(j):
        return (j, them) if axis == "prow" else (them, j)

    barrier = pltpu.get_barrier_semaphore()

    def greet(i, c):
        j = lax.rem(me + i, n)
        pl.semaphore_signal(barrier, 1, device_id=dev(j), device_id_type=MESH)
        return c

    lax.fori_loop(1, n, greet, 0)
    pl.semaphore_wait(barrier, n - 1)

    def scatter(j, s):
        return pltpu.make_async_remote_copy(
            src_ref=x_ref.at[j],
            dst_ref=recv.at[s],
            send_sem=ssend.at[j],
            recv_sem=srecv.at[s],
            device_id=dev(j),
            device_id_type=MESH,
        )

    def spread(j):
        return pltpu.make_async_remote_copy(
            src_ref=x_ref.at[j],
            dst_ref=gath.at[j],
            send_sem=bsend.at[j],
            recv_sem=brecv.at[0],
            device_id=dev(j),
            device_id_type=MESH,
        )

    if summed > 0:
        def start_scatter(i, c):
            j = lax.rem(me + i, n)

            @pl.when(j < summed)
            def _():
                scatter(j, me).start()

            return c

        lax.fori_loop(1, n, start_scatter, 0)

    if summed < n:
        @pl.when(me == source)
        def _():
            def start_spread(i, c):
                j = lax.rem(me + i, n)

                @pl.when(j >= summed)
                def _():
                    spread(j).start()

                return c

            lax.fori_loop(1, n, start_spread, 0)
            if source >= summed:
                gath[source] = x_ref[source]

    if summed > 0:
        @pl.when(me < summed)
        def _():
            recv[me] = x_ref[me]

            def wait_scatter(i, c):
                s = lax.rem(me + n - i, n)
                scatter(s, s).wait_recv()
                return c

            lax.fori_loop(1, n, wait_scatter, 0)
            total = recv[0].astype(jnp.float32)
            for s in range(1, n):
                total = total + recv[s].astype(jnp.float32)
            gath[me] = total.astype(gath.dtype)

        def wait_scatter_sent(i, c):
            j = lax.rem(me + i, n)

            @pl.when(j < summed)
            def _():
                scatter(j, me).wait_send()

            return c

        lax.fori_loop(1, n, wait_scatter_sent, 0)

    if summed < n:
        @pl.when((me >= summed) & (me != source))
        def _():
            spread(me).wait_recv()

        @pl.when(me == source)
        def _():
            def wait_spread_sent(i, c):
                j = lax.rem(me + i, n)

                @pl.when(j >= summed)
                def _():
                    spread(j).wait_send()

                return c

            lax.fori_loop(1, n, wait_spread_sent, 0)

    def gather(j, s):
        return pltpu.make_async_remote_copy(
            src_ref=gath.at[s],
            dst_ref=gath.at[s],
            send_sem=gsend.at[j],
            recv_sem=grecv.at[s],
            device_id=dev(j),
            device_id_type=MESH,
        )

    def start_gather(i, c):
        gather(lax.rem(me + i, n), me).start()
        return c

    lax.fori_loop(1, n, start_gather, 0)

    def wait_gather(i, c):
        gather(lax.rem(me + n - i, n), lax.rem(me + n - i, n)).wait_recv()
        gather(lax.rem(me + i, n), me).wait_send()
        return c

    lax.fori_loop(1, n, wait_gather, 0)
    o_ref[...] = gath[...]


def axis_sum(x, axis, other, collective_id, summed_rows, source):
    n = lax.axis_size(axis)
    chunks = x.reshape(n, x.shape[0] // n, x.shape[1])
    summed = summed_rows // chunks.shape[1]
    out = pl.pallas_call(
        functools.partial(sum_kernel, axis, other, n, summed, source),
        out_shape=jax.ShapeDtypeStruct(chunks.shape, chunks.dtype),
        in_specs=[pl.BlockSpec(memory_space=pltpu.VMEM)],
        out_specs=pl.BlockSpec(memory_space=pltpu.VMEM),
        scratch_shapes=[
            pltpu.VMEM(chunks.shape, chunks.dtype),
            pltpu.VMEM(chunks.shape, chunks.dtype),
            pltpu.SemaphoreType.DMA((n,)),
            pltpu.SemaphoreType.DMA((n,)),
            pltpu.SemaphoreType.DMA((n,)),
            pltpu.SemaphoreType.DMA((1,)),
            pltpu.SemaphoreType.DMA((n,)),
            pltpu.SemaphoreType.DMA((n,)),
        ],
        compiler_params=pltpu.CompilerParams(
            collective_id=collective_id, has_side_effects=True
        ),
    )(chunks)
    return out.reshape(x.shape)


def group_kernel(stride, size, mode, x_ref, o_ref, buf, send, recv):
    p = lax.axis_index("prow")
    q = lax.axis_index("pcol")
    me = lax.rem(p // stride, size)
    base = p - me * stride

    def dev(k):
        return (base + k * stride, q)

    barrier = pltpu.get_barrier_semaphore()

    def greet(i, c):
        pl.semaphore_signal(barrier, 1, device_id=dev(lax.rem(me + i, size)), device_id_type=MESH)
        return c

    lax.fori_loop(1, size, greet, 0)
    pl.semaphore_wait(barrier, size - 1)

    def copy(k, s):
        src = x_ref.at[k] if mode == "rs" else buf.at[s]
        return pltpu.make_async_remote_copy(
            src_ref=src,
            dst_ref=buf.at[s],
            send_sem=send.at[k],
            recv_sem=recv.at[s],
            device_id=dev(k),
            device_id_type=MESH,
        )

    if mode == "ag":
        buf[me] = x_ref[...]

    def start(i, c):
        copy(lax.rem(me + i, size), me).start()
        return c

    lax.fori_loop(1, size, start, 0)
    if mode == "rs":
        buf[me] = x_ref[me]

    def wait(i, c):
        s = lax.rem(me + size - i, size)
        copy(s, s).wait_recv()
        copy(lax.rem(me + i, size), me).wait_send()
        return c

    lax.fori_loop(1, size, wait, 0)
    if mode == "rs":
        total = buf[0].astype(jnp.float32)
        for s in range(1, size):
            total = total + buf[s].astype(jnp.float32)
        o_ref[...] = total.astype(o_ref.dtype)
    else:
        o_ref[...] = buf[...]


def group_step(x, stride, size, mode, collective_id):
    if mode == "rs":
        chunks = x.reshape(size, x.shape[0] // size, x.shape[1])
        out_shape = chunks.shape[1:]
        buf_shape = chunks.shape
    else:
        chunks = x
        out_shape = (size,) + x.shape
        buf_shape = out_shape
    out = pl.pallas_call(
        functools.partial(group_kernel, stride, size, mode),
        out_shape=jax.ShapeDtypeStruct(out_shape, x.dtype),
        in_specs=[pl.BlockSpec(memory_space=pltpu.VMEM)],
        out_specs=pl.BlockSpec(memory_space=pltpu.VMEM),
        scratch_shapes=[
            pltpu.VMEM(buf_shape, x.dtype),
            pltpu.SemaphoreType.DMA((size,)),
            pltpu.SemaphoreType.DMA((size,)),
        ],
        compiler_params=pltpu.CompilerParams(
            collective_id=collective_id, has_side_effects=True
        ),
    )(chunks)
    if mode == "ag":
        out = out.reshape(size * x.shape[0], x.shape[1])
    return out


def prow_kernel(xd, yd, top, t_ref, o_ref, b1, a2, b2, b3, b4, sends, recvs, tsend, trecv):
    p = lax.axis_index("prow")
    q = lax.axis_index("pcol")
    xi = lax.rem(p, xd)
    yi = p // xd
    xt, yt = top % xd, top // xd

    def xdev(k):
        return (yi * xd + k, q)

    def ydev(k):
        return (k * xd + xi, q)

    barrier = pltpu.get_barrier_semaphore()

    def greet_x(i, c):
        pl.semaphore_signal(barrier, 1, device_id=xdev(lax.rem(xi + i, xd)), device_id_type=MESH)
        return c

    def greet_y(i, c):
        pl.semaphore_signal(barrier, 1, device_id=ydev(lax.rem(yi + i, yd)), device_id_type=MESH)
        return c

    lax.fori_loop(1, xd, greet_x, 0)
    lax.fori_loop(1, yd, greet_y, 0)
    pl.semaphore_wait(barrier, xd + yd - 2)

    def exchange(phase, src, dst, me, size, dev):
        def copy(k, s):
            return pltpu.make_async_remote_copy(
                src_ref=src(k, s),
                dst_ref=dst(s),
                send_sem=sends.at[phase, k],
                recv_sem=recvs.at[phase, s],
                device_id=dev(k),
                device_id_type=MESH,
            )

        def start(i, c):
            copy(lax.rem(me + i, size), me).start()
            return c

        lax.fori_loop(1, size, start, 0)

        def wait(i, c):
            s = lax.rem(me + size - i, size)
            copy(s, s).wait_recv()
            copy(lax.rem(me + i, size), me).wait_send()
            return c

        lax.fori_loop(1, size, wait, 0)

    def total(parts, size):
        acc = parts(0).astype(jnp.float32)
        for s in range(1, size):
            acc = acc + parts(s).astype(jnp.float32)
        return acc

    def top_copy(k):
        return pltpu.make_async_remote_copy(
            src_ref=t_ref.at[k, 1],
            dst_ref=b1.at[xt, 1],
            send_sem=tsend.at[k],
            recv_sem=trecv.at[0],
            device_id=xdev(k),
            device_id_type=MESH,
        )

    @pl.when(p == top)
    def _():
        def start(i, c):
            top_copy(lax.rem(xi + i, xd)).start()
            return c

        lax.fori_loop(1, xd, start, 0)

    exchange(0, lambda k, s: t_ref.at[k, 0], lambda s: b1.at[s, 0], xi, xd, xdev)
    b1[xi, 0] = t_ref[xi, 0]
    top_half = (yd // 2, b1.shape[2] * 2 // yd, b1.shape[3])
    a2[: yd // 2] = total(lambda s: b1[s, 0], xd).astype(a2.dtype).reshape(top_half)

    @pl.when(p == top)
    def _():
        def sent(i, c):
            top_copy(lax.rem(xi + i, xd)).wait_send()
            return c

        lax.fori_loop(1, xd, sent, 0)
        a3 = t_ref[xi, 1]
        a2[yd // 2 :] = a3.reshape(top_half)

    @pl.when((yi == yt) & (p != top))
    def _():
        top_copy(xi).wait_recv()
        a2[yd // 2 :] = b1[xt, 1].reshape(top_half)

    @pl.when(yi != yt)
    def _():
        a2[yd // 2 :] = jnp.zeros(top_half, a2.dtype)

    exchange(1, lambda k, s: a2.at[k], lambda s: b2.at[s], yi, yd, ydev)
    b2[yi] = a2[yi]
    b3[yi] = total(lambda s: b2[s], yd).astype(b3.dtype)
    exchange(2, lambda k, s: b3.at[s], lambda s: b3.at[s], yi, yd, ydev)
    b4[xi] = b3[...].reshape(b4.shape[1:])
    exchange(3, lambda k, s: b4.at[s], lambda s: b4.at[s], xi, xd, xdev)
    o_ref[...] = b4[...]


def prow_sum(picked, top_part, xd, top):
    yd = lax.axis_size("prow") // xd
    rows, cols = picked.shape
    chunks = jnp.stack(
        [picked.reshape(xd, rows // xd, cols), top_part.reshape(xd, rows // xd, cols)], axis=1
    )
    part = 2 * rows // xd // yd
    out = pl.pallas_call(
        functools.partial(prow_kernel, xd, yd, top),
        out_shape=jax.ShapeDtypeStruct((xd, yd, part, cols), picked.dtype),
        in_specs=[pl.BlockSpec(memory_space=pltpu.VMEM)],
        out_specs=pl.BlockSpec(memory_space=pltpu.VMEM),
        scratch_shapes=[
            pltpu.VMEM(chunks.shape, picked.dtype),
            pltpu.VMEM((yd, part, cols), picked.dtype),
            pltpu.VMEM((yd, part, cols), picked.dtype),
            pltpu.VMEM((yd, part, cols), picked.dtype),
            pltpu.VMEM((xd, yd, part, cols), picked.dtype),
            pltpu.SemaphoreType.DMA((4, max(xd, yd))),
            pltpu.SemaphoreType.DMA((4, max(xd, yd))),
            pltpu.SemaphoreType.DMA((xd,)),
            pltpu.SemaphoreType.DMA((1,)),
        ],
        compiler_params=pltpu.CompilerParams(collective_id=10 + top, has_side_effects=True),
    )(chunks)
    out = out.reshape(xd, 2, rows // xd, cols)
    return out[:, 0].reshape(rows, cols), out[:, 1].reshape(rows, cols)


def pcol_kernel(nz, source, x_ref, o_ref, g, p1send, p1recv, p2send, p2recv, p3send, p3recv):
    q = lax.axis_index("pcol")
    p = lax.axis_index("prow")
    nc = lax.axis_size("pcol") // nz
    z = q // nc
    c = lax.rem(q, nc)
    zs, cs = source // nc, source % nc

    def dev(zz, cc):
        return (p, zz * nc + cc)

    barrier = pltpu.get_barrier_semaphore()
    n = nz * nc

    def greet(i, carry):
        j = lax.rem(q + i, n)
        pl.semaphore_signal(barrier, 1, device_id=(p, j), device_id_type=MESH)
        return carry

    lax.fori_loop(1, n, greet, 0)
    pl.semaphore_wait(barrier, n - 1)

    def spread(j):
        return pltpu.make_async_remote_copy(
            src_ref=x_ref.at[j],
            dst_ref=g.at[j],
            send_sem=p1send.at[j],
            recv_sem=p1recv.at[0],
            device_id=dev(j, cs),
            device_id_type=MESH,
        )

    def ring(j, s):
        return pltpu.make_async_remote_copy(
            src_ref=g.at[s],
            dst_ref=g.at[s],
            send_sem=p2send.at[j],
            recv_sem=p2recv.at[s],
            device_id=dev(j, cs),
            device_id_type=MESH,
        )

    def partner(zz):
        return pltpu.make_async_remote_copy(
            src_ref=g,
            dst_ref=g,
            send_sem=p3send.at[0],
            recv_sem=p3recv.at[0],
            device_id=dev(zz, 1 - cs),
            device_id_type=MESH,
        )

    @pl.when(q == source)
    def _():
        def start(i, carry):
            spread(lax.rem(zs + i, nz)).start()
            return carry

        lax.fori_loop(1, nz, start, 0)
        g[zs] = x_ref[zs]

        def sent(i, carry):
            spread(lax.rem(zs + i, nz)).wait_send()
            return carry

        lax.fori_loop(1, nz, sent, 0)

    @pl.when((c == cs) & (z != zs))
    def _():
        spread(z).wait_recv()

    @pl.when(c == cs)
    def _():
        def start(i, carry):
            ring(lax.rem(z + i, nz), z).start()
            return carry

        lax.fori_loop(1, nz, start, 0)

        def wait(i, carry):
            s = lax.rem(z + nz - i, nz)
            ring(s, s).wait_recv()
            ring(lax.rem(z + i, nz), z).wait_send()
            return carry

        lax.fori_loop(1, nz, wait, 0)
        partner(z).start()
        partner(z).wait_send()

    @pl.when(c != cs)
    def _():
        partner(z).wait_recv()

    o_ref[...] = g[...]


def pcol_bcast(x, nz, source, collective_id):
    rows, cols = x.shape
    chunks = x.reshape(nz, rows // nz, cols)
    out = pl.pallas_call(
        functools.partial(pcol_kernel, nz, source),
        out_shape=jax.ShapeDtypeStruct(chunks.shape, x.dtype),
        in_specs=[pl.BlockSpec(memory_space=pltpu.VMEM)],
        out_specs=pl.BlockSpec(memory_space=pltpu.VMEM),
        scratch_shapes=[
            pltpu.VMEM(chunks.shape, x.dtype),
            pltpu.SemaphoreType.DMA((nz,)),
            pltpu.SemaphoreType.DMA((1,)),
            pltpu.SemaphoreType.DMA((nz,)),
            pltpu.SemaphoreType.DMA((nz,)),
            pltpu.SemaphoreType.DMA((1,)),
            pltpu.SemaphoreType.DMA((1,)),
        ],
        compiler_params=pltpu.CompilerParams(collective_id=collective_id, has_side_effects=True),
    )(chunks)
    return out.reshape(rows, cols)


def local(x_devices, z_chips, matrix, pivots, lower_inverse, upper_inverse):
    row_count = lax.axis_size("prow")
    col_count = lax.axis_size("pcol")
    my_row = lax.axis_index("prow")
    my_col = lax.axis_index("pcol")
    blocks_down, block, blocks_across, _ = matrix.shape
    local_rows = blocks_down * block
    local_cols = blocks_across * block
    current = matrix.reshape(local_rows, local_cols)
    row_place = jnp.arange(local_rows)
    col_place = jnp.arange(local_cols)
    global_rows = (row_place // block * row_count + my_row) * block + row_place % block
    global_cols = (col_place // block * col_count + my_col) * block + col_place % block
    for panel in range(pivots.shape[0]):
        start = panel * block
        chosen = pivots[panel]
        block_row = chosen // block
        is_mine = block_row % row_count == my_row
        local_index = block_row // row_count * block + chosen % block
        safe_index = jnp.where(is_mine, local_index, 0)
        picked = jnp.where(is_mine[:, None], current[safe_index], jnp.zeros((), jnp.bfloat16))
        top_holder = panel % row_count
        top_first = panel // row_count * block
        is_top = my_row == top_holder
        top_local = current[top_first : top_first + block]
        top_part = jnp.where(is_top, top_local, jnp.zeros((), jnp.bfloat16))
        incoming, old_top = prow_sum(picked, top_part, x_devices, top_holder)
        target = jnp.where(is_mine, local_index, local_rows)
        current = current.at[target].set(old_top, mode="drop")
        top_now = current[top_first : top_first + block]
        current = current.at[top_first : top_first + block].set(
            jnp.where(is_top, incoming, top_now)
        )
        panel_holder = panel % col_count
        panel_first = panel // col_count * block
        panel_cols = current[:, panel_first : panel_first + block]
        factor = jnp.dot(
            panel_cols, upper_inverse[panel], preferred_element_type=jnp.float32
        ).astype(jnp.bfloat16)
        is_panel = my_col == panel_holder
        factor = jnp.where(is_panel, factor, jnp.zeros((), jnp.bfloat16))
        lower = pcol_bcast(factor, z_chips, panel_holder, 20 + panel)
        upper = jnp.dot(
            lower_inverse[panel], incoming, preferred_element_type=jnp.float32
        ).astype(jnp.bfloat16)
        row_mask = global_rows >= start + block
        col_mask = global_cols >= start + block
        product = jnp.dot(lower, upper, preferred_element_type=jnp.float32)
        changed = (current.astype(jnp.float32) - product).astype(jnp.bfloat16)
        below = row_mask[:, None]
        right = col_mask[None, :]
        in_panel = is_panel & (col_place // block == panel_first // block)[None, :]
        in_top = is_top & (row_place // block == top_first // block)[:, None]
        lower_wide = jnp.broadcast_to(
            lower[:, None, :], (local_rows, blocks_across, block)
        ).reshape(local_rows, local_cols)
        upper_tall = jnp.broadcast_to(
            upper[None], (blocks_down, block, local_cols)
        ).reshape(local_rows, local_cols)
        current = jnp.where(
            below & right,
            changed,
            jnp.where(
                in_panel & below,
                lower_wide,
                jnp.where(in_top & right, upper_tall, current),
            ),
        )
    return current.reshape(matrix.shape)


def solution(mesh):
    x_devices = len({d.coords[0] for d in mesh.devices[:, 0]})
    z_chips = len({d.coords[2] for d in mesh.devices[0, :]})
    in_specs = (P(None, "prow", None, "pcol"), P(), P(), P())
    out_specs = P(None, "prow", None, "pcol")
    return jax.shard_map(functools.partial(local, x_devices, z_chips), mesh=mesh, in_specs=in_specs, out_specs=out_specs, check_vma=False)
```

```python
import functools

import jax
import jax.numpy as jnp
from jax import lax
from jax.experimental import pallas as pl
from jax.experimental.pallas import tpu as pltpu
from jax.sharding import PartitionSpec as P

MESH = pl.DeviceIdType.MESH


def sum_kernel(axis, other, n, summed, source, x_ref, o_ref, recv, gath, ssend, srecv,
               bsend, brecv, gsend, grecv):
    me = lax.axis_index(axis)
    them = lax.axis_index(other)

    def dev(j):
        return (j, them) if axis == "prow" else (them, j)

    barrier = pltpu.get_barrier_semaphore()

    def greet(i, c):
        j = lax.rem(me + i, n)
        pl.semaphore_signal(barrier, 1, device_id=dev(j), device_id_type=MESH)
        return c

    lax.fori_loop(1, n, greet, 0)
    pl.semaphore_wait(barrier, n - 1)

    def scatter(j, s):
        return pltpu.make_async_remote_copy(
            src_ref=x_ref.at[j],
            dst_ref=recv.at[s],
            send_sem=ssend.at[j],
            recv_sem=srecv.at[s],
            device_id=dev(j),
            device_id_type=MESH,
        )

    def spread(j):
        return pltpu.make_async_remote_copy(
            src_ref=x_ref.at[j],
            dst_ref=gath.at[j],
            send_sem=bsend.at[j],
            recv_sem=brecv.at[0],
            device_id=dev(j),
            device_id_type=MESH,
        )

    if summed > 0:
        def start_scatter(i, c):
            j = lax.rem(me + i, n)

            @pl.when(j < summed)
            def _():
                scatter(j, me).start()

            return c

        lax.fori_loop(1, n, start_scatter, 0)

    if summed < n:
        @pl.when(me == source)
        def _():
            def start_spread(i, c):
                j = lax.rem(me + i, n)

                @pl.when(j >= summed)
                def _():
                    spread(j).start()

                return c

            lax.fori_loop(1, n, start_spread, 0)
            if source >= summed:
                gath[source] = x_ref[source]

    if summed > 0:
        @pl.when(me < summed)
        def _():
            recv[me] = x_ref[me]

            def wait_scatter(i, c):
                s = lax.rem(me + n - i, n)
                scatter(s, s).wait_recv()
                return c

            lax.fori_loop(1, n, wait_scatter, 0)
            total = recv[0].astype(jnp.float32)
            for s in range(1, n):
                total = total + recv[s].astype(jnp.float32)
            gath[me] = total.astype(gath.dtype)

        def wait_scatter_sent(i, c):
            j = lax.rem(me + i, n)

            @pl.when(j < summed)
            def _():
                scatter(j, me).wait_send()

            return c

        lax.fori_loop(1, n, wait_scatter_sent, 0)

    if summed < n:
        @pl.when((me >= summed) & (me != source))
        def _():
            spread(me).wait_recv()

        @pl.when(me == source)
        def _():
            def wait_spread_sent(i, c):
                j = lax.rem(me + i, n)

                @pl.when(j >= summed)
                def _():
                    spread(j).wait_send()

                return c

            lax.fori_loop(1, n, wait_spread_sent, 0)

    def gather(j, s):
        return pltpu.make_async_remote_copy(
            src_ref=gath.at[s],
            dst_ref=gath.at[s],
            send_sem=gsend.at[j],
            recv_sem=grecv.at[s],
            device_id=dev(j),
            device_id_type=MESH,
        )

    def start_gather(i, c):
        gather(lax.rem(me + i, n), me).start()
        return c

    lax.fori_loop(1, n, start_gather, 0)

    def wait_gather(i, c):
        gather(lax.rem(me + n - i, n), lax.rem(me + n - i, n)).wait_recv()
        gather(lax.rem(me + i, n), me).wait_send()
        return c

    lax.fori_loop(1, n, wait_gather, 0)
    o_ref[...] = gath[...]


def axis_sum(x, axis, other, collective_id, summed_rows, source):
    n = lax.axis_size(axis)
    chunks = x.reshape(n, x.shape[0] // n, x.shape[1])
    summed = summed_rows // chunks.shape[1]
    out = pl.pallas_call(
        functools.partial(sum_kernel, axis, other, n, summed, source),
        out_shape=jax.ShapeDtypeStruct(chunks.shape, chunks.dtype),
        in_specs=[pl.BlockSpec(memory_space=pltpu.VMEM)],
        out_specs=pl.BlockSpec(memory_space=pltpu.VMEM),
        scratch_shapes=[
            pltpu.VMEM(chunks.shape, chunks.dtype),
            pltpu.VMEM(chunks.shape, chunks.dtype),
            pltpu.SemaphoreType.DMA((n,)),
            pltpu.SemaphoreType.DMA((n,)),
            pltpu.SemaphoreType.DMA((n,)),
            pltpu.SemaphoreType.DMA((1,)),
            pltpu.SemaphoreType.DMA((n,)),
            pltpu.SemaphoreType.DMA((n,)),
        ],
        compiler_params=pltpu.CompilerParams(
            collective_id=collective_id, has_side_effects=True
        ),
    )(chunks)
    return out.reshape(x.shape)


def group_kernel(stride, size, mode, x_ref, o_ref, buf, send, recv):
    p = lax.axis_index("prow")
    q = lax.axis_index("pcol")
    me = lax.rem(p // stride, size)
    base = p - me * stride

    def dev(k):
        return (base + k * stride, q)

    barrier = pltpu.get_barrier_semaphore()

    def greet(i, c):
        pl.semaphore_signal(barrier, 1, device_id=dev(lax.rem(me + i, size)), device_id_type=MESH)
        return c

    lax.fori_loop(1, size, greet, 0)
    pl.semaphore_wait(barrier, size - 1)

    def copy(k, s):
        src = x_ref.at[k] if mode == "rs" else buf.at[s]
        return pltpu.make_async_remote_copy(
            src_ref=src,
            dst_ref=buf.at[s],
            send_sem=send.at[k],
            recv_sem=recv.at[s],
            device_id=dev(k),
            device_id_type=MESH,
        )

    if mode == "ag":
        buf[me] = x_ref[...]

    def start(i, c):
        copy(lax.rem(me + i, size), me).start()
        return c

    lax.fori_loop(1, size, start, 0)
    if mode == "rs":
        buf[me] = x_ref[me]

    def wait(i, c):
        s = lax.rem(me + size - i, size)
        copy(s, s).wait_recv()
        copy(lax.rem(me + i, size), me).wait_send()
        return c

    lax.fori_loop(1, size, wait, 0)
    if mode == "rs":
        total = buf[0].astype(jnp.float32)
        for s in range(1, size):
            total = total + buf[s].astype(jnp.float32)
        o_ref[...] = total.astype(o_ref.dtype)
    else:
        o_ref[...] = buf[...]


def group_step(x, stride, size, mode, collective_id):
    if mode == "rs":
        chunks = x.reshape(size, x.shape[0] // size, x.shape[1])
        out_shape = chunks.shape[1:]
        buf_shape = chunks.shape
    else:
        chunks = x
        out_shape = (size,) + x.shape
        buf_shape = out_shape
    out = pl.pallas_call(
        functools.partial(group_kernel, stride, size, mode),
        out_shape=jax.ShapeDtypeStruct(out_shape, x.dtype),
        in_specs=[pl.BlockSpec(memory_space=pltpu.VMEM)],
        out_specs=pl.BlockSpec(memory_space=pltpu.VMEM),
        scratch_shapes=[
            pltpu.VMEM(buf_shape, x.dtype),
            pltpu.SemaphoreType.DMA((size,)),
            pltpu.SemaphoreType.DMA((size,)),
        ],
        compiler_params=pltpu.CompilerParams(
            collective_id=collective_id, has_side_effects=True
        ),
    )(chunks)
    if mode == "ag":
        out = out.reshape(size * x.shape[0], x.shape[1])
    return out


def prow_kernel(xd, yd, top, t_ref, o_ref, b1, a2, b2, b3, b4, sends, recvs, tsend, trecv):
    p = lax.axis_index("prow")
    q = lax.axis_index("pcol")
    xi = lax.rem(p, xd)
    yi = p // xd
    xt, yt = top % xd, top // xd

    def xdev(k):
        return (yi * xd + k, q)

    def ydev(k):
        return (k * xd + xi, q)

    barrier = pltpu.get_barrier_semaphore()

    def greet_x(i, c):
        pl.semaphore_signal(barrier, 1, device_id=xdev(lax.rem(xi + i, xd)), device_id_type=MESH)
        return c

    def greet_y(i, c):
        pl.semaphore_signal(barrier, 1, device_id=ydev(lax.rem(yi + i, yd)), device_id_type=MESH)
        return c

    lax.fori_loop(1, xd, greet_x, 0)
    lax.fori_loop(1, yd, greet_y, 0)
    pl.semaphore_wait(barrier, xd + yd - 2)

    def exchange(phase, src, dst, me, size, dev):
        def copy(k, s):
            return pltpu.make_async_remote_copy(
                src_ref=src(k, s),
                dst_ref=dst(s),
                send_sem=sends.at[phase, k],
                recv_sem=recvs.at[phase, s],
                device_id=dev(k),
                device_id_type=MESH,
            )

        def start(i, c):
            copy(lax.rem(me + i, size), me).start()
            return c

        lax.fori_loop(1, size, start, 0)

        def wait(i, c):
            s = lax.rem(me + size - i, size)
            copy(s, s).wait_recv()
            copy(lax.rem(me + i, size), me).wait_send()
            return c

        lax.fori_loop(1, size, wait, 0)

    def total(parts, size):
        acc = parts(0).astype(jnp.float32)
        for s in range(1, size):
            acc = acc + parts(s).astype(jnp.float32)
        return acc

    def top_copy(k):
        return pltpu.make_async_remote_copy(
            src_ref=t_ref.at[k, 1],
            dst_ref=b1.at[xt, 1],
            send_sem=tsend.at[k],
            recv_sem=trecv.at[0],
            device_id=xdev(k),
            device_id_type=MESH,
        )

    @pl.when(p == top)
    def _():
        def start(i, c):
            top_copy(lax.rem(xi + i, xd)).start()
            return c

        lax.fori_loop(1, xd, start, 0)

    exchange(0, lambda k, s: t_ref.at[k, 0], lambda s: b1.at[s, 0], xi, xd, xdev)
    b1[xi, 0] = t_ref[xi, 0]
    top_half = (yd // 2, b1.shape[2] * 2 // yd, b1.shape[3])
    a2[: yd // 2] = total(lambda s: b1[s, 0], xd).astype(a2.dtype).reshape(top_half)

    @pl.when(p == top)
    def _():
        def sent(i, c):
            top_copy(lax.rem(xi + i, xd)).wait_send()
            return c

        lax.fori_loop(1, xd, sent, 0)
        a3 = t_ref[xi, 1]
        a2[yd // 2 :] = a3.reshape(top_half)

    @pl.when((yi == yt) & (p != top))
    def _():
        top_copy(xi).wait_recv()
        a2[yd // 2 :] = b1[xt, 1].reshape(top_half)

    @pl.when(yi != yt)
    def _():
        a2[yd // 2 :] = jnp.zeros(top_half, a2.dtype)

    def ycopy(k, s):
        return pltpu.make_async_remote_copy(
            src_ref=a2.at[k],
            dst_ref=b2.at[s],
            send_sem=sends.at[1, k],
            recv_sem=recvs.at[1, s],
            device_id=ydev(k),
            device_id_type=MESH,
        )

    def ystart(i, c):
        k = lax.rem(yi + i, yd)

        @pl.when((k < yd // 2) | (yi == yt))
        def _():
            ycopy(k, yi).start()

        return c

    lax.fori_loop(1, yd, ystart, 0)

    @pl.when(yi < yd // 2)
    def _():
        def wait(i, c):
            s = lax.rem(yi + yd - i, yd)
            ycopy(s, s).wait_recv()
            return c

        lax.fori_loop(1, yd, wait, 0)
        b2[yi] = a2[yi]
        b3[yi] = total(lambda s: b2[s], yd).astype(b3.dtype)

    @pl.when((yi >= yd // 2) & (yi != yt))
    def _():
        ycopy(yt, yt).wait_recv()
        b3[yi] = b2[yt]

    @pl.when((yi >= yd // 2) & (yi == yt))
    def _():
        b3[yi] = a2[yi]

    def ysent(i, c):
        k = lax.rem(yi + i, yd)

        @pl.when((k < yd // 2) | (yi == yt))
        def _():
            ycopy(k, yi).wait_send()

        return c

    lax.fori_loop(1, yd, ysent, 0)
    exchange(2, lambda k, s: b3.at[s], lambda s: b3.at[s], yi, yd, ydev)
    b4[xi] = b3[...].reshape(b4.shape[1:])
    exchange(3, lambda k, s: b4.at[s], lambda s: b4.at[s], xi, xd, xdev)
    o_ref[...] = b4[...]


def prow_sum(picked, top_part, xd, top):
    yd = lax.axis_size("prow") // xd
    rows, cols = picked.shape
    chunks = jnp.stack(
        [picked.reshape(xd, rows // xd, cols), top_part.reshape(xd, rows // xd, cols)], axis=1
    )
    part = 2 * rows // xd // yd
    out = pl.pallas_call(
        functools.partial(prow_kernel, xd, yd, top),
        out_shape=jax.ShapeDtypeStruct((xd, yd, part, cols), picked.dtype),
        in_specs=[pl.BlockSpec(memory_space=pltpu.VMEM)],
        out_specs=pl.BlockSpec(memory_space=pltpu.VMEM),
        scratch_shapes=[
            pltpu.VMEM(chunks.shape, picked.dtype),
            pltpu.VMEM((yd, part, cols), picked.dtype),
            pltpu.VMEM((yd, part, cols), picked.dtype),
            pltpu.VMEM((yd, part, cols), picked.dtype),
            pltpu.VMEM((xd, yd, part, cols), picked.dtype),
            pltpu.SemaphoreType.DMA((4, max(xd, yd))),
            pltpu.SemaphoreType.DMA((4, max(xd, yd))),
            pltpu.SemaphoreType.DMA((xd,)),
            pltpu.SemaphoreType.DMA((1,)),
        ],
        compiler_params=pltpu.CompilerParams(collective_id=10 + top, has_side_effects=True),
    )(chunks)
    out = out.reshape(xd, 2, rows // xd, cols)
    return out[:, 0].reshape(rows, cols), out[:, 1].reshape(rows, cols)


def pcol_kernel(nz, source, x_ref, o_ref, g, p1send, p1recv, p2send, p2recv, p3send, p3recv):
    q = lax.axis_index("pcol")
    p = lax.axis_index("prow")
    nc = lax.axis_size("pcol") // nz
    z = q // nc
    c = lax.rem(q, nc)
    zs, cs = source // nc, source % nc

    def dev(zz, cc):
        return (p, zz * nc + cc)

    barrier = pltpu.get_barrier_semaphore()
    n = nz * nc

    def greet(i, carry):
        j = lax.rem(q + i, n)
        pl.semaphore_signal(barrier, 1, device_id=(p, j), device_id_type=MESH)
        return carry

    lax.fori_loop(1, n, greet, 0)
    pl.semaphore_wait(barrier, n - 1)

    def spread(j):
        return pltpu.make_async_remote_copy(
            src_ref=x_ref.at[j],
            dst_ref=g.at[j],
            send_sem=p1send.at[j],
            recv_sem=p1recv.at[0],
            device_id=dev(j, cs),
            device_id_type=MESH,
        )

    def ring(j, s):
        return pltpu.make_async_remote_copy(
            src_ref=g.at[s],
            dst_ref=g.at[s],
            send_sem=p2send.at[j],
            recv_sem=p2recv.at[s],
            device_id=dev(j, cs),
            device_id_type=MESH,
        )

    def partner(zz):
        return pltpu.make_async_remote_copy(
            src_ref=g,
            dst_ref=g,
            send_sem=p3send.at[0],
            recv_sem=p3recv.at[0],
            device_id=dev(zz, 1 - cs),
            device_id_type=MESH,
        )

    @pl.when(q == source)
    def _():
        def start(i, carry):
            spread(lax.rem(zs + i, nz)).start()
            return carry

        lax.fori_loop(1, nz, start, 0)
        g[zs] = x_ref[zs]

        def sent(i, carry):
            spread(lax.rem(zs + i, nz)).wait_send()
            return carry

        lax.fori_loop(1, nz, sent, 0)

    @pl.when((c == cs) & (z != zs))
    def _():
        spread(z).wait_recv()

    @pl.when(c == cs)
    def _():
        def start(i, carry):
            ring(lax.rem(z + i, nz), z).start()
            return carry

        lax.fori_loop(1, nz, start, 0)

        def wait(i, carry):
            s = lax.rem(z + nz - i, nz)
            ring(s, s).wait_recv()
            ring(lax.rem(z + i, nz), z).wait_send()
            return carry

        lax.fori_loop(1, nz, wait, 0)
        partner(z).start()
        partner(z).wait_send()

    @pl.when(c != cs)
    def _():
        partner(z).wait_recv()

    o_ref[...] = g[...]


def pcol_bcast(x, nz, source, collective_id):
    rows, cols = x.shape
    chunks = x.reshape(nz, rows // nz, cols)
    out = pl.pallas_call(
        functools.partial(pcol_kernel, nz, source),
        out_shape=jax.ShapeDtypeStruct(chunks.shape, x.dtype),
        in_specs=[pl.BlockSpec(memory_space=pltpu.VMEM)],
        out_specs=pl.BlockSpec(memory_space=pltpu.VMEM),
        scratch_shapes=[
            pltpu.VMEM(chunks.shape, x.dtype),
            pltpu.SemaphoreType.DMA((nz,)),
            pltpu.SemaphoreType.DMA((1,)),
            pltpu.SemaphoreType.DMA((nz,)),
            pltpu.SemaphoreType.DMA((nz,)),
            pltpu.SemaphoreType.DMA((1,)),
            pltpu.SemaphoreType.DMA((1,)),
        ],
        compiler_params=pltpu.CompilerParams(collective_id=collective_id, has_side_effects=True),
    )(chunks)
    return out.reshape(rows, cols)


def local(x_devices, z_chips, matrix, pivots, lower_inverse, upper_inverse):
    row_count = lax.axis_size("prow")
    col_count = lax.axis_size("pcol")
    my_row = lax.axis_index("prow")
    my_col = lax.axis_index("pcol")
    blocks_down, block, blocks_across, _ = matrix.shape
    local_rows = blocks_down * block
    local_cols = blocks_across * block
    current = matrix.reshape(local_rows, local_cols)
    row_place = jnp.arange(local_rows)
    col_place = jnp.arange(local_cols)
    global_rows = (row_place // block * row_count + my_row) * block + row_place % block
    global_cols = (col_place // block * col_count + my_col) * block + col_place % block
    for panel in range(pivots.shape[0]):
        start = panel * block
        chosen = pivots[panel]
        block_row = chosen // block
        is_mine = block_row % row_count == my_row
        local_index = block_row // row_count * block + chosen % block
        safe_index = jnp.where(is_mine, local_index, 0)
        picked = jnp.where(is_mine[:, None], current[safe_index], jnp.zeros((), jnp.bfloat16))
        top_holder = panel % row_count
        top_first = panel // row_count * block
        is_top = my_row == top_holder
        top_local = current[top_first : top_first + block]
        top_part = jnp.where(is_top, top_local, jnp.zeros((), jnp.bfloat16))
        incoming, old_top = prow_sum(picked, top_part, x_devices, top_holder)
        target = jnp.where(is_mine, local_index, local_rows)
        current = current.at[target].set(old_top, mode="drop")
        top_now = current[top_first : top_first + block]
        current = current.at[top_first : top_first + block].set(
            jnp.where(is_top, incoming, top_now)
        )
        panel_holder = panel % col_count
        panel_first = panel // col_count * block
        panel_cols = current[:, panel_first : panel_first + block]
        factor = jnp.dot(
            panel_cols, upper_inverse[panel], preferred_element_type=jnp.float32
        ).astype(jnp.bfloat16)
        is_panel = my_col == panel_holder
        factor = jnp.where(is_panel, factor, jnp.zeros((), jnp.bfloat16))
        lower = pcol_bcast(factor, z_chips, panel_holder, 20 + panel)
        upper = jnp.dot(
            lower_inverse[panel], incoming, preferred_element_type=jnp.float32
        ).astype(jnp.bfloat16)
        row_mask = global_rows >= start + block
        col_mask = global_cols >= start + block
        product = jnp.dot(lower, upper, preferred_element_type=jnp.float32)
        changed = (current.astype(jnp.float32) - product).astype(jnp.bfloat16)
        below = row_mask[:, None]
        right = col_mask[None, :]
        in_panel = is_panel & (col_place // block == panel_first // block)[None, :]
        in_top = is_top & (row_place // block == top_first // block)[:, None]
        lower_wide = jnp.broadcast_to(
            lower[:, None, :], (local_rows, blocks_across, block)
        ).reshape(local_rows, local_cols)
        upper_tall = jnp.broadcast_to(
            upper[None], (blocks_down, block, local_cols)
        ).reshape(local_rows, local_cols)
        current = jnp.where(
            below & right,
            changed,
            jnp.where(
                in_panel & below,
                lower_wide,
                jnp.where(in_top & right, upper_tall, current),
            ),
        )
    return current.reshape(matrix.shape)


def solution(mesh):
    x_devices = len({d.coords[0] for d in mesh.devices[:, 0]})
    z_chips = len({d.coords[2] for d in mesh.devices[0, :]})
    in_specs = (P(None, "prow", None, "pcol"), P(), P(), P())
    out_specs = P(None, "prow", None, "pcol")
    return jax.shard_map(functools.partial(local, x_devices, z_chips), mesh=mesh, in_specs=in_specs, out_specs=out_specs, check_vma=False)
```

```python
import functools

import jax
import jax.numpy as jnp
from jax import lax
from jax.experimental import pallas as pl
from jax.experimental.pallas import tpu as pltpu
from jax.sharding import PartitionSpec as P

MESH = pl.DeviceIdType.MESH


def sum_kernel(axis, other, n, summed, source, x_ref, o_ref, recv, gath, ssend, srecv,
               bsend, brecv, gsend, grecv):
    me = lax.axis_index(axis)
    them = lax.axis_index(other)

    def dev(j):
        return (j, them) if axis == "prow" else (them, j)

    barrier = pltpu.get_barrier_semaphore()

    def greet(i, c):
        j = lax.rem(me + i, n)
        pl.semaphore_signal(barrier, 1, device_id=dev(j), device_id_type=MESH)
        return c

    lax.fori_loop(1, n, greet, 0)
    pl.semaphore_wait(barrier, n - 1)

    def scatter(j, s):
        return pltpu.make_async_remote_copy(
            src_ref=x_ref.at[j],
            dst_ref=recv.at[s],
            send_sem=ssend.at[j],
            recv_sem=srecv.at[s],
            device_id=dev(j),
            device_id_type=MESH,
        )

    def spread(j):
        return pltpu.make_async_remote_copy(
            src_ref=x_ref.at[j],
            dst_ref=gath.at[j],
            send_sem=bsend.at[j],
            recv_sem=brecv.at[0],
            device_id=dev(j),
            device_id_type=MESH,
        )

    if summed > 0:
        def start_scatter(i, c):
            j = lax.rem(me + i, n)

            @pl.when(j < summed)
            def _():
                scatter(j, me).start()

            return c

        lax.fori_loop(1, n, start_scatter, 0)

    if summed < n:
        @pl.when(me == source)
        def _():
            def start_spread(i, c):
                j = lax.rem(me + i, n)

                @pl.when(j >= summed)
                def _():
                    spread(j).start()

                return c

            lax.fori_loop(1, n, start_spread, 0)
            if source >= summed:
                gath[source] = x_ref[source]

    if summed > 0:
        @pl.when(me < summed)
        def _():
            recv[me] = x_ref[me]

            def wait_scatter(i, c):
                s = lax.rem(me + n - i, n)
                scatter(s, s).wait_recv()
                return c

            lax.fori_loop(1, n, wait_scatter, 0)
            total = recv[0].astype(jnp.float32)
            for s in range(1, n):
                total = total + recv[s].astype(jnp.float32)
            gath[me] = total.astype(gath.dtype)

        def wait_scatter_sent(i, c):
            j = lax.rem(me + i, n)

            @pl.when(j < summed)
            def _():
                scatter(j, me).wait_send()

            return c

        lax.fori_loop(1, n, wait_scatter_sent, 0)

    if summed < n:
        @pl.when((me >= summed) & (me != source))
        def _():
            spread(me).wait_recv()

        @pl.when(me == source)
        def _():
            def wait_spread_sent(i, c):
                j = lax.rem(me + i, n)

                @pl.when(j >= summed)
                def _():
                    spread(j).wait_send()

                return c

            lax.fori_loop(1, n, wait_spread_sent, 0)

    def gather(j, s):
        return pltpu.make_async_remote_copy(
            src_ref=gath.at[s],
            dst_ref=gath.at[s],
            send_sem=gsend.at[j],
            recv_sem=grecv.at[s],
            device_id=dev(j),
            device_id_type=MESH,
        )

    def start_gather(i, c):
        gather(lax.rem(me + i, n), me).start()
        return c

    lax.fori_loop(1, n, start_gather, 0)

    def wait_gather(i, c):
        gather(lax.rem(me + n - i, n), lax.rem(me + n - i, n)).wait_recv()
        gather(lax.rem(me + i, n), me).wait_send()
        return c

    lax.fori_loop(1, n, wait_gather, 0)
    o_ref[...] = gath[...]


def axis_sum(x, axis, other, collective_id, summed_rows, source):
    n = lax.axis_size(axis)
    chunks = x.reshape(n, x.shape[0] // n, x.shape[1])
    summed = summed_rows // chunks.shape[1]
    out = pl.pallas_call(
        functools.partial(sum_kernel, axis, other, n, summed, source),
        out_shape=jax.ShapeDtypeStruct(chunks.shape, chunks.dtype),
        in_specs=[pl.BlockSpec(memory_space=pltpu.VMEM)],
        out_specs=pl.BlockSpec(memory_space=pltpu.VMEM),
        scratch_shapes=[
            pltpu.VMEM(chunks.shape, chunks.dtype),
            pltpu.VMEM(chunks.shape, chunks.dtype),
            pltpu.SemaphoreType.DMA((n,)),
            pltpu.SemaphoreType.DMA((n,)),
            pltpu.SemaphoreType.DMA((n,)),
            pltpu.SemaphoreType.DMA((1,)),
            pltpu.SemaphoreType.DMA((n,)),
            pltpu.SemaphoreType.DMA((n,)),
        ],
        compiler_params=pltpu.CompilerParams(
            collective_id=collective_id, has_side_effects=True
        ),
    )(chunks)
    return out.reshape(x.shape)


def group_kernel(stride, size, mode, x_ref, o_ref, buf, send, recv):
    p = lax.axis_index("prow")
    q = lax.axis_index("pcol")
    me = lax.rem(p // stride, size)
    base = p - me * stride

    def dev(k):
        return (base + k * stride, q)

    barrier = pltpu.get_barrier_semaphore()

    def greet(i, c):
        pl.semaphore_signal(barrier, 1, device_id=dev(lax.rem(me + i, size)), device_id_type=MESH)
        return c

    lax.fori_loop(1, size, greet, 0)
    pl.semaphore_wait(barrier, size - 1)

    def copy(k, s):
        src = x_ref.at[k] if mode == "rs" else buf.at[s]
        return pltpu.make_async_remote_copy(
            src_ref=src,
            dst_ref=buf.at[s],
            send_sem=send.at[k],
            recv_sem=recv.at[s],
            device_id=dev(k),
            device_id_type=MESH,
        )

    if mode == "ag":
        buf[me] = x_ref[...]

    def start(i, c):
        copy(lax.rem(me + i, size), me).start()
        return c

    lax.fori_loop(1, size, start, 0)
    if mode == "rs":
        buf[me] = x_ref[me]

    def wait(i, c):
        s = lax.rem(me + size - i, size)
        copy(s, s).wait_recv()
        copy(lax.rem(me + i, size), me).wait_send()
        return c

    lax.fori_loop(1, size, wait, 0)
    if mode == "rs":
        total = buf[0].astype(jnp.float32)
        for s in range(1, size):
            total = total + buf[s].astype(jnp.float32)
        o_ref[...] = total.astype(o_ref.dtype)
    else:
        o_ref[...] = buf[...]


def group_step(x, stride, size, mode, collective_id):
    if mode == "rs":
        chunks = x.reshape(size, x.shape[0] // size, x.shape[1])
        out_shape = chunks.shape[1:]
        buf_shape = chunks.shape
    else:
        chunks = x
        out_shape = (size,) + x.shape
        buf_shape = out_shape
    out = pl.pallas_call(
        functools.partial(group_kernel, stride, size, mode),
        out_shape=jax.ShapeDtypeStruct(out_shape, x.dtype),
        in_specs=[pl.BlockSpec(memory_space=pltpu.VMEM)],
        out_specs=pl.BlockSpec(memory_space=pltpu.VMEM),
        scratch_shapes=[
            pltpu.VMEM(buf_shape, x.dtype),
            pltpu.SemaphoreType.DMA((size,)),
            pltpu.SemaphoreType.DMA((size,)),
        ],
        compiler_params=pltpu.CompilerParams(
            collective_id=collective_id, has_side_effects=True
        ),
    )(chunks)
    if mode == "ag":
        out = out.reshape(size * x.shape[0], x.shape[1])
    return out


def prow_kernel(xd, yd, top, t_ref, o_ref, b1, a2, b2, b3, b4, sends, recvs, tsend, trecv, rsend, trecv2):
    p = lax.axis_index("prow")
    q = lax.axis_index("pcol")
    xi = lax.rem(p, xd)
    yi = p // xd
    xt, yt = top % xd, top // xd

    def xdev(k):
        return (yi * xd + k, q)

    def ydev(k):
        return (k * xd + xi, q)

    barrier = pltpu.get_barrier_semaphore()

    def greet_x(i, c):
        pl.semaphore_signal(barrier, 1, device_id=xdev(lax.rem(xi + i, xd)), device_id_type=MESH)
        return c

    def greet_y(i, c):
        pl.semaphore_signal(barrier, 1, device_id=ydev(lax.rem(yi + i, yd)), device_id_type=MESH)
        return c

    lax.fori_loop(1, xd, greet_x, 0)
    lax.fori_loop(1, yd, greet_y, 0)
    pl.semaphore_wait(barrier, xd + yd - 2)

    def exchange(phase, src, dst, me, size, dev):
        def copy(k, s):
            return pltpu.make_async_remote_copy(
                src_ref=src(k, s),
                dst_ref=dst(s),
                send_sem=sends.at[phase, k],
                recv_sem=recvs.at[phase, s],
                device_id=dev(k),
                device_id_type=MESH,
            )

        def start(i, c):
            copy(lax.rem(me + i, size), me).start()
            return c

        lax.fori_loop(1, size, start, 0)

        def wait(i, c):
            s = lax.rem(me + size - i, size)
            copy(s, s).wait_recv()
            copy(lax.rem(me + i, size), me).wait_send()
            return c

        lax.fori_loop(1, size, wait, 0)

    def total(parts, size):
        acc = parts(0).astype(jnp.float32)
        for s in range(1, size):
            acc = acc + parts(s).astype(jnp.float32)
        return acc

    def top_copy(k):
        return pltpu.make_async_remote_copy(
            src_ref=t_ref.at[k, 1],
            dst_ref=b1.at[xt, 1],
            send_sem=tsend.at[k],
            recv_sem=trecv.at[0],
            device_id=xdev(k),
            device_id_type=MESH,
        )

    @pl.when(p == top)
    def _():
        def start(i, c):
            top_copy(lax.rem(xi + i, xd)).start()
            return c

        lax.fori_loop(1, xd, start, 0)

    exchange(0, lambda k, s: t_ref.at[k, 0], lambda s: b1.at[s, 0], xi, xd, xdev)
    b1[xi, 0] = t_ref[xi, 0]
    top_half = (yd // 2, b1.shape[2] * 2 // yd, b1.shape[3])
    a2[: yd // 2] = total(lambda s: b1[s, 0], xd).astype(a2.dtype).reshape(top_half)

    @pl.when(p == top)
    def _():
        def sent(i, c):
            top_copy(lax.rem(xi + i, xd)).wait_send()
            return c

        lax.fori_loop(1, xd, sent, 0)
        a3 = t_ref[xi, 1]
        a2[yd // 2 :] = a3.reshape(top_half)

    @pl.when((yi == yt) & (p != top))
    def _():
        top_copy(xi).wait_recv()
        a2[yd // 2 :] = b1[xt, 1].reshape(top_half)

    @pl.when(yi != yt)
    def _():
        a2[yd // 2 :] = jnp.zeros(top_half, a2.dtype)

    def ycopy(k, s):
        return pltpu.make_async_remote_copy(
            src_ref=a2.at[k],
            dst_ref=b2.at[s],
            send_sem=sends.at[1, k],
            recv_sem=recvs.at[1, s],
            device_id=ydev(k),
            device_id_type=MESH,
        )

    def ystart(i, c):
        k = lax.rem(yi + i, yd)

        @pl.when((k < yd // 2) | (yi == yt))
        def _():
            ycopy(k, yi).start()

        return c

    lax.fori_loop(1, yd, ystart, 0)

    @pl.when(yi < yd // 2)
    def _():
        def wait(i, c):
            s = lax.rem(yi + yd - i, yd)
            ycopy(s, s).wait_recv()
            return c

        lax.fori_loop(1, yd, wait, 0)
        b2[yi] = a2[yi]
        b3[yi] = total(lambda s: b2[s], yd).astype(b3.dtype)

    @pl.when((yi >= yd // 2) & (yi != yt))
    def _():
        ycopy(yt, yt).wait_recv()
        b3[yi] = b2[yt]

    @pl.when((yi >= yd // 2) & (yi == yt))
    def _():
        b3[yi] = a2[yi]

    def ysent(i, c):
        k = lax.rem(yi + i, yd)

        @pl.when((k < yd // 2) | (yi == yt))
        def _():
            ycopy(k, yi).wait_send()

        return c

    lax.fori_loop(1, yd, ysent, 0)
    exchange(2, lambda k, s: b3.at[s], lambda s: b3.at[s], yi, yd, ydev)
    b4[xi] = b3[...].reshape(b4.shape[1:])
    if xd == 4:
        left, right = lax.rem(xi + 3, 4), lax.rem(xi + 1, 4)
        h = yd // 2

        def near(k, s):
            return pltpu.make_async_remote_copy(
                src_ref=b4.at[s],
                dst_ref=b4.at[s],
                send_sem=sends.at[3, k],
                recv_sem=recvs.at[3, s],
                device_id=xdev(k),
                device_id_type=MESH,
            )

        def relay(k, s, lo, slot):
            return pltpu.make_async_remote_copy(
                src_ref=b4.at[s, pl.ds(lo, h)],
                dst_ref=b4.at[s, pl.ds(lo, h)],
                send_sem=rsend.at[slot],
                recv_sem=trecv2.at[slot],
                device_id=xdev(k),
                device_id_type=MESH,
            )

        near(right, xi).start()
        near(left, xi).start()
        near(left, left).wait_recv()
        relay(right, left, h, 1).start()
        near(right, right).wait_recv()
        relay(left, right, 0, 0).start()
        far = lax.rem(xi + 2, 4)
        relay(left, far, h, 1).wait_recv()
        relay(right, far, 0, 0).wait_recv()
        near(right, xi).wait_send()
        near(left, xi).wait_send()
        relay(right, left, h, 1).wait_send()
        relay(left, right, 0, 0).wait_send()
    else:
        exchange(3, lambda k, s: b4.at[s], lambda s: b4.at[s], xi, xd, xdev)
    o_ref[...] = b4[...]


def prow_sum(picked, top_part, xd, top):
    yd = lax.axis_size("prow") // xd
    rows, cols = picked.shape
    chunks = jnp.stack(
        [picked.reshape(xd, rows // xd, cols), top_part.reshape(xd, rows // xd, cols)], axis=1
    )
    part = 2 * rows // xd // yd
    out = pl.pallas_call(
        functools.partial(prow_kernel, xd, yd, top),
        out_shape=jax.ShapeDtypeStruct((xd, yd, part, cols), picked.dtype),
        in_specs=[pl.BlockSpec(memory_space=pltpu.VMEM)],
        out_specs=pl.BlockSpec(memory_space=pltpu.VMEM),
        scratch_shapes=[
            pltpu.VMEM(chunks.shape, picked.dtype),
            pltpu.VMEM((yd, part, cols), picked.dtype),
            pltpu.VMEM((yd, part, cols), picked.dtype),
            pltpu.VMEM((yd, part, cols), picked.dtype),
            pltpu.VMEM((xd, yd, part, cols), picked.dtype),
            pltpu.SemaphoreType.DMA((4, max(xd, yd))),
            pltpu.SemaphoreType.DMA((4, max(xd, yd))),
            pltpu.SemaphoreType.DMA((xd,)),
            pltpu.SemaphoreType.DMA((1,)),
            pltpu.SemaphoreType.DMA((2,)),
            pltpu.SemaphoreType.DMA((2,)),
        ],
        compiler_params=pltpu.CompilerParams(collective_id=10 + top, has_side_effects=True),
    )(chunks)
    out = out.reshape(xd, 2, rows // xd, cols)
    return out[:, 0].reshape(rows, cols), out[:, 1].reshape(rows, cols)


def pcol_kernel(nz, source, x_ref, o_ref, g, p1send, p1recv, p2send, p2recv, p3send, p3recv):
    q = lax.axis_index("pcol")
    p = lax.axis_index("prow")
    nc = lax.axis_size("pcol") // nz
    z = q // nc
    c = lax.rem(q, nc)
    zs, cs = source // nc, source % nc

    def dev(zz, cc):
        return (p, zz * nc + cc)

    barrier = pltpu.get_barrier_semaphore()
    n = nz * nc

    def greet(i, carry):
        j = lax.rem(q + i, n)
        pl.semaphore_signal(barrier, 1, device_id=(p, j), device_id_type=MESH)
        return carry

    lax.fori_loop(1, n, greet, 0)
    pl.semaphore_wait(barrier, n - 1)

    def spread(j):
        return pltpu.make_async_remote_copy(
            src_ref=x_ref.at[j],
            dst_ref=g.at[j],
            send_sem=p1send.at[j],
            recv_sem=p1recv.at[0],
            device_id=dev(j, cs),
            device_id_type=MESH,
        )

    def ring(j, s):
        return pltpu.make_async_remote_copy(
            src_ref=g.at[s],
            dst_ref=g.at[s],
            send_sem=p2send.at[j],
            recv_sem=p2recv.at[s],
            device_id=dev(j, cs),
            device_id_type=MESH,
        )

    def partner(zz):
        return pltpu.make_async_remote_copy(
            src_ref=g,
            dst_ref=g,
            send_sem=p3send.at[0],
            recv_sem=p3recv.at[0],
            device_id=dev(zz, 1 - cs),
            device_id_type=MESH,
        )

    @pl.when(q == source)
    def _():
        def start(i, carry):
            spread(lax.rem(zs + i, nz)).start()
            return carry

        lax.fori_loop(1, nz, start, 0)
        g[zs] = x_ref[zs]

        def sent(i, carry):
            spread(lax.rem(zs + i, nz)).wait_send()
            return carry

        lax.fori_loop(1, nz, sent, 0)

    @pl.when((c == cs) & (z != zs))
    def _():
        spread(z).wait_recv()

    @pl.when(c == cs)
    def _():
        def start(i, carry):
            ring(lax.rem(z + i, nz), z).start()
            return carry

        lax.fori_loop(1, nz, start, 0)

        def wait(i, carry):
            s = lax.rem(z + nz - i, nz)
            ring(s, s).wait_recv()
            ring(lax.rem(z + i, nz), z).wait_send()
            return carry

        lax.fori_loop(1, nz, wait, 0)
        partner(z).start()
        partner(z).wait_send()

    @pl.when(c != cs)
    def _():
        partner(z).wait_recv()

    o_ref[...] = g[...]


def pcol_bcast(x, nz, source, collective_id):
    rows, cols = x.shape
    chunks = x.reshape(nz, rows // nz, cols)
    out = pl.pallas_call(
        functools.partial(pcol_kernel, nz, source),
        out_shape=jax.ShapeDtypeStruct(chunks.shape, x.dtype),
        in_specs=[pl.BlockSpec(memory_space=pltpu.VMEM)],
        out_specs=pl.BlockSpec(memory_space=pltpu.VMEM),
        scratch_shapes=[
            pltpu.VMEM(chunks.shape, x.dtype),
            pltpu.SemaphoreType.DMA((nz,)),
            pltpu.SemaphoreType.DMA((1,)),
            pltpu.SemaphoreType.DMA((nz,)),
            pltpu.SemaphoreType.DMA((nz,)),
            pltpu.SemaphoreType.DMA((1,)),
            pltpu.SemaphoreType.DMA((1,)),
        ],
        compiler_params=pltpu.CompilerParams(collective_id=collective_id, has_side_effects=True),
    )(chunks)
    return out.reshape(rows, cols)


def local(x_devices, z_chips, matrix, pivots, lower_inverse, upper_inverse):
    row_count = lax.axis_size("prow")
    col_count = lax.axis_size("pcol")
    my_row = lax.axis_index("prow")
    my_col = lax.axis_index("pcol")
    blocks_down, block, blocks_across, _ = matrix.shape
    local_rows = blocks_down * block
    local_cols = blocks_across * block
    current = matrix.reshape(local_rows, local_cols)
    row_place = jnp.arange(local_rows)
    col_place = jnp.arange(local_cols)
    global_rows = (row_place // block * row_count + my_row) * block + row_place % block
    global_cols = (col_place // block * col_count + my_col) * block + col_place % block
    for panel in range(pivots.shape[0]):
        start = panel * block
        chosen = pivots[panel]
        block_row = chosen // block
        is_mine = block_row % row_count == my_row
        local_index = block_row // row_count * block + chosen % block
        safe_index = jnp.where(is_mine, local_index, 0)
        picked = jnp.where(is_mine[:, None], current[safe_index], jnp.zeros((), jnp.bfloat16))
        top_holder = panel % row_count
        top_first = panel // row_count * block
        is_top = my_row == top_holder
        top_local = current[top_first : top_first + block]
        top_part = jnp.where(is_top, top_local, jnp.zeros((), jnp.bfloat16))
        incoming, old_top = prow_sum(picked, top_part, x_devices, top_holder)
        target = jnp.where(is_mine, local_index, local_rows)
        current = current.at[target].set(old_top, mode="drop")
        top_now = current[top_first : top_first + block]
        current = current.at[top_first : top_first + block].set(
            jnp.where(is_top, incoming, top_now)
        )
        panel_holder = panel % col_count
        panel_first = panel // col_count * block
        panel_cols = current[:, panel_first : panel_first + block]
        factor = jnp.dot(
            panel_cols, upper_inverse[panel], preferred_element_type=jnp.float32
        ).astype(jnp.bfloat16)
        is_panel = my_col == panel_holder
        factor = jnp.where(is_panel, factor, jnp.zeros((), jnp.bfloat16))
        lower = pcol_bcast(factor, z_chips, panel_holder, 20 + panel)
        upper = jnp.dot(
            lower_inverse[panel], incoming, preferred_element_type=jnp.float32
        ).astype(jnp.bfloat16)
        row_mask = global_rows >= start + block
        col_mask = global_cols >= start + block
        product = jnp.dot(lower, upper, preferred_element_type=jnp.float32)
        changed = (current.astype(jnp.float32) - product).astype(jnp.bfloat16)
        below = row_mask[:, None]
        right = col_mask[None, :]
        in_panel = is_panel & (col_place // block == panel_first // block)[None, :]
        in_top = is_top & (row_place // block == top_first // block)[:, None]
        lower_wide = jnp.broadcast_to(
            lower[:, None, :], (local_rows, blocks_across, block)
        ).reshape(local_rows, local_cols)
        upper_tall = jnp.broadcast_to(
            upper[None], (blocks_down, block, local_cols)
        ).reshape(local_rows, local_cols)
        current = jnp.where(
            below & right,
            changed,
            jnp.where(
                in_panel & below,
                lower_wide,
                jnp.where(in_top & right, upper_tall, current),
            ),
        )
    return current.reshape(matrix.shape)


def solution(mesh):
    x_devices = len({d.coords[0] for d in mesh.devices[:, 0]})
    z_chips = len({d.coords[2] for d in mesh.devices[0, :]})
    in_specs = (P(None, "prow", None, "pcol"), P(), P(), P())
    out_specs = P(None, "prow", None, "pcol")
    return jax.shard_map(functools.partial(local, x_devices, z_chips), mesh=mesh, in_specs=in_specs, out_specs=out_specs, check_vma=False)
```

```python
import functools

import jax
import jax.numpy as jnp
from jax import lax
from jax.experimental import pallas as pl
from jax.experimental.pallas import tpu as pltpu
from jax.sharding import PartitionSpec as P

MESH = pl.DeviceIdType.MESH


def sum_kernel(axis, other, n, summed, source, x_ref, o_ref, recv, gath, ssend, srecv,
               bsend, brecv, gsend, grecv):
    me = lax.axis_index(axis)
    them = lax.axis_index(other)

    def dev(j):
        return (j, them) if axis == "prow" else (them, j)

    barrier = pltpu.get_barrier_semaphore()

    def greet(i, c):
        j = lax.rem(me + i, n)
        pl.semaphore_signal(barrier, 1, device_id=dev(j), device_id_type=MESH)
        return c

    lax.fori_loop(1, n, greet, 0)
    pl.semaphore_wait(barrier, n - 1)

    def scatter(j, s):
        return pltpu.make_async_remote_copy(
            src_ref=x_ref.at[j],
            dst_ref=recv.at[s],
            send_sem=ssend.at[j],
            recv_sem=srecv.at[s],
            device_id=dev(j),
            device_id_type=MESH,
        )

    def spread(j):
        return pltpu.make_async_remote_copy(
            src_ref=x_ref.at[j],
            dst_ref=gath.at[j],
            send_sem=bsend.at[j],
            recv_sem=brecv.at[0],
            device_id=dev(j),
            device_id_type=MESH,
        )

    if summed > 0:
        def start_scatter(i, c):
            j = lax.rem(me + i, n)

            @pl.when(j < summed)
            def _():
                scatter(j, me).start()

            return c

        lax.fori_loop(1, n, start_scatter, 0)

    if summed < n:
        @pl.when(me == source)
        def _():
            def start_spread(i, c):
                j = lax.rem(me + i, n)

                @pl.when(j >= summed)
                def _():
                    spread(j).start()

                return c

            lax.fori_loop(1, n, start_spread, 0)
            if source >= summed:
                gath[source] = x_ref[source]

    if summed > 0:
        @pl.when(me < summed)
        def _():
            recv[me] = x_ref[me]

            def wait_scatter(i, c):
                s = lax.rem(me + n - i, n)
                scatter(s, s).wait_recv()
                return c

            lax.fori_loop(1, n, wait_scatter, 0)
            total = recv[0].astype(jnp.float32)
            for s in range(1, n):
                total = total + recv[s].astype(jnp.float32)
            gath[me] = total.astype(gath.dtype)

        def wait_scatter_sent(i, c):
            j = lax.rem(me + i, n)

            @pl.when(j < summed)
            def _():
                scatter(j, me).wait_send()

            return c

        lax.fori_loop(1, n, wait_scatter_sent, 0)

    if summed < n:
        @pl.when((me >= summed) & (me != source))
        def _():
            spread(me).wait_recv()

        @pl.when(me == source)
        def _():
            def wait_spread_sent(i, c):
                j = lax.rem(me + i, n)

                @pl.when(j >= summed)
                def _():
                    spread(j).wait_send()

                return c

            lax.fori_loop(1, n, wait_spread_sent, 0)

    def gather(j, s):
        return pltpu.make_async_remote_copy(
            src_ref=gath.at[s],
            dst_ref=gath.at[s],
            send_sem=gsend.at[j],
            recv_sem=grecv.at[s],
            device_id=dev(j),
            device_id_type=MESH,
        )

    def start_gather(i, c):
        gather(lax.rem(me + i, n), me).start()
        return c

    lax.fori_loop(1, n, start_gather, 0)

    def wait_gather(i, c):
        gather(lax.rem(me + n - i, n), lax.rem(me + n - i, n)).wait_recv()
        gather(lax.rem(me + i, n), me).wait_send()
        return c

    lax.fori_loop(1, n, wait_gather, 0)
    o_ref[...] = gath[...]


def axis_sum(x, axis, other, collective_id, summed_rows, source):
    n = lax.axis_size(axis)
    chunks = x.reshape(n, x.shape[0] // n, x.shape[1])
    summed = summed_rows // chunks.shape[1]
    out = pl.pallas_call(
        functools.partial(sum_kernel, axis, other, n, summed, source),
        out_shape=jax.ShapeDtypeStruct(chunks.shape, chunks.dtype),
        in_specs=[pl.BlockSpec(memory_space=pltpu.VMEM)],
        out_specs=pl.BlockSpec(memory_space=pltpu.VMEM),
        scratch_shapes=[
            pltpu.VMEM(chunks.shape, chunks.dtype),
            pltpu.VMEM(chunks.shape, chunks.dtype),
            pltpu.SemaphoreType.DMA((n,)),
            pltpu.SemaphoreType.DMA((n,)),
            pltpu.SemaphoreType.DMA((n,)),
            pltpu.SemaphoreType.DMA((1,)),
            pltpu.SemaphoreType.DMA((n,)),
            pltpu.SemaphoreType.DMA((n,)),
        ],
        compiler_params=pltpu.CompilerParams(
            collective_id=collective_id, has_side_effects=True
        ),
    )(chunks)
    return out.reshape(x.shape)


def group_kernel(stride, size, mode, x_ref, o_ref, buf, send, recv):
    p = lax.axis_index("prow")
    q = lax.axis_index("pcol")
    me = lax.rem(p // stride, size)
    base = p - me * stride

    def dev(k):
        return (base + k * stride, q)

    barrier = pltpu.get_barrier_semaphore()

    def greet(i, c):
        pl.semaphore_signal(barrier, 1, device_id=dev(lax.rem(me + i, size)), device_id_type=MESH)
        return c

    lax.fori_loop(1, size, greet, 0)
    pl.semaphore_wait(barrier, size - 1)

    def copy(k, s):
        src = x_ref.at[k] if mode == "rs" else buf.at[s]
        return pltpu.make_async_remote_copy(
            src_ref=src,
            dst_ref=buf.at[s],
            send_sem=send.at[k],
            recv_sem=recv.at[s],
            device_id=dev(k),
            device_id_type=MESH,
        )

    if mode == "ag":
        buf[me] = x_ref[...]

    def start(i, c):
        copy(lax.rem(me + i, size), me).start()
        return c

    lax.fori_loop(1, size, start, 0)
    if mode == "rs":
        buf[me] = x_ref[me]

    def wait(i, c):
        s = lax.rem(me + size - i, size)
        copy(s, s).wait_recv()
        copy(lax.rem(me + i, size), me).wait_send()
        return c

    lax.fori_loop(1, size, wait, 0)
    if mode == "rs":
        total = buf[0].astype(jnp.float32)
        for s in range(1, size):
            total = total + buf[s].astype(jnp.float32)
        o_ref[...] = total.astype(o_ref.dtype)
    else:
        o_ref[...] = buf[...]


def group_step(x, stride, size, mode, collective_id):
    if mode == "rs":
        chunks = x.reshape(size, x.shape[0] // size, x.shape[1])
        out_shape = chunks.shape[1:]
        buf_shape = chunks.shape
    else:
        chunks = x
        out_shape = (size,) + x.shape
        buf_shape = out_shape
    out = pl.pallas_call(
        functools.partial(group_kernel, stride, size, mode),
        out_shape=jax.ShapeDtypeStruct(out_shape, x.dtype),
        in_specs=[pl.BlockSpec(memory_space=pltpu.VMEM)],
        out_specs=pl.BlockSpec(memory_space=pltpu.VMEM),
        scratch_shapes=[
            pltpu.VMEM(buf_shape, x.dtype),
            pltpu.SemaphoreType.DMA((size,)),
            pltpu.SemaphoreType.DMA((size,)),
        ],
        compiler_params=pltpu.CompilerParams(
            collective_id=collective_id, has_side_effects=True
        ),
    )(chunks)
    if mode == "ag":
        out = out.reshape(size * x.shape[0], x.shape[1])
    return out


def prow_kernel(xd, yd, top, t_ref, o_ref, b1, a2, b2, b3, b4, sends, recvs, tsend, trecv):
    p = lax.axis_index("prow")
    q = lax.axis_index("pcol")
    xi = lax.rem(p, xd)
    yi = p // xd
    xt, yt = top % xd, top // xd

    def xdev(k):
        return (yi * xd + k, q)

    def ydev(k):
        return (k * xd + xi, q)

    barrier = pltpu.get_barrier_semaphore()

    def greet_x(i, c):
        pl.semaphore_signal(barrier, 1, device_id=xdev(lax.rem(xi + i, xd)), device_id_type=MESH)
        return c

    def greet_y(i, c):
        pl.semaphore_signal(barrier, 1, device_id=ydev(lax.rem(yi + i, yd)), device_id_type=MESH)
        return c

    lax.fori_loop(1, xd, greet_x, 0)
    lax.fori_loop(1, yd, greet_y, 0)
    pl.semaphore_wait(barrier, xd + yd - 2)

    def exchange(phase, src, dst, me, size, dev):
        def copy(k, s):
            return pltpu.make_async_remote_copy(
                src_ref=src(k, s),
                dst_ref=dst(s),
                send_sem=sends.at[phase, k],
                recv_sem=recvs.at[phase, s],
                device_id=dev(k),
                device_id_type=MESH,
            )

        def start(i, c):
            copy(lax.rem(me + i, size), me).start()
            return c

        lax.fori_loop(1, size, start, 0)

        def wait(i, c):
            s = lax.rem(me + size - i, size)
            copy(s, s).wait_recv()
            copy(lax.rem(me + i, size), me).wait_send()
            return c

        lax.fori_loop(1, size, wait, 0)

    def total(parts, size):
        acc = parts(0).astype(jnp.float32)
        for s in range(1, size):
            acc = acc + parts(s).astype(jnp.float32)
        return acc

    def top_copy(k):
        return pltpu.make_async_remote_copy(
            src_ref=t_ref.at[k, 1],
            dst_ref=b1.at[xt, 1],
            send_sem=tsend.at[k],
            recv_sem=trecv.at[0],
            device_id=xdev(k),
            device_id_type=MESH,
        )

    @pl.when(p == top)
    def _():
        def start(i, c):
            top_copy(lax.rem(xi + i, xd)).start()
            return c

        lax.fori_loop(1, xd, start, 0)

    exchange(0, lambda k, s: t_ref.at[k, 0], lambda s: b1.at[s, 0], xi, xd, xdev)
    b1[xi, 0] = t_ref[xi, 0]
    top_half = (yd // 2, b1.shape[2] * 2 // yd, b1.shape[3])
    a2[: yd // 2] = total(lambda s: b1[s, 0], xd).astype(a2.dtype).reshape(top_half)

    @pl.when(p == top)
    def _():
        def sent(i, c):
            top_copy(lax.rem(xi + i, xd)).wait_send()
            return c

        lax.fori_loop(1, xd, sent, 0)
        a3 = t_ref[xi, 1]
        a2[yd // 2 :] = a3.reshape(top_half)

    @pl.when((yi == yt) & (p != top))
    def _():
        top_copy(xi).wait_recv()
        a2[yd // 2 :] = b1[xt, 1].reshape(top_half)

    @pl.when(yi != yt)
    def _():
        a2[yd // 2 :] = jnp.zeros(top_half, a2.dtype)

    exchange(1, lambda k, s: a2.at[k], lambda s: b2.at[s], yi, yd, ydev)
    b2[yi] = a2[yi]
    b3[yi] = total(lambda s: b2[s], yd).astype(b3.dtype)
    exchange(2, lambda k, s: b3.at[s], lambda s: b3.at[s], yi, yd, ydev)
    b4[xi] = b3[...].reshape(b4.shape[1:])
    exchange(3, lambda k, s: b4.at[s], lambda s: b4.at[s], xi, xd, xdev)
    o_ref[...] = b4[...]


def prow_sum(picked, top_part, xd, top):
    yd = lax.axis_size("prow") // xd
    rows, cols = picked.shape
    chunks = jnp.stack(
        [picked.reshape(xd, rows // xd, cols), top_part.reshape(xd, rows // xd, cols)], axis=1
    )
    part = 2 * rows // xd // yd
    out = pl.pallas_call(
        functools.partial(prow_kernel, xd, yd, top),
        out_shape=jax.ShapeDtypeStruct((xd, yd, part, cols), picked.dtype),
        in_specs=[pl.BlockSpec(memory_space=pltpu.VMEM)],
        out_specs=pl.BlockSpec(memory_space=pltpu.VMEM),
        scratch_shapes=[
            pltpu.VMEM(chunks.shape, picked.dtype),
            pltpu.VMEM((yd, part, cols), picked.dtype),
            pltpu.VMEM((yd, part, cols), picked.dtype),
            pltpu.VMEM((yd, part, cols), picked.dtype),
            pltpu.VMEM((xd, yd, part, cols), picked.dtype),
            pltpu.SemaphoreType.DMA((4, max(xd, yd))),
            pltpu.SemaphoreType.DMA((4, max(xd, yd))),
            pltpu.SemaphoreType.DMA((xd,)),
            pltpu.SemaphoreType.DMA((1,)),
        ],
        compiler_params=pltpu.CompilerParams(collective_id=10 + top, has_side_effects=True),
    )(chunks)
    out = out.reshape(xd, 2, rows // xd, cols)
    return out[:, 0].reshape(rows, cols), out[:, 1].reshape(rows, cols)


def pcol_kernel(nz, source, x_ref, o_ref, g, p1send, p1recv, p2send, p2recv, p3send, p3recv):
    q = lax.axis_index("pcol")
    p = lax.axis_index("prow")
    nc = lax.axis_size("pcol") // nz
    z = q // nc
    c = lax.rem(q, nc)
    zs, cs = source // nc, source % nc

    def dev(zz, cc):
        return (p, zz * nc + cc)

    barrier = pltpu.get_barrier_semaphore()
    n = nz * nc

    def greet(i, carry):
        j = lax.rem(q + i, n)
        pl.semaphore_signal(barrier, 1, device_id=(p, j), device_id_type=MESH)
        return carry

    lax.fori_loop(1, n, greet, 0)
    pl.semaphore_wait(barrier, n - 1)

    def spread(t):
        zz, cc = t // nc, lax.rem(t, nc)
        return pltpu.make_async_remote_copy(
            src_ref=x_ref.at[cc, zz],
            dst_ref=g.at[cc, zz],
            send_sem=p1send.at[t],
            recv_sem=p1recv.at[0],
            device_id=dev(zz, cc),
            device_id_type=MESH,
        )

    def ring(j, s):
        return pltpu.make_async_remote_copy(
            src_ref=g.at[c, s],
            dst_ref=g.at[c, s],
            send_sem=p2send.at[j],
            recv_sem=p2recv.at[s],
            device_id=dev(j, c),
            device_id_type=MESH,
        )

    def partner(cc, other):
        return pltpu.make_async_remote_copy(
            src_ref=g.at[cc],
            dst_ref=g.at[cc],
            send_sem=p3send.at[0],
            recv_sem=p3recv.at[0],
            device_id=dev(z, other),
            device_id_type=MESH,
        )

    @pl.when(q == source)
    def _():
        def start(i, carry):
            spread(lax.rem(q + i, n)).start()
            return carry

        lax.fori_loop(1, n, start, 0)
        g[cs, zs] = x_ref[cs, zs]

        def sent(i, carry):
            spread(lax.rem(q + i, n)).wait_send()
            return carry

        lax.fori_loop(1, n, sent, 0)

    @pl.when(q != source)
    def _():
        spread(q).wait_recv()

    def start(i, carry):
        ring(lax.rem(z + i, nz), z).start()
        return carry

    lax.fori_loop(1, nz, start, 0)

    def wait(i, carry):
        s = lax.rem(z + nz - i, nz)
        ring(s, s).wait_recv()
        ring(lax.rem(z + i, nz), z).wait_send()
        return carry

    lax.fori_loop(1, nz, wait, 0)
    partner(c, 1 - c).start()
    partner(1 - c, 1 - c).wait_recv()
    partner(c, 1 - c).wait_send()
    o_ref[...] = g[...]


def pcol_bcast(x, nz, source, collective_id):
    rows, cols = x.shape
    nc = lax.axis_size("pcol") // nz
    chunks = x.reshape(nc, nz, rows // nz // nc, cols)
    n = nz * nc
    out = pl.pallas_call(
        functools.partial(pcol_kernel, nz, source),
        out_shape=jax.ShapeDtypeStruct(chunks.shape, x.dtype),
        in_specs=[pl.BlockSpec(memory_space=pltpu.VMEM)],
        out_specs=pl.BlockSpec(memory_space=pltpu.VMEM),
        scratch_shapes=[
            pltpu.VMEM(chunks.shape, x.dtype),
            pltpu.SemaphoreType.DMA((n,)),
            pltpu.SemaphoreType.DMA((1,)),
            pltpu.SemaphoreType.DMA((nz,)),
            pltpu.SemaphoreType.DMA((nz,)),
            pltpu.SemaphoreType.DMA((1,)),
            pltpu.SemaphoreType.DMA((1,)),
        ],
        compiler_params=pltpu.CompilerParams(collective_id=collective_id, has_side_effects=True),
    )(chunks)
    return out.reshape(rows, cols)


def local(x_devices, z_chips, matrix, pivots, lower_inverse, upper_inverse):
    row_count = lax.axis_size("prow")
    col_count = lax.axis_size("pcol")
    my_row = lax.axis_index("prow")
    my_col = lax.axis_index("pcol")
    blocks_down, block, blocks_across, _ = matrix.shape
    local_rows = blocks_down * block
    local_cols = blocks_across * block
    current = matrix.reshape(local_rows, local_cols)
    row_place = jnp.arange(local_rows)
    col_place = jnp.arange(local_cols)
    global_rows = (row_place // block * row_count + my_row) * block + row_place % block
    global_cols = (col_place // block * col_count + my_col) * block + col_place % block
    for panel in range(pivots.shape[0]):
        start = panel * block
        chosen = pivots[panel]
        block_row = chosen // block
        is_mine = block_row % row_count == my_row
        local_index = block_row // row_count * block + chosen % block
        safe_index = jnp.where(is_mine, local_index, 0)
        picked = jnp.where(is_mine[:, None], current[safe_index], jnp.zeros((), jnp.bfloat16))
        top_holder = panel % row_count
        top_first = panel // row_count * block
        is_top = my_row == top_holder
        top_local = current[top_first : top_first + block]
        top_part = jnp.where(is_top, top_local, jnp.zeros((), jnp.bfloat16))
        incoming, old_top = prow_sum(picked, top_part, x_devices, top_holder)
        target = jnp.where(is_mine, local_index, local_rows)
        current = current.at[target].set(old_top, mode="drop")
        top_now = current[top_first : top_first + block]
        current = current.at[top_first : top_first + block].set(
            jnp.where(is_top, incoming, top_now)
        )
        panel_holder = panel % col_count
        panel_first = panel // col_count * block
        panel_cols = current[:, panel_first : panel_first + block]
        factor = jnp.dot(
            panel_cols, upper_inverse[panel], preferred_element_type=jnp.float32
        ).astype(jnp.bfloat16)
        is_panel = my_col == panel_holder
        factor = jnp.where(is_panel, factor, jnp.zeros((), jnp.bfloat16))
        lower = pcol_bcast(factor, z_chips, panel_holder, 20 + panel)
        upper = jnp.dot(
            lower_inverse[panel], incoming, preferred_element_type=jnp.float32
        ).astype(jnp.bfloat16)
        row_mask = global_rows >= start + block
        col_mask = global_cols >= start + block
        product = jnp.dot(lower, upper, preferred_element_type=jnp.float32)
        changed = (current.astype(jnp.float32) - product).astype(jnp.bfloat16)
        below = row_mask[:, None]
        right = col_mask[None, :]
        in_panel = is_panel & (col_place // block == panel_first // block)[None, :]
        in_top = is_top & (row_place // block == top_first // block)[:, None]
        lower_wide = jnp.broadcast_to(
            lower[:, None, :], (local_rows, blocks_across, block)
        ).reshape(local_rows, local_cols)
        upper_tall = jnp.broadcast_to(
            upper[None], (blocks_down, block, local_cols)
        ).reshape(local_rows, local_cols)
        current = jnp.where(
            below & right,
            changed,
            jnp.where(
                in_panel & below,
                lower_wide,
                jnp.where(in_top & right, upper_tall, current),
            ),
        )
    return current.reshape(matrix.shape)


def solution(mesh):
    x_devices = len({d.coords[0] for d in mesh.devices[:, 0]})
    z_chips = len({d.coords[2] for d in mesh.devices[0, :]})
    in_specs = (P(None, "prow", None, "pcol"), P(), P(), P())
    out_specs = P(None, "prow", None, "pcol")
    return jax.shard_map(functools.partial(local, x_devices, z_chips), mesh=mesh, in_specs=in_specs, out_specs=out_specs, check_vma=False)
```

```python
import functools

import jax
import jax.numpy as jnp
from jax import lax
from jax.experimental import pallas as pl
from jax.experimental.pallas import tpu as pltpu
from jax.sharding import PartitionSpec as P

MESH = pl.DeviceIdType.MESH


def sum_kernel(axis, other, n, summed, source, x_ref, o_ref, recv, gath, ssend, srecv,
               bsend, brecv, gsend, grecv):
    me = lax.axis_index(axis)
    them = lax.axis_index(other)

    def dev(j):
        return (j, them) if axis == "prow" else (them, j)

    barrier = pltpu.get_barrier_semaphore()

    def greet(i, c):
        j = lax.rem(me + i, n)
        pl.semaphore_signal(barrier, 1, device_id=dev(j), device_id_type=MESH)
        return c

    lax.fori_loop(1, n, greet, 0)
    pl.semaphore_wait(barrier, n - 1)

    def scatter(j, s):
        return pltpu.make_async_remote_copy(
            src_ref=x_ref.at[j],
            dst_ref=recv.at[s],
            send_sem=ssend.at[j],
            recv_sem=srecv.at[s],
            device_id=dev(j),
            device_id_type=MESH,
        )

    def spread(j):
        return pltpu.make_async_remote_copy(
            src_ref=x_ref.at[j],
            dst_ref=gath.at[j],
            send_sem=bsend.at[j],
            recv_sem=brecv.at[0],
            device_id=dev(j),
            device_id_type=MESH,
        )

    if summed > 0:
        def start_scatter(i, c):
            j = lax.rem(me + i, n)

            @pl.when(j < summed)
            def _():
                scatter(j, me).start()

            return c

        lax.fori_loop(1, n, start_scatter, 0)

    if summed < n:
        @pl.when(me == source)
        def _():
            def start_spread(i, c):
                j = lax.rem(me + i, n)

                @pl.when(j >= summed)
                def _():
                    spread(j).start()

                return c

            lax.fori_loop(1, n, start_spread, 0)
            if source >= summed:
                gath[source] = x_ref[source]

    if summed > 0:
        @pl.when(me < summed)
        def _():
            recv[me] = x_ref[me]

            def wait_scatter(i, c):
                s = lax.rem(me + n - i, n)
                scatter(s, s).wait_recv()
                return c

            lax.fori_loop(1, n, wait_scatter, 0)
            total = recv[0].astype(jnp.float32)
            for s in range(1, n):
                total = total + recv[s].astype(jnp.float32)
            gath[me] = total.astype(gath.dtype)

        def wait_scatter_sent(i, c):
            j = lax.rem(me + i, n)

            @pl.when(j < summed)
            def _():
                scatter(j, me).wait_send()

            return c

        lax.fori_loop(1, n, wait_scatter_sent, 0)

    if summed < n:
        @pl.when((me >= summed) & (me != source))
        def _():
            spread(me).wait_recv()

        @pl.when(me == source)
        def _():
            def wait_spread_sent(i, c):
                j = lax.rem(me + i, n)

                @pl.when(j >= summed)
                def _():
                    spread(j).wait_send()

                return c

            lax.fori_loop(1, n, wait_spread_sent, 0)

    def gather(j, s):
        return pltpu.make_async_remote_copy(
            src_ref=gath.at[s],
            dst_ref=gath.at[s],
            send_sem=gsend.at[j],
            recv_sem=grecv.at[s],
            device_id=dev(j),
            device_id_type=MESH,
        )

    def start_gather(i, c):
        gather(lax.rem(me + i, n), me).start()
        return c

    lax.fori_loop(1, n, start_gather, 0)

    def wait_gather(i, c):
        gather(lax.rem(me + n - i, n), lax.rem(me + n - i, n)).wait_recv()
        gather(lax.rem(me + i, n), me).wait_send()
        return c

    lax.fori_loop(1, n, wait_gather, 0)
    o_ref[...] = gath[...]


def axis_sum(x, axis, other, collective_id, summed_rows, source):
    n = lax.axis_size(axis)
    chunks = x.reshape(n, x.shape[0] // n, x.shape[1])
    summed = summed_rows // chunks.shape[1]
    out = pl.pallas_call(
        functools.partial(sum_kernel, axis, other, n, summed, source),
        out_shape=jax.ShapeDtypeStruct(chunks.shape, chunks.dtype),
        in_specs=[pl.BlockSpec(memory_space=pltpu.VMEM)],
        out_specs=pl.BlockSpec(memory_space=pltpu.VMEM),
        scratch_shapes=[
            pltpu.VMEM(chunks.shape, chunks.dtype),
            pltpu.VMEM(chunks.shape, chunks.dtype),
            pltpu.SemaphoreType.DMA((n,)),
            pltpu.SemaphoreType.DMA((n,)),
            pltpu.SemaphoreType.DMA((n,)),
            pltpu.SemaphoreType.DMA((1,)),
            pltpu.SemaphoreType.DMA((n,)),
            pltpu.SemaphoreType.DMA((n,)),
        ],
        compiler_params=pltpu.CompilerParams(
            collective_id=collective_id, has_side_effects=True
        ),
    )(chunks)
    return out.reshape(x.shape)


def group_kernel(stride, size, mode, x_ref, o_ref, buf, send, recv):
    p = lax.axis_index("prow")
    q = lax.axis_index("pcol")
    me = lax.rem(p // stride, size)
    base = p - me * stride

    def dev(k):
        return (base + k * stride, q)

    barrier = pltpu.get_barrier_semaphore()

    def greet(i, c):
        pl.semaphore_signal(barrier, 1, device_id=dev(lax.rem(me + i, size)), device_id_type=MESH)
        return c

    lax.fori_loop(1, size, greet, 0)
    pl.semaphore_wait(barrier, size - 1)

    def copy(k, s):
        src = x_ref.at[k] if mode == "rs" else buf.at[s]
        return pltpu.make_async_remote_copy(
            src_ref=src,
            dst_ref=buf.at[s],
            send_sem=send.at[k],
            recv_sem=recv.at[s],
            device_id=dev(k),
            device_id_type=MESH,
        )

    if mode == "ag":
        buf[me] = x_ref[...]

    def start(i, c):
        copy(lax.rem(me + i, size), me).start()
        return c

    lax.fori_loop(1, size, start, 0)
    if mode == "rs":
        buf[me] = x_ref[me]

    def wait(i, c):
        s = lax.rem(me + size - i, size)
        copy(s, s).wait_recv()
        copy(lax.rem(me + i, size), me).wait_send()
        return c

    lax.fori_loop(1, size, wait, 0)
    if mode == "rs":
        total = buf[0].astype(jnp.float32)
        for s in range(1, size):
            total = total + buf[s].astype(jnp.float32)
        o_ref[...] = total.astype(o_ref.dtype)
    else:
        o_ref[...] = buf[...]


def group_step(x, stride, size, mode, collective_id):
    if mode == "rs":
        chunks = x.reshape(size, x.shape[0] // size, x.shape[1])
        out_shape = chunks.shape[1:]
        buf_shape = chunks.shape
    else:
        chunks = x
        out_shape = (size,) + x.shape
        buf_shape = out_shape
    out = pl.pallas_call(
        functools.partial(group_kernel, stride, size, mode),
        out_shape=jax.ShapeDtypeStruct(out_shape, x.dtype),
        in_specs=[pl.BlockSpec(memory_space=pltpu.VMEM)],
        out_specs=pl.BlockSpec(memory_space=pltpu.VMEM),
        scratch_shapes=[
            pltpu.VMEM(buf_shape, x.dtype),
            pltpu.SemaphoreType.DMA((size,)),
            pltpu.SemaphoreType.DMA((size,)),
        ],
        compiler_params=pltpu.CompilerParams(
            collective_id=collective_id, has_side_effects=True
        ),
    )(chunks)
    if mode == "ag":
        out = out.reshape(size * x.shape[0], x.shape[1])
    return out


def prow_kernel(xd, yd, top, t_ref, o_ref, b1, a2, b2, b3, b4, sends, recvs, tsend, trecv):
    p = lax.axis_index("prow")
    q = lax.axis_index("pcol")
    xi = lax.rem(p, xd)
    yi = p // xd
    xt, yt = top % xd, top // xd

    def xdev(k):
        return (yi * xd + k, q)

    def ydev(k):
        return (k * xd + xi, q)

    barrier = pltpu.get_barrier_semaphore()

    def greet_x(i, c):
        pl.semaphore_signal(barrier, 1, device_id=xdev(lax.rem(xi + i, xd)), device_id_type=MESH)
        return c

    def greet_y(i, c):
        pl.semaphore_signal(barrier, 1, device_id=ydev(lax.rem(yi + i, yd)), device_id_type=MESH)
        return c

    lax.fori_loop(1, xd, greet_x, 0)
    lax.fori_loop(1, yd, greet_y, 0)
    pl.semaphore_wait(barrier, xd + yd - 2)

    def exchange(phase, src, dst, me, size, dev):
        def copy(k, s):
            return pltpu.make_async_remote_copy(
                src_ref=src(k, s),
                dst_ref=dst(s),
                send_sem=sends.at[phase, k],
                recv_sem=recvs.at[phase, s],
                device_id=dev(k),
                device_id_type=MESH,
            )

        def start(i, c):
            copy(lax.rem(me + i, size), me).start()
            return c

        lax.fori_loop(1, size, start, 0)

        def wait(i, c):
            s = lax.rem(me + size - i, size)
            copy(s, s).wait_recv()
            copy(lax.rem(me + i, size), me).wait_send()
            return c

        lax.fori_loop(1, size, wait, 0)

    def total(parts, size):
        acc = parts(0).astype(jnp.float32)
        for s in range(1, size):
            acc = acc + parts(s).astype(jnp.float32)
        return acc

    def top_copy(k):
        return pltpu.make_async_remote_copy(
            src_ref=t_ref.at[k, 1],
            dst_ref=b1.at[xt, 1],
            send_sem=tsend.at[k],
            recv_sem=trecv.at[0],
            device_id=xdev(k),
            device_id_type=MESH,
        )

    @pl.when(p == top)
    def _():
        def start(i, c):
            top_copy(lax.rem(xi + i, xd)).start()
            return c

        lax.fori_loop(1, xd, start, 0)

    exchange(0, lambda k, s: t_ref.at[k, 0], lambda s: b1.at[s, 0], xi, xd, xdev)
    b1[xi, 0] = t_ref[xi, 0]
    top_half = (yd // 2, b1.shape[2] * 2 // yd, b1.shape[3])
    a2[: yd // 2] = total(lambda s: b1[s, 0], xd).astype(a2.dtype).reshape(top_half)

    @pl.when(p == top)
    def _():
        def sent(i, c):
            top_copy(lax.rem(xi + i, xd)).wait_send()
            return c

        lax.fori_loop(1, xd, sent, 0)
        a3 = t_ref[xi, 1]
        a2[yd // 2 :] = a3.reshape(top_half)

    @pl.when((yi == yt) & (p != top))
    def _():
        top_copy(xi).wait_recv()
        a2[yd // 2 :] = b1[xt, 1].reshape(top_half)

    @pl.when(yi != yt)
    def _():
        a2[yd // 2 :] = jnp.zeros(top_half, a2.dtype)

    exchange(1, lambda k, s: a2.at[k], lambda s: b2.at[s], yi, yd, ydev)
    b2[yi] = a2[yi]
    b3[yi] = total(lambda s: b2[s], yd).astype(b3.dtype)
    exchange(2, lambda k, s: b3.at[s], lambda s: b3.at[s], yi, yd, ydev)
    b4[xi] = b3[...].reshape(b4.shape[1:])
    exchange(3, lambda k, s: b4.at[s], lambda s: b4.at[s], xi, xd, xdev)
    o_ref[...] = b4[...]


def prow_sum(picked, top_part, xd, top):
    yd = lax.axis_size("prow") // xd
    rows, cols = picked.shape
    chunks = jnp.stack(
        [picked.reshape(xd, rows // xd, cols), top_part.reshape(xd, rows // xd, cols)], axis=1
    )
    part = 2 * rows // xd // yd
    out = pl.pallas_call(
        functools.partial(prow_kernel, xd, yd, top),
        out_shape=jax.ShapeDtypeStruct((xd, yd, part, cols), picked.dtype),
        in_specs=[pl.BlockSpec(memory_space=pltpu.VMEM)],
        out_specs=pl.BlockSpec(memory_space=pltpu.VMEM),
        scratch_shapes=[
            pltpu.VMEM(chunks.shape, picked.dtype),
            pltpu.VMEM((yd, part, cols), picked.dtype),
            pltpu.VMEM((yd, part, cols), picked.dtype),
            pltpu.VMEM((yd, part, cols), picked.dtype),
            pltpu.VMEM((xd, yd, part, cols), picked.dtype),
            pltpu.SemaphoreType.DMA((4, max(xd, yd))),
            pltpu.SemaphoreType.DMA((4, max(xd, yd))),
            pltpu.SemaphoreType.DMA((xd,)),
            pltpu.SemaphoreType.DMA((1,)),
        ],
        compiler_params=pltpu.CompilerParams(collective_id=10 + top, has_side_effects=True),
    )(chunks)
    out = out.reshape(xd, 2, rows // xd, cols)
    return out[:, 0].reshape(rows, cols), out[:, 1].reshape(rows, cols)


def pcol_kernel(nz, source, x_ref, o_ref, g, p1send, p1recv, p2send, p2recv, p3send, p3recv):
    q = lax.axis_index("pcol")
    p = lax.axis_index("prow")
    nc = lax.axis_size("pcol") // nz
    z = q // nc
    c = lax.rem(q, nc)
    zs, cs = source // nc, source % nc

    def dev(zz, cc):
        return (p, zz * nc + cc)

    barrier = pltpu.get_barrier_semaphore()
    pl.semaphore_signal(barrier, 1, device_id=dev(z, 1 - c), device_id_type=MESH)

    @pl.when(c == cs)
    def _():
        def greet(i, carry):
            pl.semaphore_signal(
                barrier, 1, device_id=dev(lax.rem(z + i, nz), cs), device_id_type=MESH
            )
            return carry

        lax.fori_loop(1, nz, greet, 0)
        pl.semaphore_wait(barrier, nz)

    @pl.when(c != cs)
    def _():
        pl.semaphore_wait(barrier, 1)

    def spread(j):
        return pltpu.make_async_remote_copy(
            src_ref=x_ref.at[j],
            dst_ref=g.at[j],
            send_sem=p1send.at[j],
            recv_sem=p1recv.at[0],
            device_id=dev(j, cs),
            device_id_type=MESH,
        )

    def ring(j, s):
        return pltpu.make_async_remote_copy(
            src_ref=g.at[s],
            dst_ref=g.at[s],
            send_sem=p2send.at[j],
            recv_sem=p2recv.at[s],
            device_id=dev(j, cs),
            device_id_type=MESH,
        )

    def partner(zz):
        return pltpu.make_async_remote_copy(
            src_ref=g,
            dst_ref=g,
            send_sem=p3send.at[0],
            recv_sem=p3recv.at[0],
            device_id=dev(zz, 1 - cs),
            device_id_type=MESH,
        )

    @pl.when(q == source)
    def _():
        def start(i, carry):
            spread(lax.rem(zs + i, nz)).start()
            return carry

        lax.fori_loop(1, nz, start, 0)
        g[zs] = x_ref[zs]

        def sent(i, carry):
            spread(lax.rem(zs + i, nz)).wait_send()
            return carry

        lax.fori_loop(1, nz, sent, 0)

    @pl.when((c == cs) & (z != zs))
    def _():
        spread(z).wait_recv()

    @pl.when(c == cs)
    def _():
        def start(i, carry):
            ring(lax.rem(z + i, nz), z).start()
            return carry

        lax.fori_loop(1, nz, start, 0)

        def wait(i, carry):
            s = lax.rem(z + nz - i, nz)
            ring(s, s).wait_recv()
            ring(lax.rem(z + i, nz), z).wait_send()
            return carry

        lax.fori_loop(1, nz, wait, 0)
        partner(z).start()
        partner(z).wait_send()

    @pl.when(c != cs)
    def _():
        partner(z).wait_recv()

    o_ref[...] = g[...]


def pcol_bcast(x, nz, source, collective_id):
    rows, cols = x.shape
    chunks = x.reshape(nz, rows // nz, cols)
    out = pl.pallas_call(
        functools.partial(pcol_kernel, nz, source),
        out_shape=jax.ShapeDtypeStruct(chunks.shape, x.dtype),
        in_specs=[pl.BlockSpec(memory_space=pltpu.VMEM)],
        out_specs=pl.BlockSpec(memory_space=pltpu.VMEM),
        scratch_shapes=[
            pltpu.VMEM(chunks.shape, x.dtype),
            pltpu.SemaphoreType.DMA((nz,)),
            pltpu.SemaphoreType.DMA((1,)),
            pltpu.SemaphoreType.DMA((nz,)),
            pltpu.SemaphoreType.DMA((nz,)),
            pltpu.SemaphoreType.DMA((1,)),
            pltpu.SemaphoreType.DMA((1,)),
        ],
        compiler_params=pltpu.CompilerParams(collective_id=collective_id, has_side_effects=True),
    )(chunks)
    return out.reshape(rows, cols)


def local(x_devices, z_chips, matrix, pivots, lower_inverse, upper_inverse):
    row_count = lax.axis_size("prow")
    col_count = lax.axis_size("pcol")
    my_row = lax.axis_index("prow")
    my_col = lax.axis_index("pcol")
    blocks_down, block, blocks_across, _ = matrix.shape
    local_rows = blocks_down * block
    local_cols = blocks_across * block
    current = matrix.reshape(local_rows, local_cols)
    row_place = jnp.arange(local_rows)
    col_place = jnp.arange(local_cols)
    global_rows = (row_place // block * row_count + my_row) * block + row_place % block
    global_cols = (col_place // block * col_count + my_col) * block + col_place % block
    for panel in range(pivots.shape[0]):
        start = panel * block
        chosen = pivots[panel]
        block_row = chosen // block
        is_mine = block_row % row_count == my_row
        local_index = block_row // row_count * block + chosen % block
        safe_index = jnp.where(is_mine, local_index, 0)
        picked = jnp.where(is_mine[:, None], current[safe_index], jnp.zeros((), jnp.bfloat16))
        top_holder = panel % row_count
        top_first = panel // row_count * block
        is_top = my_row == top_holder
        top_local = current[top_first : top_first + block]
        top_part = jnp.where(is_top, top_local, jnp.zeros((), jnp.bfloat16))
        incoming, old_top = prow_sum(picked, top_part, x_devices, top_holder)
        target = jnp.where(is_mine, local_index, local_rows)
        current = current.at[target].set(old_top, mode="drop")
        top_now = current[top_first : top_first + block]
        current = current.at[top_first : top_first + block].set(
            jnp.where(is_top, incoming, top_now)
        )
        panel_holder = panel % col_count
        panel_first = panel // col_count * block
        panel_cols = current[:, panel_first : panel_first + block]
        factor = jnp.dot(
            panel_cols, upper_inverse[panel], preferred_element_type=jnp.float32
        ).astype(jnp.bfloat16)
        is_panel = my_col == panel_holder
        factor = jnp.where(is_panel, factor, jnp.zeros((), jnp.bfloat16))
        lower = pcol_bcast(factor, z_chips, panel_holder, 20 + panel)
        upper = jnp.dot(
            lower_inverse[panel], incoming, preferred_element_type=jnp.float32
        ).astype(jnp.bfloat16)
        row_mask = global_rows >= start + block
        col_mask = global_cols >= start + block
        product = jnp.dot(lower, upper, preferred_element_type=jnp.float32)
        changed = (current.astype(jnp.float32) - product).astype(jnp.bfloat16)
        below = row_mask[:, None]
        right = col_mask[None, :]
        in_panel = is_panel & (col_place // block == panel_first // block)[None, :]
        in_top = is_top & (row_place // block == top_first // block)[:, None]
        lower_wide = jnp.broadcast_to(
            lower[:, None, :], (local_rows, blocks_across, block)
        ).reshape(local_rows, local_cols)
        upper_tall = jnp.broadcast_to(
            upper[None], (blocks_down, block, local_cols)
        ).reshape(local_rows, local_cols)
        current = jnp.where(
            below & right,
            changed,
            jnp.where(
                in_panel & below,
                lower_wide,
                jnp.where(in_top & right, upper_tall, current),
            ),
        )
    return current.reshape(matrix.shape)


def solution(mesh):
    x_devices = len({d.coords[0] for d in mesh.devices[:, 0]})
    z_chips = len({d.coords[2] for d in mesh.devices[0, :]})
    in_specs = (P(None, "prow", None, "pcol"), P(), P(), P())
    out_specs = P(None, "prow", None, "pcol")
    return jax.shard_map(functools.partial(local, x_devices, z_chips), mesh=mesh, in_specs=in_specs, out_specs=out_specs, check_vma=False)
```

```python
import functools

import jax
import jax.numpy as jnp
from jax import lax
from jax.experimental import pallas as pl
from jax.experimental.pallas import tpu as pltpu
from jax.sharding import PartitionSpec as P

MESH = pl.DeviceIdType.MESH


def sum_kernel(axis, other, n, summed, source, x_ref, o_ref, recv, gath, ssend, srecv,
               bsend, brecv, gsend, grecv):
    me = lax.axis_index(axis)
    them = lax.axis_index(other)

    def dev(j):
        return (j, them) if axis == "prow" else (them, j)

    barrier = pltpu.get_barrier_semaphore()

    def greet(i, c):
        j = lax.rem(me + i, n)
        pl.semaphore_signal(barrier, 1, device_id=dev(j), device_id_type=MESH)
        return c

    lax.fori_loop(1, n, greet, 0)
    pl.semaphore_wait(barrier, n - 1)

    def scatter(j, s):
        return pltpu.make_async_remote_copy(
            src_ref=x_ref.at[j],
            dst_ref=recv.at[s],
            send_sem=ssend.at[j],
            recv_sem=srecv.at[s],
            device_id=dev(j),
            device_id_type=MESH,
        )

    def spread(j):
        return pltpu.make_async_remote_copy(
            src_ref=x_ref.at[j],
            dst_ref=gath.at[j],
            send_sem=bsend.at[j],
            recv_sem=brecv.at[0],
            device_id=dev(j),
            device_id_type=MESH,
        )

    if summed > 0:
        def start_scatter(i, c):
            j = lax.rem(me + i, n)

            @pl.when(j < summed)
            def _():
                scatter(j, me).start()

            return c

        lax.fori_loop(1, n, start_scatter, 0)

    if summed < n:
        @pl.when(me == source)
        def _():
            def start_spread(i, c):
                j = lax.rem(me + i, n)

                @pl.when(j >= summed)
                def _():
                    spread(j).start()

                return c

            lax.fori_loop(1, n, start_spread, 0)
            if source >= summed:
                gath[source] = x_ref[source]

    if summed > 0:
        @pl.when(me < summed)
        def _():
            recv[me] = x_ref[me]

            def wait_scatter(i, c):
                s = lax.rem(me + n - i, n)
                scatter(s, s).wait_recv()
                return c

            lax.fori_loop(1, n, wait_scatter, 0)
            total = recv[0].astype(jnp.float32)
            for s in range(1, n):
                total = total + recv[s].astype(jnp.float32)
            gath[me] = total.astype(gath.dtype)

        def wait_scatter_sent(i, c):
            j = lax.rem(me + i, n)

            @pl.when(j < summed)
            def _():
                scatter(j, me).wait_send()

            return c

        lax.fori_loop(1, n, wait_scatter_sent, 0)

    if summed < n:
        @pl.when((me >= summed) & (me != source))
        def _():
            spread(me).wait_recv()

        @pl.when(me == source)
        def _():
            def wait_spread_sent(i, c):
                j = lax.rem(me + i, n)

                @pl.when(j >= summed)
                def _():
                    spread(j).wait_send()

                return c

            lax.fori_loop(1, n, wait_spread_sent, 0)

    def gather(j, s):
        return pltpu.make_async_remote_copy(
            src_ref=gath.at[s],
            dst_ref=gath.at[s],
            send_sem=gsend.at[j],
            recv_sem=grecv.at[s],
            device_id=dev(j),
            device_id_type=MESH,
        )

    def start_gather(i, c):
        gather(lax.rem(me + i, n), me).start()
        return c

    lax.fori_loop(1, n, start_gather, 0)

    def wait_gather(i, c):
        gather(lax.rem(me + n - i, n), lax.rem(me + n - i, n)).wait_recv()
        gather(lax.rem(me + i, n), me).wait_send()
        return c

    lax.fori_loop(1, n, wait_gather, 0)
    o_ref[...] = gath[...]


def axis_sum(x, axis, other, collective_id, summed_rows, source):
    n = lax.axis_size(axis)
    chunks = x.reshape(n, x.shape[0] // n, x.shape[1])
    summed = summed_rows // chunks.shape[1]
    out = pl.pallas_call(
        functools.partial(sum_kernel, axis, other, n, summed, source),
        out_shape=jax.ShapeDtypeStruct(chunks.shape, chunks.dtype),
        in_specs=[pl.BlockSpec(memory_space=pltpu.VMEM)],
        out_specs=pl.BlockSpec(memory_space=pltpu.VMEM),
        scratch_shapes=[
            pltpu.VMEM(chunks.shape, chunks.dtype),
            pltpu.VMEM(chunks.shape, chunks.dtype),
            pltpu.SemaphoreType.DMA((n,)),
            pltpu.SemaphoreType.DMA((n,)),
            pltpu.SemaphoreType.DMA((n,)),
            pltpu.SemaphoreType.DMA((1,)),
            pltpu.SemaphoreType.DMA((n,)),
            pltpu.SemaphoreType.DMA((n,)),
        ],
        compiler_params=pltpu.CompilerParams(
            collective_id=collective_id, has_side_effects=True
        ),
    )(chunks)
    return out.reshape(x.shape)


def group_kernel(stride, size, mode, x_ref, o_ref, buf, send, recv):
    p = lax.axis_index("prow")
    q = lax.axis_index("pcol")
    me = lax.rem(p // stride, size)
    base = p - me * stride

    def dev(k):
        return (base + k * stride, q)

    barrier = pltpu.get_barrier_semaphore()

    def greet(i, c):
        pl.semaphore_signal(barrier, 1, device_id=dev(lax.rem(me + i, size)), device_id_type=MESH)
        return c

    lax.fori_loop(1, size, greet, 0)
    pl.semaphore_wait(barrier, size - 1)

    def copy(k, s):
        src = x_ref.at[k] if mode == "rs" else buf.at[s]
        return pltpu.make_async_remote_copy(
            src_ref=src,
            dst_ref=buf.at[s],
            send_sem=send.at[k],
            recv_sem=recv.at[s],
            device_id=dev(k),
            device_id_type=MESH,
        )

    if mode == "ag":
        buf[me] = x_ref[...]

    def start(i, c):
        copy(lax.rem(me + i, size), me).start()
        return c

    lax.fori_loop(1, size, start, 0)
    if mode == "rs":
        buf[me] = x_ref[me]

    def wait(i, c):
        s = lax.rem(me + size - i, size)
        copy(s, s).wait_recv()
        copy(lax.rem(me + i, size), me).wait_send()
        return c

    lax.fori_loop(1, size, wait, 0)
    if mode == "rs":
        total = buf[0].astype(jnp.float32)
        for s in range(1, size):
            total = total + buf[s].astype(jnp.float32)
        o_ref[...] = total.astype(o_ref.dtype)
    else:
        o_ref[...] = buf[...]


def group_step(x, stride, size, mode, collective_id):
    if mode == "rs":
        chunks = x.reshape(size, x.shape[0] // size, x.shape[1])
        out_shape = chunks.shape[1:]
        buf_shape = chunks.shape
    else:
        chunks = x
        out_shape = (size,) + x.shape
        buf_shape = out_shape
    out = pl.pallas_call(
        functools.partial(group_kernel, stride, size, mode),
        out_shape=jax.ShapeDtypeStruct(out_shape, x.dtype),
        in_specs=[pl.BlockSpec(memory_space=pltpu.VMEM)],
        out_specs=pl.BlockSpec(memory_space=pltpu.VMEM),
        scratch_shapes=[
            pltpu.VMEM(buf_shape, x.dtype),
            pltpu.SemaphoreType.DMA((size,)),
            pltpu.SemaphoreType.DMA((size,)),
        ],
        compiler_params=pltpu.CompilerParams(
            collective_id=collective_id, has_side_effects=True
        ),
    )(chunks)
    if mode == "ag":
        out = out.reshape(size * x.shape[0], x.shape[1])
    return out


def prow_kernel(xd, yd, top, t_ref, o_ref, b1, a2, b2, b3, b4, sends, recvs, tsend, trecv):
    p = lax.axis_index("prow")
    q = lax.axis_index("pcol")
    xi = lax.rem(p, xd)
    yi = p // xd
    xt, yt = top % xd, top // xd

    def xdev(k):
        return (yi * xd + k, q)

    def ydev(k):
        return (k * xd + xi, q)

    barrier = pltpu.get_barrier_semaphore()

    def greet_x(i, c):
        pl.semaphore_signal(barrier, 1, device_id=xdev(lax.rem(xi + i, xd)), device_id_type=MESH)
        return c

    def greet_y(i, c):
        pl.semaphore_signal(barrier, 1, device_id=ydev(lax.rem(yi + i, yd)), device_id_type=MESH)
        return c

    lax.fori_loop(1, xd, greet_x, 0)
    lax.fori_loop(1, yd, greet_y, 0)
    pl.semaphore_wait(barrier, xd + yd - 2)

    def exchange(phase, src, dst, me, size, dev):
        def copy(k, s):
            return pltpu.make_async_remote_copy(
                src_ref=src(k, s),
                dst_ref=dst(s),
                send_sem=sends.at[phase, k],
                recv_sem=recvs.at[phase, s],
                device_id=dev(k),
                device_id_type=MESH,
            )

        def start(i, c):
            copy(lax.rem(me + i, size), me).start()
            return c

        lax.fori_loop(1, size, start, 0)

        def wait(i, c):
            s = lax.rem(me + size - i, size)
            copy(s, s).wait_recv()
            copy(lax.rem(me + i, size), me).wait_send()
            return c

        lax.fori_loop(1, size, wait, 0)

    def total(parts, size):
        acc = parts(0).astype(jnp.float32)
        for s in range(1, size):
            acc = acc + parts(s).astype(jnp.float32)
        return acc

    def top_copy(k):
        return pltpu.make_async_remote_copy(
            src_ref=t_ref.at[k, 1],
            dst_ref=b1.at[xt, 1],
            send_sem=tsend.at[k],
            recv_sem=trecv.at[0],
            device_id=xdev(k),
            device_id_type=MESH,
        )

    @pl.when(p == top)
    def _():
        def start(i, c):
            top_copy(lax.rem(xi + i, xd)).start()
            return c

        lax.fori_loop(1, xd, start, 0)

    exchange(0, lambda k, s: t_ref.at[k, 0], lambda s: b1.at[s, 0], xi, xd, xdev)
    b1[xi, 0] = t_ref[xi, 0]
    top_half = (yd // 2, b1.shape[2] * 2 // yd, b1.shape[3])
    a2[: yd // 2] = total(lambda s: b1[s, 0], xd).astype(a2.dtype).reshape(top_half)

    @pl.when(p == top)
    def _():
        def sent(i, c):
            top_copy(lax.rem(xi + i, xd)).wait_send()
            return c

        lax.fori_loop(1, xd, sent, 0)
        a3 = t_ref[xi, 1]
        a2[yd // 2 :] = a3.reshape(top_half)

    @pl.when((yi == yt) & (p != top))
    def _():
        top_copy(xi).wait_recv()
        a2[yd // 2 :] = b1[xt, 1].reshape(top_half)

    @pl.when(yi != yt)
    def _():
        a2[yd // 2 :] = jnp.zeros(top_half, a2.dtype)

    exchange(1, lambda k, s: a2.at[k], lambda s: b2.at[s], yi, yd, ydev)
    b2[yi] = a2[yi]
    b3[yi] = total(lambda s: b2[s], yd).astype(b3.dtype)
    exchange(2, lambda k, s: b3.at[s], lambda s: b3.at[s], yi, yd, ydev)
    b4[xi] = b3[...].reshape(b4.shape[1:])
    exchange(3, lambda k, s: b4.at[s], lambda s: b4.at[s], xi, xd, xdev)
    o_ref[...] = b4[...]


def prow_sum(picked, top_part, xd, top):
    yd = lax.axis_size("prow") // xd
    rows, cols = picked.shape
    chunks = jnp.stack(
        [picked.reshape(xd, rows // xd, cols), top_part.reshape(xd, rows // xd, cols)], axis=1
    )
    part = 2 * rows // xd // yd
    out = pl.pallas_call(
        functools.partial(prow_kernel, xd, yd, top),
        out_shape=jax.ShapeDtypeStruct((xd, yd, part, cols), picked.dtype),
        in_specs=[pl.BlockSpec(memory_space=pltpu.VMEM)],
        out_specs=pl.BlockSpec(memory_space=pltpu.VMEM),
        scratch_shapes=[
            pltpu.VMEM(chunks.shape, picked.dtype),
            pltpu.VMEM((yd, part, cols), picked.dtype),
            pltpu.VMEM((yd, part, cols), picked.dtype),
            pltpu.VMEM((yd, part, cols), picked.dtype),
            pltpu.VMEM((xd, yd, part, cols), picked.dtype),
            pltpu.SemaphoreType.DMA((4, max(xd, yd))),
            pltpu.SemaphoreType.DMA((4, max(xd, yd))),
            pltpu.SemaphoreType.DMA((xd,)),
            pltpu.SemaphoreType.DMA((1,)),
        ],
        compiler_params=pltpu.CompilerParams(collective_id=10 + top, has_side_effects=True),
    )(chunks)
    out = out.reshape(xd, 2, rows // xd, cols)
    return out[:, 0].reshape(rows, cols), out[:, 1].reshape(rows, cols)


def pcol_kernel(nz, source, x_ref, o_ref, g, p1send, p1recv, p2send, p2recv, p3send, p3recv):
    q = lax.axis_index("pcol")
    p = lax.axis_index("prow")
    nc = lax.axis_size("pcol") // nz
    z = q // nc
    c = lax.rem(q, nc)
    zs, cs = source // nc, source % nc

    def dev(zz, cc):
        return (p, zz * nc + cc)

    barrier = pltpu.get_barrier_semaphore()
    pl.semaphore_signal(barrier, 1, device_id=dev(z, 1 - c), device_id_type=MESH)

    @pl.when(c == cs)
    def _():
        def greet(i, carry):
            pl.semaphore_signal(
                barrier, 1, device_id=dev(lax.rem(z + i, nz), cs), device_id_type=MESH
            )
            return carry

        lax.fori_loop(1, nz, greet, 0)
        pl.semaphore_wait(barrier, nz)

    @pl.when(c != cs)
    def _():
        pl.semaphore_wait(barrier, 1)

    def spread(j):
        return pltpu.make_async_remote_copy(
            src_ref=x_ref.at[j],
            dst_ref=g.at[j],
            send_sem=p1send.at[j],
            recv_sem=p1recv.at[0],
            device_id=dev(j, cs),
            device_id_type=MESH,
        )

    def ring(j, s):
        return pltpu.make_async_remote_copy(
            src_ref=g.at[s],
            dst_ref=g.at[s],
            send_sem=p2send.at[j],
            recv_sem=p2recv.at[s],
            device_id=dev(j, cs),
            device_id_type=MESH,
        )

    def partner(zz):
        return pltpu.make_async_remote_copy(
            src_ref=g,
            dst_ref=g,
            send_sem=p3send.at[0],
            recv_sem=p3recv.at[0],
            device_id=dev(zz, 1 - cs),
            device_id_type=MESH,
        )

    @pl.when(q == source)
    def _():
        def start(i, carry):
            spread(lax.rem(zs + i, nz)).start()
            return carry

        lax.fori_loop(1, nz, start, 0)
        g[zs] = x_ref[zs]

    @pl.when((c == cs) & (z != zs))
    def _():
        spread(z).wait_recv()

    @pl.when(c == cs)
    def _():
        def start(i, carry):
            ring(lax.rem(z + i, nz), z).start()
            return carry

        lax.fori_loop(1, nz, start, 0)

        def wait(i, carry):
            s = lax.rem(z + nz - i, nz)
            ring(s, s).wait_recv()
            ring(lax.rem(z + i, nz), z).wait_send()
            return carry

        lax.fori_loop(1, nz, wait, 0)
        partner(z).start()
        partner(z).wait_send()

    @pl.when(c != cs)
    def _():
        partner(z).wait_recv()

    @pl.when(q == source)
    def _():
        def sent(i, carry):
            spread(lax.rem(zs + i, nz)).wait_send()
            return carry

        lax.fori_loop(1, nz, sent, 0)

    o_ref[...] = g[...]


def pcol_bcast(x, nz, source, collective_id):
    rows, cols = x.shape
    chunks = x.reshape(nz, rows // nz, cols)
    out = pl.pallas_call(
        functools.partial(pcol_kernel, nz, source),
        out_shape=jax.ShapeDtypeStruct(chunks.shape, x.dtype),
        in_specs=[pl.BlockSpec(memory_space=pltpu.VMEM)],
        out_specs=pl.BlockSpec(memory_space=pltpu.VMEM),
        scratch_shapes=[
            pltpu.VMEM(chunks.shape, x.dtype),
            pltpu.SemaphoreType.DMA((nz,)),
            pltpu.SemaphoreType.DMA((1,)),
            pltpu.SemaphoreType.DMA((nz,)),
            pltpu.SemaphoreType.DMA((nz,)),
            pltpu.SemaphoreType.DMA((1,)),
            pltpu.SemaphoreType.DMA((1,)),
        ],
        compiler_params=pltpu.CompilerParams(collective_id=collective_id, has_side_effects=True),
    )(chunks)
    return out.reshape(rows, cols)


def local(x_devices, z_chips, matrix, pivots, lower_inverse, upper_inverse):
    row_count = lax.axis_size("prow")
    col_count = lax.axis_size("pcol")
    my_row = lax.axis_index("prow")
    my_col = lax.axis_index("pcol")
    blocks_down, block, blocks_across, _ = matrix.shape
    local_rows = blocks_down * block
    local_cols = blocks_across * block
    current = matrix.reshape(local_rows, local_cols)
    row_place = jnp.arange(local_rows)
    col_place = jnp.arange(local_cols)
    global_rows = (row_place // block * row_count + my_row) * block + row_place % block
    global_cols = (col_place // block * col_count + my_col) * block + col_place % block
    for panel in range(pivots.shape[0]):
        start = panel * block
        chosen = pivots[panel]
        block_row = chosen // block
        is_mine = block_row % row_count == my_row
        local_index = block_row // row_count * block + chosen % block
        safe_index = jnp.where(is_mine, local_index, 0)
        picked = jnp.where(is_mine[:, None], current[safe_index], jnp.zeros((), jnp.bfloat16))
        top_holder = panel % row_count
        top_first = panel // row_count * block
        is_top = my_row == top_holder
        top_local = current[top_first : top_first + block]
        top_part = jnp.where(is_top, top_local, jnp.zeros((), jnp.bfloat16))
        incoming, old_top = prow_sum(picked, top_part, x_devices, top_holder)
        target = jnp.where(is_mine, local_index, local_rows)
        current = current.at[target].set(old_top, mode="drop")
        top_now = current[top_first : top_first + block]
        current = current.at[top_first : top_first + block].set(
            jnp.where(is_top, incoming, top_now)
        )
        panel_holder = panel % col_count
        panel_first = panel // col_count * block
        panel_cols = current[:, panel_first : panel_first + block]
        factor = jnp.dot(
            panel_cols, upper_inverse[panel], preferred_element_type=jnp.float32
        ).astype(jnp.bfloat16)
        is_panel = my_col == panel_holder
        factor = jnp.where(is_panel, factor, jnp.zeros((), jnp.bfloat16))
        lower = pcol_bcast(factor, z_chips, panel_holder, 20 + panel)
        upper = jnp.dot(
            lower_inverse[panel], incoming, preferred_element_type=jnp.float32
        ).astype(jnp.bfloat16)
        row_mask = global_rows >= start + block
        col_mask = global_cols >= start + block
        product = jnp.dot(lower, upper, preferred_element_type=jnp.float32)
        changed = (current.astype(jnp.float32) - product).astype(jnp.bfloat16)
        below = row_mask[:, None]
        right = col_mask[None, :]
        in_panel = is_panel & (col_place // block == panel_first // block)[None, :]
        in_top = is_top & (row_place // block == top_first // block)[:, None]
        lower_wide = jnp.broadcast_to(
            lower[:, None, :], (local_rows, blocks_across, block)
        ).reshape(local_rows, local_cols)
        upper_tall = jnp.broadcast_to(
            upper[None], (blocks_down, block, local_cols)
        ).reshape(local_rows, local_cols)
        current = jnp.where(
            below & right,
            changed,
            jnp.where(
                in_panel & below,
                lower_wide,
                jnp.where(in_top & right, upper_tall, current),
            ),
        )
    return current.reshape(matrix.shape)


def solution(mesh):
    x_devices = len({d.coords[0] for d in mesh.devices[:, 0]})
    z_chips = len({d.coords[2] for d in mesh.devices[0, :]})
    in_specs = (P(None, "prow", None, "pcol"), P(), P(), P())
    out_specs = P(None, "prow", None, "pcol")
    return jax.shard_map(functools.partial(local, x_devices, z_chips), mesh=mesh, in_specs=in_specs, out_specs=out_specs, check_vma=False)
```

```python
import functools

import jax
import jax.numpy as jnp
from jax import lax
from jax.experimental import pallas as pl
from jax.experimental.pallas import tpu as pltpu
from jax.sharding import PartitionSpec as P

MESH = pl.DeviceIdType.MESH


def sum_kernel(axis, other, n, summed, source, x_ref, o_ref, recv, gath, ssend, srecv,
               bsend, brecv, gsend, grecv):
    me = lax.axis_index(axis)
    them = lax.axis_index(other)

    def dev(j):
        return (j, them) if axis == "prow" else (them, j)

    barrier = pltpu.get_barrier_semaphore()

    def greet(i, c):
        j = lax.rem(me + i, n)
        pl.semaphore_signal(barrier, 1, device_id=dev(j), device_id_type=MESH)
        return c

    lax.fori_loop(1, n, greet, 0)
    pl.semaphore_wait(barrier, n - 1)

    def scatter(j, s):
        return pltpu.make_async_remote_copy(
            src_ref=x_ref.at[j],
            dst_ref=recv.at[s],
            send_sem=ssend.at[j],
            recv_sem=srecv.at[s],
            device_id=dev(j),
            device_id_type=MESH,
        )

    def spread(j):
        return pltpu.make_async_remote_copy(
            src_ref=x_ref.at[j],
            dst_ref=gath.at[j],
            send_sem=bsend.at[j],
            recv_sem=brecv.at[0],
            device_id=dev(j),
            device_id_type=MESH,
        )

    if summed > 0:
        def start_scatter(i, c):
            j = lax.rem(me + i, n)

            @pl.when(j < summed)
            def _():
                scatter(j, me).start()

            return c

        lax.fori_loop(1, n, start_scatter, 0)

    if summed < n:
        @pl.when(me == source)
        def _():
            def start_spread(i, c):
                j = lax.rem(me + i, n)

                @pl.when(j >= summed)
                def _():
                    spread(j).start()

                return c

            lax.fori_loop(1, n, start_spread, 0)
            if source >= summed:
                gath[source] = x_ref[source]

    if summed > 0:
        @pl.when(me < summed)
        def _():
            recv[me] = x_ref[me]

            def wait_scatter(i, c):
                s = lax.rem(me + n - i, n)
                scatter(s, s).wait_recv()
                return c

            lax.fori_loop(1, n, wait_scatter, 0)
            total = recv[0].astype(jnp.float32)
            for s in range(1, n):
                total = total + recv[s].astype(jnp.float32)
            gath[me] = total.astype(gath.dtype)

        def wait_scatter_sent(i, c):
            j = lax.rem(me + i, n)

            @pl.when(j < summed)
            def _():
                scatter(j, me).wait_send()

            return c

        lax.fori_loop(1, n, wait_scatter_sent, 0)

    if summed < n:
        @pl.when((me >= summed) & (me != source))
        def _():
            spread(me).wait_recv()

        @pl.when(me == source)
        def _():
            def wait_spread_sent(i, c):
                j = lax.rem(me + i, n)

                @pl.when(j >= summed)
                def _():
                    spread(j).wait_send()

                return c

            lax.fori_loop(1, n, wait_spread_sent, 0)

    def gather(j, s):
        return pltpu.make_async_remote_copy(
            src_ref=gath.at[s],
            dst_ref=gath.at[s],
            send_sem=gsend.at[j],
            recv_sem=grecv.at[s],
            device_id=dev(j),
            device_id_type=MESH,
        )

    def start_gather(i, c):
        gather(lax.rem(me + i, n), me).start()
        return c

    lax.fori_loop(1, n, start_gather, 0)

    def wait_gather(i, c):
        gather(lax.rem(me + n - i, n), lax.rem(me + n - i, n)).wait_recv()
        gather(lax.rem(me + i, n), me).wait_send()
        return c

    lax.fori_loop(1, n, wait_gather, 0)
    o_ref[...] = gath[...]


def axis_sum(x, axis, other, collective_id, summed_rows, source):
    n = lax.axis_size(axis)
    chunks = x.reshape(n, x.shape[0] // n, x.shape[1])
    summed = summed_rows // chunks.shape[1]
    out = pl.pallas_call(
        functools.partial(sum_kernel, axis, other, n, summed, source),
        out_shape=jax.ShapeDtypeStruct(chunks.shape, chunks.dtype),
        in_specs=[pl.BlockSpec(memory_space=pltpu.VMEM)],
        out_specs=pl.BlockSpec(memory_space=pltpu.VMEM),
        scratch_shapes=[
            pltpu.VMEM(chunks.shape, chunks.dtype),
            pltpu.VMEM(chunks.shape, chunks.dtype),
            pltpu.SemaphoreType.DMA((n,)),
            pltpu.SemaphoreType.DMA((n,)),
            pltpu.SemaphoreType.DMA((n,)),
            pltpu.SemaphoreType.DMA((1,)),
            pltpu.SemaphoreType.DMA((n,)),
            pltpu.SemaphoreType.DMA((n,)),
        ],
        compiler_params=pltpu.CompilerParams(
            collective_id=collective_id, has_side_effects=True
        ),
    )(chunks)
    return out.reshape(x.shape)


def group_kernel(stride, size, mode, x_ref, o_ref, buf, send, recv):
    p = lax.axis_index("prow")
    q = lax.axis_index("pcol")
    me = lax.rem(p // stride, size)
    base = p - me * stride

    def dev(k):
        return (base + k * stride, q)

    barrier = pltpu.get_barrier_semaphore()

    def greet(i, c):
        pl.semaphore_signal(barrier, 1, device_id=dev(lax.rem(me + i, size)), device_id_type=MESH)
        return c

    lax.fori_loop(1, size, greet, 0)
    pl.semaphore_wait(barrier, size - 1)

    def copy(k, s):
        src = x_ref.at[k] if mode == "rs" else buf.at[s]
        return pltpu.make_async_remote_copy(
            src_ref=src,
            dst_ref=buf.at[s],
            send_sem=send.at[k],
            recv_sem=recv.at[s],
            device_id=dev(k),
            device_id_type=MESH,
        )

    if mode == "ag":
        buf[me] = x_ref[...]

    def start(i, c):
        copy(lax.rem(me + i, size), me).start()
        return c

    lax.fori_loop(1, size, start, 0)
    if mode == "rs":
        buf[me] = x_ref[me]

    def wait(i, c):
        s = lax.rem(me + size - i, size)
        copy(s, s).wait_recv()
        copy(lax.rem(me + i, size), me).wait_send()
        return c

    lax.fori_loop(1, size, wait, 0)
    if mode == "rs":
        total = buf[0].astype(jnp.float32)
        for s in range(1, size):
            total = total + buf[s].astype(jnp.float32)
        o_ref[...] = total.astype(o_ref.dtype)
    else:
        o_ref[...] = buf[...]


def group_step(x, stride, size, mode, collective_id):
    if mode == "rs":
        chunks = x.reshape(size, x.shape[0] // size, x.shape[1])
        out_shape = chunks.shape[1:]
        buf_shape = chunks.shape
    else:
        chunks = x
        out_shape = (size,) + x.shape
        buf_shape = out_shape
    out = pl.pallas_call(
        functools.partial(group_kernel, stride, size, mode),
        out_shape=jax.ShapeDtypeStruct(out_shape, x.dtype),
        in_specs=[pl.BlockSpec(memory_space=pltpu.VMEM)],
        out_specs=pl.BlockSpec(memory_space=pltpu.VMEM),
        scratch_shapes=[
            pltpu.VMEM(buf_shape, x.dtype),
            pltpu.SemaphoreType.DMA((size,)),
            pltpu.SemaphoreType.DMA((size,)),
        ],
        compiler_params=pltpu.CompilerParams(
            collective_id=collective_id, has_side_effects=True
        ),
    )(chunks)
    if mode == "ag":
        out = out.reshape(size * x.shape[0], x.shape[1])
    return out


def prow_kernel(xd, yd, top, t_ref, o_ref, b1, a2, b2, b3, b4, sends, recvs, tsend, trecv):
    p = lax.axis_index("prow")
    q = lax.axis_index("pcol")
    xi = lax.rem(p, xd)
    yi = p // xd
    xt, yt = top % xd, top // xd

    def xdev(k):
        return (yi * xd + k, q)

    def ydev(k):
        return (k * xd + xi, q)

    barrier = pltpu.get_barrier_semaphore()

    def greet_x(i, c):
        pl.semaphore_signal(barrier, 1, device_id=xdev(lax.rem(xi + i, xd)), device_id_type=MESH)
        return c

    def greet_y(i, c):
        pl.semaphore_signal(barrier, 1, device_id=ydev(lax.rem(yi + i, yd)), device_id_type=MESH)
        return c

    lax.fori_loop(1, xd, greet_x, 0)
    lax.fori_loop(1, yd, greet_y, 0)
    pl.semaphore_wait(barrier, xd + yd - 2)

    def exchange(phase, src, dst, me, size, dev):
        def copy(k, s):
            return pltpu.make_async_remote_copy(
                src_ref=src(k, s),
                dst_ref=dst(s),
                send_sem=sends.at[phase, k],
                recv_sem=recvs.at[phase, s],
                device_id=dev(k),
                device_id_type=MESH,
            )

        def start(i, c):
            copy(lax.rem(me + i, size), me).start()
            return c

        lax.fori_loop(1, size, start, 0)

        def wait(i, c):
            s = lax.rem(me + size - i, size)
            copy(s, s).wait_recv()
            copy(lax.rem(me + i, size), me).wait_send()
            return c

        lax.fori_loop(1, size, wait, 0)

    def total(parts, size):
        acc = parts(0).astype(jnp.float32)
        for s in range(1, size):
            acc = acc + parts(s).astype(jnp.float32)
        return acc

    def top_copy(k):
        return pltpu.make_async_remote_copy(
            src_ref=t_ref.at[k, 1],
            dst_ref=b1.at[xt, 1],
            send_sem=tsend.at[k],
            recv_sem=trecv.at[0],
            device_id=xdev(k),
            device_id_type=MESH,
        )

    @pl.when(p == top)
    def _():
        def start(i, c):
            top_copy(lax.rem(xi + i, xd)).start()
            return c

        lax.fori_loop(1, xd, start, 0)

    exchange(0, lambda k, s: t_ref.at[k, 0], lambda s: b1.at[s, 0], xi, xd, xdev)
    b1[xi, 0] = t_ref[xi, 0]
    top_half = (yd // 2, b1.shape[2] * 2 // yd, b1.shape[3])
    a2[: yd // 2] = total(lambda s: b1[s, 0], xd).astype(a2.dtype).reshape(top_half)

    @pl.when(p == top)
    def _():
        def sent(i, c):
            top_copy(lax.rem(xi + i, xd)).wait_send()
            return c

        lax.fori_loop(1, xd, sent, 0)
        a3 = t_ref[xi, 1]
        a2[yd // 2 :] = a3.reshape(top_half)

    @pl.when((yi == yt) & (p != top))
    def _():
        top_copy(xi).wait_recv()
        a2[yd // 2 :] = b1[xt, 1].reshape(top_half)

    @pl.when(yi != yt)
    def _():
        a2[yd // 2 :] = jnp.zeros(top_half, a2.dtype)

    exchange(1, lambda k, s: a2.at[k], lambda s: b2.at[s], yi, yd, ydev)
    b2[yi] = a2[yi]
    b3[yi] = total(lambda s: b2[s], yd).astype(b3.dtype)
    exchange(2, lambda k, s: b3.at[s], lambda s: b3.at[s], yi, yd, ydev)
    b4[xi] = b3[...].reshape(b4.shape[1:])
    exchange(3, lambda k, s: b4.at[s], lambda s: b4.at[s], xi, xd, xdev)
    o_ref[...] = b4[...]


def prow_sum(picked, top_part, xd, top):
    yd = lax.axis_size("prow") // xd
    rows, cols = picked.shape
    chunks = jnp.stack(
        [picked.reshape(xd, rows // xd, cols), top_part.reshape(xd, rows // xd, cols)], axis=1
    )
    part = 2 * rows // xd // yd
    out = pl.pallas_call(
        functools.partial(prow_kernel, xd, yd, top),
        out_shape=jax.ShapeDtypeStruct((xd, yd, part, cols), picked.dtype),
        in_specs=[pl.BlockSpec(memory_space=pltpu.VMEM)],
        out_specs=pl.BlockSpec(memory_space=pltpu.VMEM),
        scratch_shapes=[
            pltpu.VMEM(chunks.shape, picked.dtype),
            pltpu.VMEM((yd, part, cols), picked.dtype),
            pltpu.VMEM((yd, part, cols), picked.dtype),
            pltpu.VMEM((yd, part, cols), picked.dtype),
            pltpu.VMEM((xd, yd, part, cols), picked.dtype),
            pltpu.SemaphoreType.DMA((4, max(xd, yd))),
            pltpu.SemaphoreType.DMA((4, max(xd, yd))),
            pltpu.SemaphoreType.DMA((xd,)),
            pltpu.SemaphoreType.DMA((1,)),
        ],
        compiler_params=pltpu.CompilerParams(collective_id=10 + top, has_side_effects=True),
    )(chunks)
    out = out.reshape(xd, 2, rows // xd, cols)
    return out[:, 0].reshape(rows, cols), out[:, 1].reshape(rows, cols)


def pcol_kernel(nz, source, x_ref, o_ref, g, p1send, p1recv, p2send, p2recv, p3send, p3recv):
    q = lax.axis_index("pcol")
    p = lax.axis_index("prow")
    nc = lax.axis_size("pcol") // nz
    z = q // nc
    c = lax.rem(q, nc)
    zs, cs = source // nc, source % nc

    def dev(zz, cc):
        return (p, zz * nc + cc)

    barrier = pltpu.get_barrier_semaphore()
    pl.semaphore_signal(barrier, 1, device_id=dev(z, 1 - c), device_id_type=MESH)

    @pl.when(c == cs)
    def _():
        def greet(i, carry):
            pl.semaphore_signal(
                barrier, 1, device_id=dev(lax.rem(z + i, nz), cs), device_id_type=MESH
            )
            return carry

        lax.fori_loop(1, nz, greet, 0)
        pl.semaphore_wait(barrier, nz)

    @pl.when(c != cs)
    def _():
        pl.semaphore_wait(barrier, 1)

    def spread(j):
        return pltpu.make_async_remote_copy(
            src_ref=x_ref.at[j],
            dst_ref=g.at[j],
            send_sem=p1send.at[j],
            recv_sem=p1recv.at[0],
            device_id=dev(j, cs),
            device_id_type=MESH,
        )

    def ring(j, s):
        return pltpu.make_async_remote_copy(
            src_ref=g.at[s],
            dst_ref=g.at[s],
            send_sem=p2send.at[j],
            recv_sem=p2recv.at[s],
            device_id=dev(j, cs),
            device_id_type=MESH,
        )

    def partner(zz):
        return pltpu.make_async_remote_copy(
            src_ref=g,
            dst_ref=g,
            send_sem=p3send.at[0],
            recv_sem=p3recv.at[0],
            device_id=dev(zz, 1 - cs),
            device_id_type=MESH,
        )

    @pl.when(q == source)
    def _():
        def start(i, carry):
            spread(lax.rem(zs + i, nz)).start()
            return carry

        lax.fori_loop(1, nz, start, 0)
        g[zs] = x_ref[zs]

    @pl.when((c == cs) & (z != zs))
    def _():
        spread(z).wait_recv()

    @pl.when(c == cs)
    def _():
        def start(i, carry):
            ring(lax.rem(z + i, nz), z).start()
            return carry

        lax.fori_loop(1, nz, start, 0)

        def wait(i, carry):
            s = lax.rem(z + nz - i, nz)
            ring(s, s).wait_recv()
            ring(lax.rem(z + i, nz), z).wait_send()
            return carry

        lax.fori_loop(1, nz, wait, 0)
        partner(z).start()
        partner(z).wait_send()

    @pl.when(c != cs)
    def _():
        partner(z).wait_recv()

    @pl.when(q == source)
    def _():
        def sent(i, carry):
            spread(lax.rem(zs + i, nz)).wait_send()
            return carry

        lax.fori_loop(1, nz, sent, 0)

    o_ref[...] = g[...]


def pcol_bcast(x, nz, source, collective_id):
    rows, cols = x.shape
    chunks = x.reshape(nz, rows // nz, cols)
    out = pl.pallas_call(
        functools.partial(pcol_kernel, nz, source),
        out_shape=jax.ShapeDtypeStruct(chunks.shape, x.dtype),
        in_specs=[pl.BlockSpec(memory_space=pltpu.VMEM)],
        out_specs=pl.BlockSpec(memory_space=pltpu.VMEM),
        scratch_shapes=[
            pltpu.VMEM(chunks.shape, x.dtype),
            pltpu.SemaphoreType.DMA((nz,)),
            pltpu.SemaphoreType.DMA((1,)),
            pltpu.SemaphoreType.DMA((nz,)),
            pltpu.SemaphoreType.DMA((nz,)),
            pltpu.SemaphoreType.DMA((1,)),
            pltpu.SemaphoreType.DMA((1,)),
        ],
        compiler_params=pltpu.CompilerParams(collective_id=collective_id, has_side_effects=True),
    )(chunks)
    return out.reshape(rows, cols)


def update_kernel(a_ref, l_ref, u_ref, rf_ref, cf_ref, o_ref):
    a = a_ref[...]
    lower = l_ref[...]
    upper = u_ref[...]
    product = jnp.dot(lower, upper, preferred_element_type=jnp.float32)
    changed = (a.astype(jnp.float32) - product).astype(a.dtype)
    reps = a.shape[1] // lower.shape[1]
    lower_wide = jnp.concatenate([lower] * reps, axis=1)
    rf = rf_ref[...]
    cf = cf_ref[...]
    below = (rf & 1) == 1
    in_top = (rf & 2) == 2
    right = (cf & 1) == 1
    in_panel = (cf & 2) == 2
    o_ref[...] = jnp.where(
        below & right,
        changed,
        jnp.where(in_panel & below, lower_wide, jnp.where(in_top & right, upper, a)),
    )


def trailing_update(a, lower, upper, row_flags, col_flags):
    rows, cols = a.shape
    block = upper.shape[0]
    return pl.pallas_call(
        update_kernel,
        out_shape=jax.ShapeDtypeStruct(a.shape, a.dtype),
        grid=(rows // block,),
        in_specs=[
            pl.BlockSpec((block, cols), lambda i: (i, 0)),
            pl.BlockSpec((block, block), lambda i: (i, 0)),
            pl.BlockSpec((block, cols), lambda i: (0, 0)),
            pl.BlockSpec((block, 1), lambda i: (i, 0)),
            pl.BlockSpec((1, cols), lambda i: (0, 0)),
        ],
        out_specs=pl.BlockSpec((block, cols), lambda i: (i, 0)),
    )(a, lower, upper, row_flags, col_flags)


def local(x_devices, z_chips, matrix, pivots, lower_inverse, upper_inverse):
    row_count = lax.axis_size("prow")
    col_count = lax.axis_size("pcol")
    my_row = lax.axis_index("prow")
    my_col = lax.axis_index("pcol")
    blocks_down, block, blocks_across, _ = matrix.shape
    local_rows = blocks_down * block
    local_cols = blocks_across * block
    current = matrix.reshape(local_rows, local_cols)
    row_place = jnp.arange(local_rows)
    col_place = jnp.arange(local_cols)
    global_rows = (row_place // block * row_count + my_row) * block + row_place % block
    global_cols = (col_place // block * col_count + my_col) * block + col_place % block
    for panel in range(pivots.shape[0]):
        start = panel * block
        chosen = pivots[panel]
        block_row = chosen // block
        is_mine = block_row % row_count == my_row
        local_index = block_row // row_count * block + chosen % block
        safe_index = jnp.where(is_mine, local_index, 0)
        picked = jnp.where(is_mine[:, None], current[safe_index], jnp.zeros((), jnp.bfloat16))
        top_holder = panel % row_count
        top_first = panel // row_count * block
        is_top = my_row == top_holder
        top_local = current[top_first : top_first + block]
        top_part = jnp.where(is_top, top_local, jnp.zeros((), jnp.bfloat16))
        incoming, old_top = prow_sum(picked, top_part, x_devices, top_holder)
        target = jnp.where(is_mine, local_index, local_rows)
        current = current.at[target].set(old_top, mode="drop")
        top_now = current[top_first : top_first + block]
        current = current.at[top_first : top_first + block].set(
            jnp.where(is_top, incoming, top_now)
        )
        panel_holder = panel % col_count
        panel_first = panel // col_count * block
        panel_cols = current[:, panel_first : panel_first + block]
        factor = jnp.dot(
            panel_cols, upper_inverse[panel], preferred_element_type=jnp.float32
        ).astype(jnp.bfloat16)
        is_panel = my_col == panel_holder
        factor = jnp.where(is_panel, factor, jnp.zeros((), jnp.bfloat16))
        lower = pcol_bcast(factor, z_chips, panel_holder, 20 + panel)
        upper = jnp.dot(
            lower_inverse[panel], incoming, preferred_element_type=jnp.float32
        ).astype(jnp.bfloat16)
        row_mask = global_rows >= start + block
        col_mask = global_cols >= start + block
        below = row_mask.astype(jnp.int32)
        right = col_mask.astype(jnp.int32)
        in_panel = (is_panel & (col_place // block == panel_first // block)).astype(jnp.int32)
        in_top = (is_top & (row_place // block == top_first // block)).astype(jnp.int32)
        current = trailing_update(
            current, lower, upper, (below + 2 * in_top)[:, None], (right + 2 * in_panel)[None, :]
        )
    return current.reshape(matrix.shape)


def solution(mesh):
    x_devices = len({d.coords[0] for d in mesh.devices[:, 0]})
    z_chips = len({d.coords[2] for d in mesh.devices[0, :]})
    in_specs = (P(None, "prow", None, "pcol"), P(), P(), P())
    out_specs = P(None, "prow", None, "pcol")
    return jax.shard_map(functools.partial(local, x_devices, z_chips), mesh=mesh, in_specs=in_specs, out_specs=out_specs, check_vma=False)
```

```python
import functools

import jax
import jax.numpy as jnp
from jax import lax
from jax.experimental import pallas as pl
from jax.experimental.pallas import tpu as pltpu
from jax.sharding import PartitionSpec as P

MESH = pl.DeviceIdType.MESH


def sum_kernel(axis, other, n, summed, source, x_ref, o_ref, recv, gath, ssend, srecv,
               bsend, brecv, gsend, grecv):
    me = lax.axis_index(axis)
    them = lax.axis_index(other)

    def dev(j):
        return (j, them) if axis == "prow" else (them, j)

    barrier = pltpu.get_barrier_semaphore()

    def greet(i, c):
        j = lax.rem(me + i, n)
        pl.semaphore_signal(barrier, 1, device_id=dev(j), device_id_type=MESH)
        return c

    lax.fori_loop(1, n, greet, 0)
    pl.semaphore_wait(barrier, n - 1)

    def scatter(j, s):
        return pltpu.make_async_remote_copy(
            src_ref=x_ref.at[j],
            dst_ref=recv.at[s],
            send_sem=ssend.at[j],
            recv_sem=srecv.at[s],
            device_id=dev(j),
            device_id_type=MESH,
        )

    def spread(j):
        return pltpu.make_async_remote_copy(
            src_ref=x_ref.at[j],
            dst_ref=gath.at[j],
            send_sem=bsend.at[j],
            recv_sem=brecv.at[0],
            device_id=dev(j),
            device_id_type=MESH,
        )

    if summed > 0:
        def start_scatter(i, c):
            j = lax.rem(me + i, n)

            @pl.when(j < summed)
            def _():
                scatter(j, me).start()

            return c

        lax.fori_loop(1, n, start_scatter, 0)

    if summed < n:
        @pl.when(me == source)
        def _():
            def start_spread(i, c):
                j = lax.rem(me + i, n)

                @pl.when(j >= summed)
                def _():
                    spread(j).start()

                return c

            lax.fori_loop(1, n, start_spread, 0)
            if source >= summed:
                gath[source] = x_ref[source]

    if summed > 0:
        @pl.when(me < summed)
        def _():
            recv[me] = x_ref[me]

            def wait_scatter(i, c):
                s = lax.rem(me + n - i, n)
                scatter(s, s).wait_recv()
                return c

            lax.fori_loop(1, n, wait_scatter, 0)
            total = recv[0].astype(jnp.float32)
            for s in range(1, n):
                total = total + recv[s].astype(jnp.float32)
            gath[me] = total.astype(gath.dtype)

        def wait_scatter_sent(i, c):
            j = lax.rem(me + i, n)

            @pl.when(j < summed)
            def _():
                scatter(j, me).wait_send()

            return c

        lax.fori_loop(1, n, wait_scatter_sent, 0)

    if summed < n:
        @pl.when((me >= summed) & (me != source))
        def _():
            spread(me).wait_recv()

        @pl.when(me == source)
        def _():
            def wait_spread_sent(i, c):
                j = lax.rem(me + i, n)

                @pl.when(j >= summed)
                def _():
                    spread(j).wait_send()

                return c

            lax.fori_loop(1, n, wait_spread_sent, 0)

    def gather(j, s):
        return pltpu.make_async_remote_copy(
            src_ref=gath.at[s],
            dst_ref=gath.at[s],
            send_sem=gsend.at[j],
            recv_sem=grecv.at[s],
            device_id=dev(j),
            device_id_type=MESH,
        )

    def start_gather(i, c):
        gather(lax.rem(me + i, n), me).start()
        return c

    lax.fori_loop(1, n, start_gather, 0)

    def wait_gather(i, c):
        gather(lax.rem(me + n - i, n), lax.rem(me + n - i, n)).wait_recv()
        gather(lax.rem(me + i, n), me).wait_send()
        return c

    lax.fori_loop(1, n, wait_gather, 0)
    o_ref[...] = gath[...]


def axis_sum(x, axis, other, collective_id, summed_rows, source):
    n = lax.axis_size(axis)
    chunks = x.reshape(n, x.shape[0] // n, x.shape[1])
    summed = summed_rows // chunks.shape[1]
    out = pl.pallas_call(
        functools.partial(sum_kernel, axis, other, n, summed, source),
        out_shape=jax.ShapeDtypeStruct(chunks.shape, chunks.dtype),
        in_specs=[pl.BlockSpec(memory_space=pltpu.VMEM)],
        out_specs=pl.BlockSpec(memory_space=pltpu.VMEM),
        scratch_shapes=[
            pltpu.VMEM(chunks.shape, chunks.dtype),
            pltpu.VMEM(chunks.shape, chunks.dtype),
            pltpu.SemaphoreType.DMA((n,)),
            pltpu.SemaphoreType.DMA((n,)),
            pltpu.SemaphoreType.DMA((n,)),
            pltpu.SemaphoreType.DMA((1,)),
            pltpu.SemaphoreType.DMA((n,)),
            pltpu.SemaphoreType.DMA((n,)),
        ],
        compiler_params=pltpu.CompilerParams(
            collective_id=collective_id, has_side_effects=True
        ),
    )(chunks)
    return out.reshape(x.shape)


def group_kernel(stride, size, mode, x_ref, o_ref, buf, send, recv):
    p = lax.axis_index("prow")
    q = lax.axis_index("pcol")
    me = lax.rem(p // stride, size)
    base = p - me * stride

    def dev(k):
        return (base + k * stride, q)

    barrier = pltpu.get_barrier_semaphore()

    def greet(i, c):
        pl.semaphore_signal(barrier, 1, device_id=dev(lax.rem(me + i, size)), device_id_type=MESH)
        return c

    lax.fori_loop(1, size, greet, 0)
    pl.semaphore_wait(barrier, size - 1)

    def copy(k, s):
        src = x_ref.at[k] if mode == "rs" else buf.at[s]
        return pltpu.make_async_remote_copy(
            src_ref=src,
            dst_ref=buf.at[s],
            send_sem=send.at[k],
            recv_sem=recv.at[s],
            device_id=dev(k),
            device_id_type=MESH,
        )

    if mode == "ag":
        buf[me] = x_ref[...]

    def start(i, c):
        copy(lax.rem(me + i, size), me).start()
        return c

    lax.fori_loop(1, size, start, 0)
    if mode == "rs":
        buf[me] = x_ref[me]

    def wait(i, c):
        s = lax.rem(me + size - i, size)
        copy(s, s).wait_recv()
        copy(lax.rem(me + i, size), me).wait_send()
        return c

    lax.fori_loop(1, size, wait, 0)
    if mode == "rs":
        total = buf[0].astype(jnp.float32)
        for s in range(1, size):
            total = total + buf[s].astype(jnp.float32)
        o_ref[...] = total.astype(o_ref.dtype)
    else:
        o_ref[...] = buf[...]


def group_step(x, stride, size, mode, collective_id):
    if mode == "rs":
        chunks = x.reshape(size, x.shape[0] // size, x.shape[1])
        out_shape = chunks.shape[1:]
        buf_shape = chunks.shape
    else:
        chunks = x
        out_shape = (size,) + x.shape
        buf_shape = out_shape
    out = pl.pallas_call(
        functools.partial(group_kernel, stride, size, mode),
        out_shape=jax.ShapeDtypeStruct(out_shape, x.dtype),
        in_specs=[pl.BlockSpec(memory_space=pltpu.VMEM)],
        out_specs=pl.BlockSpec(memory_space=pltpu.VMEM),
        scratch_shapes=[
            pltpu.VMEM(buf_shape, x.dtype),
            pltpu.SemaphoreType.DMA((size,)),
            pltpu.SemaphoreType.DMA((size,)),
        ],
        compiler_params=pltpu.CompilerParams(
            collective_id=collective_id, has_side_effects=True
        ),
    )(chunks)
    if mode == "ag":
        out = out.reshape(size * x.shape[0], x.shape[1])
    return out


def prow_kernel(xd, yd, top, t_ref, o_ref, b1, a2, b2, b3, b4, sends, recvs, tsend, trecv):
    p = lax.axis_index("prow")
    q = lax.axis_index("pcol")
    xi = lax.rem(p, xd)
    yi = p // xd
    xt, yt = top % xd, top // xd

    def xdev(k):
        return (yi * xd + k, q)

    def ydev(k):
        return (k * xd + xi, q)

    barrier = pltpu.get_barrier_semaphore()

    def greet_x(i, c):
        pl.semaphore_signal(barrier, 1, device_id=xdev(lax.rem(xi + i, xd)), device_id_type=MESH)
        return c

    def greet_y(i, c):
        pl.semaphore_signal(barrier, 1, device_id=ydev(lax.rem(yi + i, yd)), device_id_type=MESH)
        return c

    lax.fori_loop(1, xd, greet_x, 0)
    lax.fori_loop(1, yd, greet_y, 0)
    pl.semaphore_wait(barrier, xd + yd - 2)

    def exchange(phase, src, dst, me, size, dev):
        def copy(k, s):
            return pltpu.make_async_remote_copy(
                src_ref=src(k, s),
                dst_ref=dst(s),
                send_sem=sends.at[phase, k],
                recv_sem=recvs.at[phase, s],
                device_id=dev(k),
                device_id_type=MESH,
            )

        def start(i, c):
            copy(lax.rem(me + i, size), me).start()
            return c

        lax.fori_loop(1, size, start, 0)

        def wait(i, c):
            s = lax.rem(me + size - i, size)
            copy(s, s).wait_recv()
            copy(lax.rem(me + i, size), me).wait_send()
            return c

        lax.fori_loop(1, size, wait, 0)

    def total(parts, size):
        acc = parts(0).astype(jnp.float32)
        for s in range(1, size):
            acc = acc + parts(s).astype(jnp.float32)
        return acc

    def top_copy(k):
        return pltpu.make_async_remote_copy(
            src_ref=t_ref.at[k, 1],
            dst_ref=b1.at[xt, 1],
            send_sem=tsend.at[k],
            recv_sem=trecv.at[0],
            device_id=xdev(k),
            device_id_type=MESH,
        )

    @pl.when(p == top)
    def _():
        def start(i, c):
            top_copy(lax.rem(xi + i, xd)).start()
            return c

        lax.fori_loop(1, xd, start, 0)

    exchange(0, lambda k, s: t_ref.at[k, 0], lambda s: b1.at[s, 0], xi, xd, xdev)
    b1[xi, 0] = t_ref[xi, 0]
    top_half = (yd // 2, b1.shape[2] * 2 // yd, b1.shape[3])
    a2[: yd // 2] = total(lambda s: b1[s, 0], xd).astype(a2.dtype).reshape(top_half)

    @pl.when(p == top)
    def _():
        def sent(i, c):
            top_copy(lax.rem(xi + i, xd)).wait_send()
            return c

        lax.fori_loop(1, xd, sent, 0)
        a3 = t_ref[xi, 1]
        a2[yd // 2 :] = a3.reshape(top_half)

    @pl.when((yi == yt) & (p != top))
    def _():
        top_copy(xi).wait_recv()
        a2[yd // 2 :] = b1[xt, 1].reshape(top_half)

    @pl.when(yi != yt)
    def _():
        a2[yd // 2 :] = jnp.zeros(top_half, a2.dtype)

    exchange(1, lambda k, s: a2.at[k], lambda s: b2.at[s], yi, yd, ydev)
    b2[yi] = a2[yi]
    b3[yi] = total(lambda s: b2[s], yd).astype(b3.dtype)
    exchange(2, lambda k, s: b3.at[s], lambda s: b3.at[s], yi, yd, ydev)
    b4[xi] = b3[...].reshape(b4.shape[1:])
    exchange(3, lambda k, s: b4.at[s], lambda s: b4.at[s], xi, xd, xdev)
    o_ref[...] = b4[...]


def prow_sum(picked, top_part, xd, top):
    yd = lax.axis_size("prow") // xd
    rows, cols = picked.shape
    chunks = jnp.stack(
        [picked.reshape(xd, rows // xd, cols), top_part.reshape(xd, rows // xd, cols)], axis=1
    )
    part = 2 * rows // xd // yd
    out = pl.pallas_call(
        functools.partial(prow_kernel, xd, yd, top),
        out_shape=jax.ShapeDtypeStruct((xd, yd, part, cols), picked.dtype),
        in_specs=[pl.BlockSpec(memory_space=pltpu.VMEM)],
        out_specs=pl.BlockSpec(memory_space=pltpu.VMEM),
        scratch_shapes=[
            pltpu.VMEM(chunks.shape, picked.dtype),
            pltpu.VMEM((yd, part, cols), picked.dtype),
            pltpu.VMEM((yd, part, cols), picked.dtype),
            pltpu.VMEM((yd, part, cols), picked.dtype),
            pltpu.VMEM((xd, yd, part, cols), picked.dtype),
            pltpu.SemaphoreType.DMA((4, max(xd, yd))),
            pltpu.SemaphoreType.DMA((4, max(xd, yd))),
            pltpu.SemaphoreType.DMA((xd,)),
            pltpu.SemaphoreType.DMA((1,)),
        ],
        compiler_params=pltpu.CompilerParams(collective_id=10 + top, has_side_effects=True),
    )(chunks)
    out = out.reshape(xd, 2, rows // xd, cols)
    return out[:, 0].reshape(rows, cols), out[:, 1].reshape(rows, cols)


def pcol_kernel(nz, source, x_ref, o_ref, g, p1send, p1recv, p2send, p2recv, p3send, p3recv):
    q = lax.axis_index("pcol")
    p = lax.axis_index("prow")
    nc = lax.axis_size("pcol") // nz
    z = q // nc
    c = lax.rem(q, nc)
    zs, cs = source // nc, source % nc

    def dev(zz, cc):
        return (p, zz * nc + cc)

    barrier = pltpu.get_barrier_semaphore()
    pl.semaphore_signal(barrier, 1, device_id=dev(z, 1 - c), device_id_type=MESH)

    @pl.when(c == cs)
    def _():
        def greet(i, carry):
            pl.semaphore_signal(
                barrier, 1, device_id=dev(lax.rem(z + i, nz), cs), device_id_type=MESH
            )
            return carry

        lax.fori_loop(1, nz, greet, 0)
        pl.semaphore_wait(barrier, nz)

    @pl.when(c != cs)
    def _():
        pl.semaphore_wait(barrier, 1)

    def spread(j):
        return pltpu.make_async_remote_copy(
            src_ref=x_ref.at[j],
            dst_ref=g.at[j],
            send_sem=p1send.at[j],
            recv_sem=p1recv.at[0],
            device_id=dev(j, cs),
            device_id_type=MESH,
        )

    def ring(j, s):
        return pltpu.make_async_remote_copy(
            src_ref=g.at[s],
            dst_ref=g.at[s],
            send_sem=p2send.at[j],
            recv_sem=p2recv.at[s],
            device_id=dev(j, cs),
            device_id_type=MESH,
        )

    def partner(zz):
        return pltpu.make_async_remote_copy(
            src_ref=g,
            dst_ref=g,
            send_sem=p3send.at[0],
            recv_sem=p3recv.at[0],
            device_id=dev(zz, 1 - cs),
            device_id_type=MESH,
        )

    @pl.when(q == source)
    def _():
        def start(i, carry):
            spread(lax.rem(zs + i, nz)).start()
            return carry

        lax.fori_loop(1, nz, start, 0)
        g[zs] = x_ref[zs]

    @pl.when((c == cs) & (z != zs))
    def _():
        spread(z).wait_recv()

    @pl.when(c == cs)
    def _():
        def start(i, carry):
            ring(lax.rem(z + i, nz), z).start()
            return carry

        lax.fori_loop(1, nz, start, 0)

        def wait(i, carry):
            s = lax.rem(z + nz - i, nz)
            ring(s, s).wait_recv()
            ring(lax.rem(z + i, nz), z).wait_send()
            return carry

        lax.fori_loop(1, nz, wait, 0)
        partner(z).start()
        partner(z).wait_send()

    @pl.when(c != cs)
    def _():
        partner(z).wait_recv()

    @pl.when(q == source)
    def _():
        def sent(i, carry):
            spread(lax.rem(zs + i, nz)).wait_send()
            return carry

        lax.fori_loop(1, nz, sent, 0)

    o_ref[...] = g[...]


def pcol_bcast(x, nz, source, collective_id):
    rows, cols = x.shape
    chunks = x.reshape(nz, rows // nz, cols)
    out = pl.pallas_call(
        functools.partial(pcol_kernel, nz, source),
        out_shape=jax.ShapeDtypeStruct(chunks.shape, x.dtype),
        in_specs=[pl.BlockSpec(memory_space=pltpu.VMEM)],
        out_specs=pl.BlockSpec(memory_space=pltpu.VMEM),
        scratch_shapes=[
            pltpu.VMEM(chunks.shape, x.dtype),
            pltpu.SemaphoreType.DMA((nz,)),
            pltpu.SemaphoreType.DMA((1,)),
            pltpu.SemaphoreType.DMA((nz,)),
            pltpu.SemaphoreType.DMA((nz,)),
            pltpu.SemaphoreType.DMA((1,)),
            pltpu.SemaphoreType.DMA((1,)),
        ],
        compiler_params=pltpu.CompilerParams(collective_id=collective_id, has_side_effects=True),
    )(chunks)
    return out.reshape(rows, cols)


def update_kernel(rf_ref, cf_ref, a_ref, l_ref, u_ref, o_ref):
    rb = rf_ref[pl.program_id(0)]
    below = (rb & 1) == 1
    in_top = (rb & 2) == 2
    lower = l_ref[...]
    block = lower.shape[1]
    for c in range(a_ref.shape[1] // block):
        cols = slice(c * block, (c + 1) * block)
        cb = cf_ref[c]
        right = (cb & 1) == 1
        in_panel = (cb & 2) == 2
        a = a_ref[:, cols]
        upper = u_ref[:, cols]
        product = jnp.dot(lower, upper, preferred_element_type=jnp.float32)
        changed = (a.astype(jnp.float32) - product).astype(a.dtype)
        o_ref[:, cols] = jnp.where(
            below & right,
            changed,
            jnp.where(in_panel & below, lower, jnp.where(in_top & right, upper, a)),
        )


def trailing_update(a, lower, upper, row_flags, col_flags):
    rows, cols = a.shape
    block = upper.shape[0]
    return pl.pallas_call(
        update_kernel,
        out_shape=jax.ShapeDtypeStruct(a.shape, a.dtype),
        grid_spec=pltpu.PrefetchScalarGridSpec(
            num_scalar_prefetch=2,
            grid=(rows // block,),
            in_specs=[
                pl.BlockSpec((block, cols), lambda i, rf, cf: (i, 0)),
                pl.BlockSpec((block, block), lambda i, rf, cf: (i, 0)),
                pl.BlockSpec((block, cols), lambda i, rf, cf: (0, 0)),
            ],
            out_specs=pl.BlockSpec((block, cols), lambda i, rf, cf: (i, 0)),
        ),
    )(row_flags, col_flags, a, lower, upper)


def local(x_devices, z_chips, matrix, pivots, lower_inverse, upper_inverse):
    row_count = lax.axis_size("prow")
    col_count = lax.axis_size("pcol")
    my_row = lax.axis_index("prow")
    my_col = lax.axis_index("pcol")
    blocks_down, block, blocks_across, _ = matrix.shape
    local_rows = blocks_down * block
    local_cols = blocks_across * block
    current = matrix.reshape(local_rows, local_cols)
    row_place = jnp.arange(local_rows)
    col_place = jnp.arange(local_cols)
    global_rows = (row_place // block * row_count + my_row) * block + row_place % block
    global_cols = (col_place // block * col_count + my_col) * block + col_place % block
    for panel in range(pivots.shape[0]):
        start = panel * block
        chosen = pivots[panel]
        block_row = chosen // block
        is_mine = block_row % row_count == my_row
        local_index = block_row // row_count * block + chosen % block
        safe_index = jnp.where(is_mine, local_index, 0)
        picked = jnp.where(is_mine[:, None], current[safe_index], jnp.zeros((), jnp.bfloat16))
        top_holder = panel % row_count
        top_first = panel // row_count * block
        is_top = my_row == top_holder
        top_local = current[top_first : top_first + block]
        top_part = jnp.where(is_top, top_local, jnp.zeros((), jnp.bfloat16))
        incoming, old_top = prow_sum(picked, top_part, x_devices, top_holder)
        target = jnp.where(is_mine, local_index, local_rows)
        current = current.at[target].set(old_top, mode="drop")
        top_now = current[top_first : top_first + block]
        current = current.at[top_first : top_first + block].set(
            jnp.where(is_top, incoming, top_now)
        )
        panel_holder = panel % col_count
        panel_first = panel // col_count * block
        panel_cols = current[:, panel_first : panel_first + block]
        factor = jnp.dot(
            panel_cols, upper_inverse[panel], preferred_element_type=jnp.float32
        ).astype(jnp.bfloat16)
        is_panel = my_col == panel_holder
        factor = jnp.where(is_panel, factor, jnp.zeros((), jnp.bfloat16))
        lower = pcol_bcast(factor, z_chips, panel_holder, 20 + panel)
        upper = jnp.dot(
            lower_inverse[panel], incoming, preferred_element_type=jnp.float32
        ).astype(jnp.bfloat16)
        row_mask = global_rows >= start + block
        col_mask = global_cols >= start + block
        row_blocks = row_place[::block] // block
        col_blocks = col_place[::block] // block
        below = (row_blocks * row_count + my_row >= panel + 1).astype(jnp.int32)
        right = (col_blocks * col_count + my_col >= panel + 1).astype(jnp.int32)
        in_top = (is_top & (row_blocks == top_first // block)).astype(jnp.int32)
        in_panel = (is_panel & (col_blocks == panel_first // block)).astype(jnp.int32)
        current = trailing_update(current, lower, upper, below + 2 * in_top, right + 2 * in_panel)
    return current.reshape(matrix.shape)


def solution(mesh):
    x_devices = len({d.coords[0] for d in mesh.devices[:, 0]})
    z_chips = len({d.coords[2] for d in mesh.devices[0, :]})
    in_specs = (P(None, "prow", None, "pcol"), P(), P(), P())
    out_specs = P(None, "prow", None, "pcol")
    return jax.shard_map(functools.partial(local, x_devices, z_chips), mesh=mesh, in_specs=in_specs, out_specs=out_specs, check_vma=False)
```

```python
import functools

import jax
import jax.numpy as jnp
from jax import lax
from jax.experimental import pallas as pl
from jax.experimental.pallas import tpu as pltpu
from jax.sharding import PartitionSpec as P

MESH = pl.DeviceIdType.MESH


def sum_kernel(axis, other, n, summed, source, x_ref, o_ref, recv, gath, ssend, srecv,
               bsend, brecv, gsend, grecv):
    me = lax.axis_index(axis)
    them = lax.axis_index(other)

    def dev(j):
        return (j, them) if axis == "prow" else (them, j)

    barrier = pltpu.get_barrier_semaphore()

    def greet(i, c):
        j = lax.rem(me + i, n)
        pl.semaphore_signal(barrier, 1, device_id=dev(j), device_id_type=MESH)
        return c

    lax.fori_loop(1, n, greet, 0)
    pl.semaphore_wait(barrier, n - 1)

    def scatter(j, s):
        return pltpu.make_async_remote_copy(
            src_ref=x_ref.at[j],
            dst_ref=recv.at[s],
            send_sem=ssend.at[j],
            recv_sem=srecv.at[s],
            device_id=dev(j),
            device_id_type=MESH,
        )

    def spread(j):
        return pltpu.make_async_remote_copy(
            src_ref=x_ref.at[j],
            dst_ref=gath.at[j],
            send_sem=bsend.at[j],
            recv_sem=brecv.at[0],
            device_id=dev(j),
            device_id_type=MESH,
        )

    if summed > 0:
        def start_scatter(i, c):
            j = lax.rem(me + i, n)

            @pl.when(j < summed)
            def _():
                scatter(j, me).start()

            return c

        lax.fori_loop(1, n, start_scatter, 0)

    if summed < n:
        @pl.when(me == source)
        def _():
            def start_spread(i, c):
                j = lax.rem(me + i, n)

                @pl.when(j >= summed)
                def _():
                    spread(j).start()

                return c

            lax.fori_loop(1, n, start_spread, 0)
            if source >= summed:
                gath[source] = x_ref[source]

    if summed > 0:
        @pl.when(me < summed)
        def _():
            recv[me] = x_ref[me]

            def wait_scatter(i, c):
                s = lax.rem(me + n - i, n)
                scatter(s, s).wait_recv()
                return c

            lax.fori_loop(1, n, wait_scatter, 0)
            total = recv[0].astype(jnp.float32)
            for s in range(1, n):
                total = total + recv[s].astype(jnp.float32)
            gath[me] = total.astype(gath.dtype)

        def wait_scatter_sent(i, c):
            j = lax.rem(me + i, n)

            @pl.when(j < summed)
            def _():
                scatter(j, me).wait_send()

            return c

        lax.fori_loop(1, n, wait_scatter_sent, 0)

    if summed < n:
        @pl.when((me >= summed) & (me != source))
        def _():
            spread(me).wait_recv()

        @pl.when(me == source)
        def _():
            def wait_spread_sent(i, c):
                j = lax.rem(me + i, n)

                @pl.when(j >= summed)
                def _():
                    spread(j).wait_send()

                return c

            lax.fori_loop(1, n, wait_spread_sent, 0)

    def gather(j, s):
        return pltpu.make_async_remote_copy(
            src_ref=gath.at[s],
            dst_ref=gath.at[s],
            send_sem=gsend.at[j],
            recv_sem=grecv.at[s],
            device_id=dev(j),
            device_id_type=MESH,
        )

    def start_gather(i, c):
        gather(lax.rem(me + i, n), me).start()
        return c

    lax.fori_loop(1, n, start_gather, 0)

    def wait_gather(i, c):
        gather(lax.rem(me + n - i, n), lax.rem(me + n - i, n)).wait_recv()
        gather(lax.rem(me + i, n), me).wait_send()
        return c

    lax.fori_loop(1, n, wait_gather, 0)
    o_ref[...] = gath[...]


def axis_sum(x, axis, other, collective_id, summed_rows, source):
    n = lax.axis_size(axis)
    chunks = x.reshape(n, x.shape[0] // n, x.shape[1])
    summed = summed_rows // chunks.shape[1]
    out = pl.pallas_call(
        functools.partial(sum_kernel, axis, other, n, summed, source),
        out_shape=jax.ShapeDtypeStruct(chunks.shape, chunks.dtype),
        in_specs=[pl.BlockSpec(memory_space=pltpu.VMEM)],
        out_specs=pl.BlockSpec(memory_space=pltpu.VMEM),
        scratch_shapes=[
            pltpu.VMEM(chunks.shape, chunks.dtype),
            pltpu.VMEM(chunks.shape, chunks.dtype),
            pltpu.SemaphoreType.DMA((n,)),
            pltpu.SemaphoreType.DMA((n,)),
            pltpu.SemaphoreType.DMA((n,)),
            pltpu.SemaphoreType.DMA((1,)),
            pltpu.SemaphoreType.DMA((n,)),
            pltpu.SemaphoreType.DMA((n,)),
        ],
        compiler_params=pltpu.CompilerParams(
            collective_id=collective_id, has_side_effects=True
        ),
    )(chunks)
    return out.reshape(x.shape)


def group_kernel(stride, size, mode, x_ref, o_ref, buf, send, recv):
    p = lax.axis_index("prow")
    q = lax.axis_index("pcol")
    me = lax.rem(p // stride, size)
    base = p - me * stride

    def dev(k):
        return (base + k * stride, q)

    barrier = pltpu.get_barrier_semaphore()

    def greet(i, c):
        pl.semaphore_signal(barrier, 1, device_id=dev(lax.rem(me + i, size)), device_id_type=MESH)
        return c

    lax.fori_loop(1, size, greet, 0)
    pl.semaphore_wait(barrier, size - 1)

    def copy(k, s):
        src = x_ref.at[k] if mode == "rs" else buf.at[s]
        return pltpu.make_async_remote_copy(
            src_ref=src,
            dst_ref=buf.at[s],
            send_sem=send.at[k],
            recv_sem=recv.at[s],
            device_id=dev(k),
            device_id_type=MESH,
        )

    if mode == "ag":
        buf[me] = x_ref[...]

    def start(i, c):
        copy(lax.rem(me + i, size), me).start()
        return c

    lax.fori_loop(1, size, start, 0)
    if mode == "rs":
        buf[me] = x_ref[me]

    def wait(i, c):
        s = lax.rem(me + size - i, size)
        copy(s, s).wait_recv()
        copy(lax.rem(me + i, size), me).wait_send()
        return c

    lax.fori_loop(1, size, wait, 0)
    if mode == "rs":
        total = buf[0].astype(jnp.float32)
        for s in range(1, size):
            total = total + buf[s].astype(jnp.float32)
        o_ref[...] = total.astype(o_ref.dtype)
    else:
        o_ref[...] = buf[...]


def group_step(x, stride, size, mode, collective_id):
    if mode == "rs":
        chunks = x.reshape(size, x.shape[0] // size, x.shape[1])
        out_shape = chunks.shape[1:]
        buf_shape = chunks.shape
    else:
        chunks = x
        out_shape = (size,) + x.shape
        buf_shape = out_shape
    out = pl.pallas_call(
        functools.partial(group_kernel, stride, size, mode),
        out_shape=jax.ShapeDtypeStruct(out_shape, x.dtype),
        in_specs=[pl.BlockSpec(memory_space=pltpu.VMEM)],
        out_specs=pl.BlockSpec(memory_space=pltpu.VMEM),
        scratch_shapes=[
            pltpu.VMEM(buf_shape, x.dtype),
            pltpu.SemaphoreType.DMA((size,)),
            pltpu.SemaphoreType.DMA((size,)),
        ],
        compiler_params=pltpu.CompilerParams(
            collective_id=collective_id, has_side_effects=True
        ),
    )(chunks)
    if mode == "ag":
        out = out.reshape(size * x.shape[0], x.shape[1])
    return out


def prow_kernel(xd, yd, top, t_ref, o_ref, b1, a2, b2, b3, b4, sends, recvs, tsend, trecv):
    p = lax.axis_index("prow")
    q = lax.axis_index("pcol")
    xi = lax.rem(p, xd)
    yi = p // xd
    xt, yt = top % xd, top // xd

    def xdev(k):
        return (yi * xd + k, q)

    def ydev(k):
        return (k * xd + xi, q)

    barrier = pltpu.get_barrier_semaphore()

    def greet_x(i, c):
        pl.semaphore_signal(barrier, 1, device_id=xdev(lax.rem(xi + i, xd)), device_id_type=MESH)
        return c

    def greet_y(i, c):
        pl.semaphore_signal(barrier, 1, device_id=ydev(lax.rem(yi + i, yd)), device_id_type=MESH)
        return c

    lax.fori_loop(1, xd, greet_x, 0)
    lax.fori_loop(1, yd, greet_y, 0)
    pl.semaphore_wait(barrier, xd + yd - 2)

    def exchange(phase, src, dst, me, size, dev):
        def copy(k, s):
            return pltpu.make_async_remote_copy(
                src_ref=src(k, s),
                dst_ref=dst(s),
                send_sem=sends.at[phase, k],
                recv_sem=recvs.at[phase, s],
                device_id=dev(k),
                device_id_type=MESH,
            )

        def start(i, c):
            copy(lax.rem(me + i, size), me).start()
            return c

        lax.fori_loop(1, size, start, 0)

        def wait(i, c):
            s = lax.rem(me + size - i, size)
            copy(s, s).wait_recv()
            copy(lax.rem(me + i, size), me).wait_send()
            return c

        lax.fori_loop(1, size, wait, 0)

    def total(parts, size):
        acc = parts(0).astype(jnp.float32)
        for s in range(1, size):
            acc = acc + parts(s).astype(jnp.float32)
        return acc

    def top_copy(k):
        return pltpu.make_async_remote_copy(
            src_ref=t_ref.at[k, 1],
            dst_ref=b1.at[xt, 1],
            send_sem=tsend.at[k],
            recv_sem=trecv.at[0],
            device_id=xdev(k),
            device_id_type=MESH,
        )

    @pl.when(p == top)
    def _():
        def start(i, c):
            top_copy(lax.rem(xi + i, xd)).start()
            return c

        lax.fori_loop(1, xd, start, 0)

    exchange(0, lambda k, s: t_ref.at[k, 0], lambda s: b1.at[s, 0], xi, xd, xdev)
    b1[xi, 0] = t_ref[xi, 0]
    top_half = (yd // 2, b1.shape[2] * 2 // yd, b1.shape[3])
    a2[: yd // 2] = total(lambda s: b1[s, 0], xd).astype(a2.dtype).reshape(top_half)

    @pl.when(p == top)
    def _():
        def sent(i, c):
            top_copy(lax.rem(xi + i, xd)).wait_send()
            return c

        lax.fori_loop(1, xd, sent, 0)
        a3 = t_ref[xi, 1]
        a2[yd // 2 :] = a3.reshape(top_half)

    @pl.when((yi == yt) & (p != top))
    def _():
        top_copy(xi).wait_recv()
        a2[yd // 2 :] = b1[xt, 1].reshape(top_half)

    @pl.when(yi != yt)
    def _():
        a2[yd // 2 :] = jnp.zeros(top_half, a2.dtype)

    exchange(1, lambda k, s: a2.at[k], lambda s: b2.at[s], yi, yd, ydev)
    b2[yi] = a2[yi]
    b3[yi] = total(lambda s: b2[s], yd).astype(b3.dtype)
    exchange(2, lambda k, s: b3.at[s], lambda s: b3.at[s], yi, yd, ydev)
    b4[xi] = b3[...].reshape(b4.shape[1:])
    exchange(3, lambda k, s: b4.at[s], lambda s: b4.at[s], xi, xd, xdev)
    o_ref[...] = b4[...]


def prow_sum(picked, top_part, xd, top):
    yd = lax.axis_size("prow") // xd
    rows, cols = picked.shape
    chunks = jnp.stack(
        [picked.reshape(xd, rows // xd, cols), top_part.reshape(xd, rows // xd, cols)], axis=1
    )
    part = 2 * rows // xd // yd
    out = pl.pallas_call(
        functools.partial(prow_kernel, xd, yd, top),
        out_shape=jax.ShapeDtypeStruct((xd, yd, part, cols), picked.dtype),
        in_specs=[pl.BlockSpec(memory_space=pltpu.VMEM)],
        out_specs=pl.BlockSpec(memory_space=pltpu.VMEM),
        scratch_shapes=[
            pltpu.VMEM(chunks.shape, picked.dtype),
            pltpu.VMEM((yd, part, cols), picked.dtype),
            pltpu.VMEM((yd, part, cols), picked.dtype),
            pltpu.VMEM((yd, part, cols), picked.dtype),
            pltpu.VMEM((xd, yd, part, cols), picked.dtype),
            pltpu.SemaphoreType.DMA((4, max(xd, yd))),
            pltpu.SemaphoreType.DMA((4, max(xd, yd))),
            pltpu.SemaphoreType.DMA((xd,)),
            pltpu.SemaphoreType.DMA((1,)),
        ],
        compiler_params=pltpu.CompilerParams(collective_id=10 + top, has_side_effects=True),
    )(chunks)
    out = out.reshape(xd, 2, rows // xd, cols)
    return out[:, 0].reshape(rows, cols), out[:, 1].reshape(rows, cols)


def pcol_kernel(nz, source, x_ref, o_ref, g, p1send, p1recv, p2send, p2recv, p3send, p3recv):
    q = lax.axis_index("pcol")
    p = lax.axis_index("prow")
    nc = lax.axis_size("pcol") // nz
    z = q // nc
    c = lax.rem(q, nc)
    zs, cs = source // nc, source % nc

    def dev(zz, cc):
        return (p, zz * nc + cc)

    barrier = pltpu.get_barrier_semaphore()
    pl.semaphore_signal(barrier, 1, device_id=dev(z, 1 - c), device_id_type=MESH)

    @pl.when(c == cs)
    def _():
        def greet(i, carry):
            pl.semaphore_signal(
                barrier, 1, device_id=dev(lax.rem(z + i, nz), cs), device_id_type=MESH
            )
            return carry

        lax.fori_loop(1, nz, greet, 0)
        pl.semaphore_wait(barrier, nz)

    @pl.when(c != cs)
    def _():
        pl.semaphore_wait(barrier, 1)

    def spread(j):
        return pltpu.make_async_remote_copy(
            src_ref=x_ref.at[j],
            dst_ref=g.at[j],
            send_sem=p1send.at[j],
            recv_sem=p1recv.at[0],
            device_id=dev(j, cs),
            device_id_type=MESH,
        )

    def ring(j, s):
        return pltpu.make_async_remote_copy(
            src_ref=g.at[s],
            dst_ref=g.at[s],
            send_sem=p2send.at[j],
            recv_sem=p2recv.at[s],
            device_id=dev(j, cs),
            device_id_type=MESH,
        )

    def partner(zz):
        return pltpu.make_async_remote_copy(
            src_ref=g,
            dst_ref=g,
            send_sem=p3send.at[0],
            recv_sem=p3recv.at[0],
            device_id=dev(zz, 1 - cs),
            device_id_type=MESH,
        )

    @pl.when(q == source)
    def _():
        def start(i, carry):
            spread(lax.rem(zs + i, nz)).start()
            return carry

        lax.fori_loop(1, nz, start, 0)
        g[zs] = x_ref[zs]

    @pl.when((c == cs) & (z != zs))
    def _():
        spread(z).wait_recv()

    @pl.when(c == cs)
    def _():
        def start(i, carry):
            ring(lax.rem(z + i, nz), z).start()
            return carry

        lax.fori_loop(1, nz, start, 0)

        def wait(i, carry):
            s = lax.rem(z + nz - i, nz)
            ring(s, s).wait_recv()
            ring(lax.rem(z + i, nz), z).wait_send()
            return carry

        lax.fori_loop(1, nz, wait, 0)
        partner(z).start()
        partner(z).wait_send()

    @pl.when(c != cs)
    def _():
        partner(z).wait_recv()

    @pl.when(q == source)
    def _():
        def sent(i, carry):
            spread(lax.rem(zs + i, nz)).wait_send()
            return carry

        lax.fori_loop(1, nz, sent, 0)

    o_ref[...] = g[...]


def pcol_bcast(x, nz, source, collective_id):
    rows, cols = x.shape
    chunks = x.reshape(nz, rows // nz, cols)
    out = pl.pallas_call(
        functools.partial(pcol_kernel, nz, source),
        out_shape=jax.ShapeDtypeStruct(chunks.shape, x.dtype),
        in_specs=[pl.BlockSpec(memory_space=pltpu.VMEM)],
        out_specs=pl.BlockSpec(memory_space=pltpu.VMEM),
        scratch_shapes=[
            pltpu.VMEM(chunks.shape, x.dtype),
            pltpu.SemaphoreType.DMA((nz,)),
            pltpu.SemaphoreType.DMA((1,)),
            pltpu.SemaphoreType.DMA((nz,)),
            pltpu.SemaphoreType.DMA((nz,)),
            pltpu.SemaphoreType.DMA((1,)),
            pltpu.SemaphoreType.DMA((1,)),
        ],
        compiler_params=pltpu.CompilerParams(collective_id=collective_id, has_side_effects=True),
    )(chunks)
    return out.reshape(rows, cols)


def update_kernel(rf_ref, cf_ref, a_ref, l_ref, u_ref, o_ref):
    block = l_ref.shape[1]
    for r in range(a_ref.shape[0] // block):
        rows = slice(r * block, (r + 1) * block)
        rb = rf_ref[r]
        below = (rb & 1) == 1
        in_top = (rb & 2) == 2
        lower = l_ref[rows, :]
        for c in range(a_ref.shape[1] // block):
            cols = slice(c * block, (c + 1) * block)
            cb = cf_ref[c]
            right = (cb & 1) == 1
            in_panel = (cb & 2) == 2
            a = a_ref[rows, cols]
            upper = u_ref[:, cols]
            product = jnp.dot(lower, upper, preferred_element_type=jnp.float32)
            changed = (a.astype(jnp.float32) - product).astype(a.dtype)
            o_ref[rows, cols] = jnp.where(
                below & right,
                changed,
                jnp.where(in_panel & below, lower, jnp.where(in_top & right, upper, a)),
            )


def trailing_update(a, lower, upper, row_flags, col_flags):
    smem = pl.BlockSpec(memory_space=pltpu.SMEM)
    vmem = pl.BlockSpec(memory_space=pltpu.VMEM)
    return pl.pallas_call(
        update_kernel,
        out_shape=jax.ShapeDtypeStruct(a.shape, a.dtype),
        in_specs=[smem, smem, vmem, vmem, vmem],
        out_specs=vmem,
    )(row_flags, col_flags, a, lower, upper)


def local(x_devices, z_chips, matrix, pivots, lower_inverse, upper_inverse):
    row_count = lax.axis_size("prow")
    col_count = lax.axis_size("pcol")
    my_row = lax.axis_index("prow")
    my_col = lax.axis_index("pcol")
    blocks_down, block, blocks_across, _ = matrix.shape
    local_rows = blocks_down * block
    local_cols = blocks_across * block
    current = matrix.reshape(local_rows, local_cols)
    row_place = jnp.arange(local_rows)
    col_place = jnp.arange(local_cols)
    global_rows = (row_place // block * row_count + my_row) * block + row_place % block
    global_cols = (col_place // block * col_count + my_col) * block + col_place % block
    for panel in range(pivots.shape[0]):
        start = panel * block
        chosen = pivots[panel]
        block_row = chosen // block
        is_mine = block_row % row_count == my_row
        local_index = block_row // row_count * block + chosen % block
        safe_index = jnp.where(is_mine, local_index, 0)
        picked = jnp.where(is_mine[:, None], current[safe_index], jnp.zeros((), jnp.bfloat16))
        top_holder = panel % row_count
        top_first = panel // row_count * block
        is_top = my_row == top_holder
        top_local = current[top_first : top_first + block]
        top_part = jnp.where(is_top, top_local, jnp.zeros((), jnp.bfloat16))
        incoming, old_top = prow_sum(picked, top_part, x_devices, top_holder)
        target = jnp.where(is_mine, local_index, local_rows)
        current = current.at[target].set(old_top, mode="drop")
        top_now = current[top_first : top_first + block]
        current = current.at[top_first : top_first + block].set(
            jnp.where(is_top, incoming, top_now)
        )
        panel_holder = panel % col_count
        panel_first = panel // col_count * block
        panel_cols = current[:, panel_first : panel_first + block]
        factor = jnp.dot(
            panel_cols, upper_inverse[panel], preferred_element_type=jnp.float32
        ).astype(jnp.bfloat16)
        is_panel = my_col == panel_holder
        factor = jnp.where(is_panel, factor, jnp.zeros((), jnp.bfloat16))
        lower = pcol_bcast(factor, z_chips, panel_holder, 20 + panel)
        upper = jnp.dot(
            lower_inverse[panel], incoming, preferred_element_type=jnp.float32
        ).astype(jnp.bfloat16)
        row_mask = global_rows >= start + block
        col_mask = global_cols >= start + block
        row_blocks = row_place[::block] // block
        col_blocks = col_place[::block] // block
        below = (row_blocks * row_count + my_row >= panel + 1).astype(jnp.int32)
        right = (col_blocks * col_count + my_col >= panel + 1).astype(jnp.int32)
        in_top = (is_top & (row_blocks == top_first // block)).astype(jnp.int32)
        in_panel = (is_panel & (col_blocks == panel_first // block)).astype(jnp.int32)
        current = trailing_update(current, lower, upper, below + 2 * in_top, right + 2 * in_panel)
    return current.reshape(matrix.shape)


def solution(mesh):
    x_devices = len({d.coords[0] for d in mesh.devices[:, 0]})
    z_chips = len({d.coords[2] for d in mesh.devices[0, :]})
    in_specs = (P(None, "prow", None, "pcol"), P(), P(), P())
    out_specs = P(None, "prow", None, "pcol")
    return jax.shard_map(functools.partial(local, x_devices, z_chips), mesh=mesh, in_specs=in_specs, out_specs=out_specs, check_vma=False)
```

```python
import functools

import jax
import jax.numpy as jnp
from jax import lax
from jax.experimental import pallas as pl
from jax.experimental.pallas import tpu as pltpu
from jax.sharding import PartitionSpec as P

MESH = pl.DeviceIdType.MESH


def sum_kernel(axis, other, n, summed, source, x_ref, o_ref, recv, gath, ssend, srecv,
               bsend, brecv, gsend, grecv):
    me = lax.axis_index(axis)
    them = lax.axis_index(other)

    def dev(j):
        return (j, them) if axis == "prow" else (them, j)

    barrier = pltpu.get_barrier_semaphore()

    def greet(i, c):
        j = lax.rem(me + i, n)
        pl.semaphore_signal(barrier, 1, device_id=dev(j), device_id_type=MESH)
        return c

    lax.fori_loop(1, n, greet, 0)
    pl.semaphore_wait(barrier, n - 1)

    def scatter(j, s):
        return pltpu.make_async_remote_copy(
            src_ref=x_ref.at[j],
            dst_ref=recv.at[s],
            send_sem=ssend.at[j],
            recv_sem=srecv.at[s],
            device_id=dev(j),
            device_id_type=MESH,
        )

    def spread(j):
        return pltpu.make_async_remote_copy(
            src_ref=x_ref.at[j],
            dst_ref=gath.at[j],
            send_sem=bsend.at[j],
            recv_sem=brecv.at[0],
            device_id=dev(j),
            device_id_type=MESH,
        )

    if summed > 0:
        def start_scatter(i, c):
            j = lax.rem(me + i, n)

            @pl.when(j < summed)
            def _():
                scatter(j, me).start()

            return c

        lax.fori_loop(1, n, start_scatter, 0)

    if summed < n:
        @pl.when(me == source)
        def _():
            def start_spread(i, c):
                j = lax.rem(me + i, n)

                @pl.when(j >= summed)
                def _():
                    spread(j).start()

                return c

            lax.fori_loop(1, n, start_spread, 0)
            if source >= summed:
                gath[source] = x_ref[source]

    if summed > 0:
        @pl.when(me < summed)
        def _():
            recv[me] = x_ref[me]

            def wait_scatter(i, c):
                s = lax.rem(me + n - i, n)
                scatter(s, s).wait_recv()
                return c

            lax.fori_loop(1, n, wait_scatter, 0)
            total = recv[0].astype(jnp.float32)
            for s in range(1, n):
                total = total + recv[s].astype(jnp.float32)
            gath[me] = total.astype(gath.dtype)

        def wait_scatter_sent(i, c):
            j = lax.rem(me + i, n)

            @pl.when(j < summed)
            def _():
                scatter(j, me).wait_send()

            return c

        lax.fori_loop(1, n, wait_scatter_sent, 0)

    if summed < n:
        @pl.when((me >= summed) & (me != source))
        def _():
            spread(me).wait_recv()

        @pl.when(me == source)
        def _():
            def wait_spread_sent(i, c):
                j = lax.rem(me + i, n)

                @pl.when(j >= summed)
                def _():
                    spread(j).wait_send()

                return c

            lax.fori_loop(1, n, wait_spread_sent, 0)

    def gather(j, s):
        return pltpu.make_async_remote_copy(
            src_ref=gath.at[s],
            dst_ref=gath.at[s],
            send_sem=gsend.at[j],
            recv_sem=grecv.at[s],
            device_id=dev(j),
            device_id_type=MESH,
        )

    def start_gather(i, c):
        gather(lax.rem(me + i, n), me).start()
        return c

    lax.fori_loop(1, n, start_gather, 0)

    def wait_gather(i, c):
        gather(lax.rem(me + n - i, n), lax.rem(me + n - i, n)).wait_recv()
        gather(lax.rem(me + i, n), me).wait_send()
        return c

    lax.fori_loop(1, n, wait_gather, 0)
    o_ref[...] = gath[...]


def axis_sum(x, axis, other, collective_id, summed_rows, source):
    n = lax.axis_size(axis)
    chunks = x.reshape(n, x.shape[0] // n, x.shape[1])
    summed = summed_rows // chunks.shape[1]
    out = pl.pallas_call(
        functools.partial(sum_kernel, axis, other, n, summed, source),
        out_shape=jax.ShapeDtypeStruct(chunks.shape, chunks.dtype),
        in_specs=[pl.BlockSpec(memory_space=pltpu.VMEM)],
        out_specs=pl.BlockSpec(memory_space=pltpu.VMEM),
        scratch_shapes=[
            pltpu.VMEM(chunks.shape, chunks.dtype),
            pltpu.VMEM(chunks.shape, chunks.dtype),
            pltpu.SemaphoreType.DMA((n,)),
            pltpu.SemaphoreType.DMA((n,)),
            pltpu.SemaphoreType.DMA((n,)),
            pltpu.SemaphoreType.DMA((1,)),
            pltpu.SemaphoreType.DMA((n,)),
            pltpu.SemaphoreType.DMA((n,)),
        ],
        compiler_params=pltpu.CompilerParams(
            collective_id=collective_id, has_side_effects=True
        ),
    )(chunks)
    return out.reshape(x.shape)


def group_kernel(stride, size, mode, x_ref, o_ref, buf, send, recv):
    p = lax.axis_index("prow")
    q = lax.axis_index("pcol")
    me = lax.rem(p // stride, size)
    base = p - me * stride

    def dev(k):
        return (base + k * stride, q)

    barrier = pltpu.get_barrier_semaphore()

    def greet(i, c):
        pl.semaphore_signal(barrier, 1, device_id=dev(lax.rem(me + i, size)), device_id_type=MESH)
        return c

    lax.fori_loop(1, size, greet, 0)
    pl.semaphore_wait(barrier, size - 1)

    def copy(k, s):
        src = x_ref.at[k] if mode == "rs" else buf.at[s]
        return pltpu.make_async_remote_copy(
            src_ref=src,
            dst_ref=buf.at[s],
            send_sem=send.at[k],
            recv_sem=recv.at[s],
            device_id=dev(k),
            device_id_type=MESH,
        )

    if mode == "ag":
        buf[me] = x_ref[...]

    def start(i, c):
        copy(lax.rem(me + i, size), me).start()
        return c

    lax.fori_loop(1, size, start, 0)
    if mode == "rs":
        buf[me] = x_ref[me]

    def wait(i, c):
        s = lax.rem(me + size - i, size)
        copy(s, s).wait_recv()
        copy(lax.rem(me + i, size), me).wait_send()
        return c

    lax.fori_loop(1, size, wait, 0)
    if mode == "rs":
        total = buf[0].astype(jnp.float32)
        for s in range(1, size):
            total = total + buf[s].astype(jnp.float32)
        o_ref[...] = total.astype(o_ref.dtype)
    else:
        o_ref[...] = buf[...]


def group_step(x, stride, size, mode, collective_id):
    if mode == "rs":
        chunks = x.reshape(size, x.shape[0] // size, x.shape[1])
        out_shape = chunks.shape[1:]
        buf_shape = chunks.shape
    else:
        chunks = x
        out_shape = (size,) + x.shape
        buf_shape = out_shape
    out = pl.pallas_call(
        functools.partial(group_kernel, stride, size, mode),
        out_shape=jax.ShapeDtypeStruct(out_shape, x.dtype),
        in_specs=[pl.BlockSpec(memory_space=pltpu.VMEM)],
        out_specs=pl.BlockSpec(memory_space=pltpu.VMEM),
        scratch_shapes=[
            pltpu.VMEM(buf_shape, x.dtype),
            pltpu.SemaphoreType.DMA((size,)),
            pltpu.SemaphoreType.DMA((size,)),
        ],
        compiler_params=pltpu.CompilerParams(
            collective_id=collective_id, has_side_effects=True
        ),
    )(chunks)
    if mode == "ag":
        out = out.reshape(size * x.shape[0], x.shape[1])
    return out


def prow_kernel(xd, yd, top, t_ref, o_ref, b1, a2, b2, b3, b4, sends, recvs, tsend, trecv):
    p = lax.axis_index("prow")
    q = lax.axis_index("pcol")
    xi = lax.rem(p, xd)
    yi = p // xd
    xt, yt = top % xd, top // xd

    def xdev(k):
        return (yi * xd + k, q)

    def ydev(k):
        return (k * xd + xi, q)

    barrier = pltpu.get_barrier_semaphore()

    def greet_x(i, c):
        pl.semaphore_signal(barrier, 1, device_id=xdev(lax.rem(xi + i, xd)), device_id_type=MESH)
        return c

    def greet_y(i, c):
        pl.semaphore_signal(barrier, 1, device_id=ydev(lax.rem(yi + i, yd)), device_id_type=MESH)
        return c

    lax.fori_loop(1, xd, greet_x, 0)
    lax.fori_loop(1, yd, greet_y, 0)
    pl.semaphore_wait(barrier, xd + yd - 2)

    def exchange(phase, src, dst, me, size, dev):
        def copy(k, s):
            return pltpu.make_async_remote_copy(
                src_ref=src(k, s),
                dst_ref=dst(s),
                send_sem=sends.at[phase, k],
                recv_sem=recvs.at[phase, s],
                device_id=dev(k),
                device_id_type=MESH,
            )

        def start(i, c):
            copy(lax.rem(me + i, size), me).start()
            return c

        lax.fori_loop(1, size, start, 0)

        def wait(i, c):
            s = lax.rem(me + size - i, size)
            copy(s, s).wait_recv()
            copy(lax.rem(me + i, size), me).wait_send()
            return c

        lax.fori_loop(1, size, wait, 0)

    def total(parts, size):
        acc = parts(0).astype(jnp.float32)
        for s in range(1, size):
            acc = acc + parts(s).astype(jnp.float32)
        return acc

    def top_copy(k):
        return pltpu.make_async_remote_copy(
            src_ref=t_ref.at[k, 1],
            dst_ref=b1.at[xt, 1],
            send_sem=tsend.at[k],
            recv_sem=trecv.at[0],
            device_id=xdev(k),
            device_id_type=MESH,
        )

    @pl.when(p == top)
    def _():
        def start(i, c):
            top_copy(lax.rem(xi + i, xd)).start()
            return c

        lax.fori_loop(1, xd, start, 0)

    exchange(0, lambda k, s: t_ref.at[k, 0], lambda s: b1.at[s, 0], xi, xd, xdev)
    b1[xi, 0] = t_ref[xi, 0]
    top_half = (yd // 2, b1.shape[2] * 2 // yd, b1.shape[3])
    a2[: yd // 2] = total(lambda s: b1[s, 0], xd).astype(a2.dtype).reshape(top_half)

    @pl.when(p == top)
    def _():
        def sent(i, c):
            top_copy(lax.rem(xi + i, xd)).wait_send()
            return c

        lax.fori_loop(1, xd, sent, 0)
        a3 = t_ref[xi, 1]
        a2[yd // 2 :] = a3.reshape(top_half)

    @pl.when((yi == yt) & (p != top))
    def _():
        top_copy(xi).wait_recv()
        a2[yd // 2 :] = b1[xt, 1].reshape(top_half)

    @pl.when(yi != yt)
    def _():
        a2[yd // 2 :] = jnp.zeros(top_half, a2.dtype)

    exchange(1, lambda k, s: a2.at[k], lambda s: b2.at[s], yi, yd, ydev)
    b2[yi] = a2[yi]
    b3[yi] = total(lambda s: b2[s], yd).astype(b3.dtype)
    exchange(2, lambda k, s: b3.at[s], lambda s: b3.at[s], yi, yd, ydev)
    b4[xi] = b3[...].reshape(b4.shape[1:])
    exchange(3, lambda k, s: b4.at[s], lambda s: b4.at[s], xi, xd, xdev)
    o_ref[...] = b4[...]


def prow_sum(picked, top_part, xd, top):
    yd = lax.axis_size("prow") // xd
    rows, cols = picked.shape
    chunks = jnp.stack(
        [picked.reshape(xd, rows // xd, cols), top_part.reshape(xd, rows // xd, cols)], axis=1
    )
    part = 2 * rows // xd // yd
    out = pl.pallas_call(
        functools.partial(prow_kernel, xd, yd, top),
        out_shape=jax.ShapeDtypeStruct((xd, yd, part, cols), picked.dtype),
        in_specs=[pl.BlockSpec(memory_space=pltpu.VMEM)],
        out_specs=pl.BlockSpec(memory_space=pltpu.VMEM),
        scratch_shapes=[
            pltpu.VMEM(chunks.shape, picked.dtype),
            pltpu.VMEM((yd, part, cols), picked.dtype),
            pltpu.VMEM((yd, part, cols), picked.dtype),
            pltpu.VMEM((yd, part, cols), picked.dtype),
            pltpu.VMEM((xd, yd, part, cols), picked.dtype),
            pltpu.SemaphoreType.DMA((4, max(xd, yd))),
            pltpu.SemaphoreType.DMA((4, max(xd, yd))),
            pltpu.SemaphoreType.DMA((xd,)),
            pltpu.SemaphoreType.DMA((1,)),
        ],
        compiler_params=pltpu.CompilerParams(collective_id=10 + top, has_side_effects=True),
    )(chunks)
    out = out.reshape(xd, 2, rows // xd, cols)
    return out[:, 0].reshape(rows, cols), out[:, 1].reshape(rows, cols)


def pcol_kernel(nz, source, x_ref, o_ref, g, p1send, p1recv, p2send, p2recv, p3send, p3recv):
    q = lax.axis_index("pcol")
    p = lax.axis_index("prow")
    nc = lax.axis_size("pcol") // nz
    z = q // nc
    c = lax.rem(q, nc)
    zs, cs = source // nc, source % nc

    def dev(zz, cc):
        return (p, zz * nc + cc)

    barrier = pltpu.get_barrier_semaphore()
    pl.semaphore_signal(barrier, 1, device_id=dev(z, 1 - c), device_id_type=MESH)

    @pl.when(c == cs)
    def _():
        def greet(i, carry):
            pl.semaphore_signal(
                barrier, 1, device_id=dev(lax.rem(z + i, nz), cs), device_id_type=MESH
            )
            return carry

        lax.fori_loop(1, nz, greet, 0)
        pl.semaphore_wait(barrier, nz)

    @pl.when(c != cs)
    def _():
        pl.semaphore_wait(barrier, 1)

    def spread(j):
        return pltpu.make_async_remote_copy(
            src_ref=x_ref.at[j],
            dst_ref=g.at[j],
            send_sem=p1send.at[j],
            recv_sem=p1recv.at[0],
            device_id=dev(j, cs),
            device_id_type=MESH,
        )

    def ring(j, s):
        return pltpu.make_async_remote_copy(
            src_ref=g.at[s],
            dst_ref=g.at[s],
            send_sem=p2send.at[j],
            recv_sem=p2recv.at[s],
            device_id=dev(j, cs),
            device_id_type=MESH,
        )

    def partner(zz):
        return pltpu.make_async_remote_copy(
            src_ref=g,
            dst_ref=g,
            send_sem=p3send.at[0],
            recv_sem=p3recv.at[0],
            device_id=dev(zz, 1 - cs),
            device_id_type=MESH,
        )

    @pl.when(q == source)
    def _():
        def start(i, carry):
            spread(lax.rem(zs + i, nz)).start()
            return carry

        lax.fori_loop(1, nz, start, 0)
        g[zs] = x_ref[zs]

    @pl.when((c == cs) & (z != zs))
    def _():
        spread(z).wait_recv()

    @pl.when(c == cs)
    def _():
        def start(i, carry):
            ring(lax.rem(z + i, nz), z).start()
            return carry

        lax.fori_loop(1, nz, start, 0)

        def wait(i, carry):
            s = lax.rem(z + nz - i, nz)
            ring(s, s).wait_recv()
            ring(lax.rem(z + i, nz), z).wait_send()
            return carry

        lax.fori_loop(1, nz, wait, 0)
        partner(z).start()
        partner(z).wait_send()

    @pl.when(c != cs)
    def _():
        partner(z).wait_recv()

    @pl.when(q == source)
    def _():
        def sent(i, carry):
            spread(lax.rem(zs + i, nz)).wait_send()
            return carry

        lax.fori_loop(1, nz, sent, 0)

    o_ref[...] = g[...]


def pcol_bcast(x, nz, source, collective_id):
    rows, cols = x.shape
    chunks = x.reshape(nz, rows // nz, cols)
    out = pl.pallas_call(
        functools.partial(pcol_kernel, nz, source),
        out_shape=jax.ShapeDtypeStruct(chunks.shape, x.dtype),
        in_specs=[pl.BlockSpec(memory_space=pltpu.VMEM)],
        out_specs=pl.BlockSpec(memory_space=pltpu.VMEM),
        scratch_shapes=[
            pltpu.VMEM(chunks.shape, x.dtype),
            pltpu.SemaphoreType.DMA((nz,)),
            pltpu.SemaphoreType.DMA((1,)),
            pltpu.SemaphoreType.DMA((nz,)),
            pltpu.SemaphoreType.DMA((nz,)),
            pltpu.SemaphoreType.DMA((1,)),
            pltpu.SemaphoreType.DMA((1,)),
        ],
        compiler_params=pltpu.CompilerParams(collective_id=collective_id, has_side_effects=True),
    )(chunks)
    return out.reshape(rows, cols)


def update_kernel(four, rf_ref, cf_ref, a_ref, l_ref, u_ref, o_ref):
    block = l_ref.shape[1]
    for r in range(a_ref.shape[0] // block):
        rows = slice(r * block, (r + 1) * block)
        rb = rf_ref[r]
        below = (rb & 1) == 1
        in_top = (rb & 2) == 2
        lower = l_ref[rows, :]
        for c in range(a_ref.shape[1] // block):
            cols = slice(c * block, (c + 1) * block)
            cb = cf_ref[c]
            right = (cb & 1) == 1
            in_panel = (cb & 2) == 2
            a = a_ref[rows, cols]
            upper = u_ref[:, cols]
            product = jnp.dot(lower, upper, preferred_element_type=jnp.float32)
            changed = (a.astype(jnp.float32) - product).astype(a.dtype)
            result = jnp.where(
                below & right,
                changed,
                jnp.where(in_panel & below, lower, jnp.where(in_top & right, upper, a)),
            )
            if four:
                o_ref[r, :, c, :] = result
            else:
                o_ref[rows, cols] = result


def trailing_update(a, lower, upper, row_flags, col_flags, out_shape=None):
    smem = pl.BlockSpec(memory_space=pltpu.SMEM)
    vmem = pl.BlockSpec(memory_space=pltpu.VMEM)
    return pl.pallas_call(
        functools.partial(update_kernel, out_shape is not None),
        out_shape=jax.ShapeDtypeStruct(out_shape or a.shape, a.dtype),
        in_specs=[smem, smem, vmem, vmem, vmem],
        out_specs=vmem,
    )(row_flags, col_flags, a, lower, upper)


def local(x_devices, z_chips, matrix, pivots, lower_inverse, upper_inverse):
    row_count = lax.axis_size("prow")
    col_count = lax.axis_size("pcol")
    my_row = lax.axis_index("prow")
    my_col = lax.axis_index("pcol")
    blocks_down, block, blocks_across, _ = matrix.shape
    local_rows = blocks_down * block
    local_cols = blocks_across * block
    current = matrix.reshape(local_rows, local_cols)
    row_place = jnp.arange(local_rows)
    col_place = jnp.arange(local_cols)
    global_rows = (row_place // block * row_count + my_row) * block + row_place % block
    global_cols = (col_place // block * col_count + my_col) * block + col_place % block
    for panel in range(pivots.shape[0]):
        start = panel * block
        chosen = pivots[panel]
        block_row = chosen // block
        is_mine = block_row % row_count == my_row
        local_index = block_row // row_count * block + chosen % block
        safe_index = jnp.where(is_mine, local_index, 0)
        picked = jnp.where(is_mine[:, None], current[safe_index], jnp.zeros((), jnp.bfloat16))
        top_holder = panel % row_count
        top_first = panel // row_count * block
        is_top = my_row == top_holder
        top_local = current[top_first : top_first + block]
        top_part = jnp.where(is_top, top_local, jnp.zeros((), jnp.bfloat16))
        incoming, old_top = prow_sum(picked, top_part, x_devices, top_holder)
        target = jnp.where(is_mine, local_index, local_rows)
        current = current.at[target].set(old_top, mode="drop")
        top_now = current[top_first : top_first + block]
        current = current.at[top_first : top_first + block].set(
            jnp.where(is_top, incoming, top_now)
        )
        panel_holder = panel % col_count
        panel_first = panel // col_count * block
        panel_cols = current[:, panel_first : panel_first + block]
        factor = jnp.dot(
            panel_cols, upper_inverse[panel], preferred_element_type=jnp.float32
        ).astype(jnp.bfloat16)
        is_panel = my_col == panel_holder
        factor = jnp.where(is_panel, factor, jnp.zeros((), jnp.bfloat16))
        lower = pcol_bcast(factor, z_chips, panel_holder, 20 + panel)
        upper = jnp.dot(
            lower_inverse[panel], incoming, preferred_element_type=jnp.float32
        ).astype(jnp.bfloat16)
        row_mask = global_rows >= start + block
        col_mask = global_cols >= start + block
        row_blocks = row_place[::block] // block
        col_blocks = col_place[::block] // block
        below = (row_blocks * row_count + my_row >= panel + 1).astype(jnp.int32)
        right = (col_blocks * col_count + my_col >= panel + 1).astype(jnp.int32)
        in_top = (is_top & (row_blocks == top_first // block)).astype(jnp.int32)
        in_panel = (is_panel & (col_blocks == panel_first // block)).astype(jnp.int32)
        last = panel == pivots.shape[0] - 1
        current = trailing_update(
            current, lower, upper, below + 2 * in_top, right + 2 * in_panel,
            matrix.shape if last else None,
        )
    return current.reshape(matrix.shape)


def solution(mesh):
    x_devices = len({d.coords[0] for d in mesh.devices[:, 0]})
    z_chips = len({d.coords[2] for d in mesh.devices[0, :]})
    in_specs = (P(None, "prow", None, "pcol"), P(), P(), P())
    out_specs = P(None, "prow", None, "pcol")
    return jax.shard_map(functools.partial(local, x_devices, z_chips), mesh=mesh, in_specs=in_specs, out_specs=out_specs, check_vma=False)
```

```python
import functools

import jax
import jax.numpy as jnp
from jax import lax
from jax.experimental import pallas as pl
from jax.experimental.pallas import tpu as pltpu
from jax.sharding import PartitionSpec as P

MESH = pl.DeviceIdType.MESH


def sum_kernel(axis, other, n, summed, source, x_ref, o_ref, recv, gath, ssend, srecv,
               bsend, brecv, gsend, grecv):
    me = lax.axis_index(axis)
    them = lax.axis_index(other)

    def dev(j):
        return (j, them) if axis == "prow" else (them, j)

    barrier = pltpu.get_barrier_semaphore()

    def greet(i, c):
        j = lax.rem(me + i, n)
        pl.semaphore_signal(barrier, 1, device_id=dev(j), device_id_type=MESH)
        return c

    lax.fori_loop(1, n, greet, 0)
    pl.semaphore_wait(barrier, n - 1)

    def scatter(j, s):
        return pltpu.make_async_remote_copy(
            src_ref=x_ref.at[j],
            dst_ref=recv.at[s],
            send_sem=ssend.at[j],
            recv_sem=srecv.at[s],
            device_id=dev(j),
            device_id_type=MESH,
        )

    def spread(j):
        return pltpu.make_async_remote_copy(
            src_ref=x_ref.at[j],
            dst_ref=gath.at[j],
            send_sem=bsend.at[j],
            recv_sem=brecv.at[0],
            device_id=dev(j),
            device_id_type=MESH,
        )

    if summed > 0:
        def start_scatter(i, c):
            j = lax.rem(me + i, n)

            @pl.when(j < summed)
            def _():
                scatter(j, me).start()

            return c

        lax.fori_loop(1, n, start_scatter, 0)

    if summed < n:
        @pl.when(me == source)
        def _():
            def start_spread(i, c):
                j = lax.rem(me + i, n)

                @pl.when(j >= summed)
                def _():
                    spread(j).start()

                return c

            lax.fori_loop(1, n, start_spread, 0)
            if source >= summed:
                gath[source] = x_ref[source]

    if summed > 0:
        @pl.when(me < summed)
        def _():
            recv[me] = x_ref[me]

            def wait_scatter(i, c):
                s = lax.rem(me + n - i, n)
                scatter(s, s).wait_recv()
                return c

            lax.fori_loop(1, n, wait_scatter, 0)
            total = recv[0].astype(jnp.float32)
            for s in range(1, n):
                total = total + recv[s].astype(jnp.float32)
            gath[me] = total.astype(gath.dtype)

        def wait_scatter_sent(i, c):
            j = lax.rem(me + i, n)

            @pl.when(j < summed)
            def _():
                scatter(j, me).wait_send()

            return c

        lax.fori_loop(1, n, wait_scatter_sent, 0)

    if summed < n:
        @pl.when((me >= summed) & (me != source))
        def _():
            spread(me).wait_recv()

        @pl.when(me == source)
        def _():
            def wait_spread_sent(i, c):
                j = lax.rem(me + i, n)

                @pl.when(j >= summed)
                def _():
                    spread(j).wait_send()

                return c

            lax.fori_loop(1, n, wait_spread_sent, 0)

    def gather(j, s):
        return pltpu.make_async_remote_copy(
            src_ref=gath.at[s],
            dst_ref=gath.at[s],
            send_sem=gsend.at[j],
            recv_sem=grecv.at[s],
            device_id=dev(j),
            device_id_type=MESH,
        )

    def start_gather(i, c):
        gather(lax.rem(me + i, n), me).start()
        return c

    lax.fori_loop(1, n, start_gather, 0)

    def wait_gather(i, c):
        gather(lax.rem(me + n - i, n), lax.rem(me + n - i, n)).wait_recv()
        gather(lax.rem(me + i, n), me).wait_send()
        return c

    lax.fori_loop(1, n, wait_gather, 0)
    o_ref[...] = gath[...]


def axis_sum(x, axis, other, collective_id, summed_rows, source):
    n = lax.axis_size(axis)
    chunks = x.reshape(n, x.shape[0] // n, x.shape[1])
    summed = summed_rows // chunks.shape[1]
    out = pl.pallas_call(
        functools.partial(sum_kernel, axis, other, n, summed, source),
        out_shape=jax.ShapeDtypeStruct(chunks.shape, chunks.dtype),
        in_specs=[pl.BlockSpec(memory_space=pltpu.VMEM)],
        out_specs=pl.BlockSpec(memory_space=pltpu.VMEM),
        scratch_shapes=[
            pltpu.VMEM(chunks.shape, chunks.dtype),
            pltpu.VMEM(chunks.shape, chunks.dtype),
            pltpu.SemaphoreType.DMA((n,)),
            pltpu.SemaphoreType.DMA((n,)),
            pltpu.SemaphoreType.DMA((n,)),
            pltpu.SemaphoreType.DMA((1,)),
            pltpu.SemaphoreType.DMA((n,)),
            pltpu.SemaphoreType.DMA((n,)),
        ],
        compiler_params=pltpu.CompilerParams(
            collective_id=collective_id, has_side_effects=True
        ),
    )(chunks)
    return out.reshape(x.shape)


def group_kernel(stride, size, mode, x_ref, o_ref, buf, send, recv):
    p = lax.axis_index("prow")
    q = lax.axis_index("pcol")
    me = lax.rem(p // stride, size)
    base = p - me * stride

    def dev(k):
        return (base + k * stride, q)

    barrier = pltpu.get_barrier_semaphore()

    def greet(i, c):
        pl.semaphore_signal(barrier, 1, device_id=dev(lax.rem(me + i, size)), device_id_type=MESH)
        return c

    lax.fori_loop(1, size, greet, 0)
    pl.semaphore_wait(barrier, size - 1)

    def copy(k, s):
        src = x_ref.at[k] if mode == "rs" else buf.at[s]
        return pltpu.make_async_remote_copy(
            src_ref=src,
            dst_ref=buf.at[s],
            send_sem=send.at[k],
            recv_sem=recv.at[s],
            device_id=dev(k),
            device_id_type=MESH,
        )

    if mode == "ag":
        buf[me] = x_ref[...]

    def start(i, c):
        copy(lax.rem(me + i, size), me).start()
        return c

    lax.fori_loop(1, size, start, 0)
    if mode == "rs":
        buf[me] = x_ref[me]

    def wait(i, c):
        s = lax.rem(me + size - i, size)
        copy(s, s).wait_recv()
        copy(lax.rem(me + i, size), me).wait_send()
        return c

    lax.fori_loop(1, size, wait, 0)
    if mode == "rs":
        total = buf[0].astype(jnp.float32)
        for s in range(1, size):
            total = total + buf[s].astype(jnp.float32)
        o_ref[...] = total.astype(o_ref.dtype)
    else:
        o_ref[...] = buf[...]


def group_step(x, stride, size, mode, collective_id):
    if mode == "rs":
        chunks = x.reshape(size, x.shape[0] // size, x.shape[1])
        out_shape = chunks.shape[1:]
        buf_shape = chunks.shape
    else:
        chunks = x
        out_shape = (size,) + x.shape
        buf_shape = out_shape
    out = pl.pallas_call(
        functools.partial(group_kernel, stride, size, mode),
        out_shape=jax.ShapeDtypeStruct(out_shape, x.dtype),
        in_specs=[pl.BlockSpec(memory_space=pltpu.VMEM)],
        out_specs=pl.BlockSpec(memory_space=pltpu.VMEM),
        scratch_shapes=[
            pltpu.VMEM(buf_shape, x.dtype),
            pltpu.SemaphoreType.DMA((size,)),
            pltpu.SemaphoreType.DMA((size,)),
        ],
        compiler_params=pltpu.CompilerParams(
            collective_id=collective_id, has_side_effects=True
        ),
    )(chunks)
    if mode == "ag":
        out = out.reshape(size * x.shape[0], x.shape[1])
    return out


def prow_kernel(xd, yd, top, t_ref, o_ref, b1, a2, b2, b3, b4, sends, recvs, tsend, trecv):
    p = lax.axis_index("prow")
    q = lax.axis_index("pcol")
    xi = lax.rem(p, xd)
    yi = p // xd
    xt, yt = top % xd, top // xd

    def xdev(k):
        return (yi * xd + k, q)

    def ydev(k):
        return (k * xd + xi, q)

    barrier = pltpu.get_barrier_semaphore()

    def greet_x(i, c):
        pl.semaphore_signal(barrier, 1, device_id=xdev(lax.rem(xi + i, xd)), device_id_type=MESH)
        return c

    def greet_y(i, c):
        pl.semaphore_signal(barrier, 1, device_id=ydev(lax.rem(yi + i, yd)), device_id_type=MESH)
        return c

    lax.fori_loop(1, xd, greet_x, 0)
    lax.fori_loop(1, yd, greet_y, 0)
    pl.semaphore_wait(barrier, xd + yd - 2)

    def exchange(phase, src, dst, me, size, dev):
        def copy(k, s):
            return pltpu.make_async_remote_copy(
                src_ref=src(k, s),
                dst_ref=dst(s),
                send_sem=sends.at[phase, k],
                recv_sem=recvs.at[phase, s],
                device_id=dev(k),
                device_id_type=MESH,
            )

        def start(i, c):
            copy(lax.rem(me + i, size), me).start()
            return c

        lax.fori_loop(1, size, start, 0)

        def wait(i, c):
            s = lax.rem(me + size - i, size)
            copy(s, s).wait_recv()
            copy(lax.rem(me + i, size), me).wait_send()
            return c

        lax.fori_loop(1, size, wait, 0)

    def total(parts, size):
        acc = parts(0).astype(jnp.float32)
        for s in range(1, size):
            acc = acc + parts(s).astype(jnp.float32)
        return acc

    def top_copy(k):
        return pltpu.make_async_remote_copy(
            src_ref=t_ref.at[k, 1],
            dst_ref=b1.at[xt, 1],
            send_sem=tsend.at[k],
            recv_sem=trecv.at[0],
            device_id=xdev(k),
            device_id_type=MESH,
        )

    @pl.when(p == top)
    def _():
        def start(i, c):
            top_copy(lax.rem(xi + i, xd)).start()
            return c

        lax.fori_loop(1, xd, start, 0)

    exchange(0, lambda k, s: t_ref.at[k, 0], lambda s: b1.at[s, 0], xi, xd, xdev)
    b1[xi, 0] = t_ref[xi, 0]
    top_half = (yd // 2, b1.shape[2] * 2 // yd, b1.shape[3])
    a2[: yd // 2] = total(lambda s: b1[s, 0], xd).astype(a2.dtype).reshape(top_half)

    @pl.when(p == top)
    def _():
        def sent(i, c):
            top_copy(lax.rem(xi + i, xd)).wait_send()
            return c

        lax.fori_loop(1, xd, sent, 0)
        a3 = t_ref[xi, 1]
        a2[yd // 2 :] = a3.reshape(top_half)

    @pl.when((yi == yt) & (p != top))
    def _():
        top_copy(xi).wait_recv()
        a2[yd // 2 :] = b1[xt, 1].reshape(top_half)

    @pl.when(yi != yt)
    def _():
        a2[yd // 2 :] = jnp.zeros(top_half, a2.dtype)

    exchange(1, lambda k, s: a2.at[k], lambda s: b2.at[s], yi, yd, ydev)
    b2[yi] = a2[yi]
    b3[yi] = total(lambda s: b2[s], yd).astype(b3.dtype)
    exchange(2, lambda k, s: b3.at[s], lambda s: b3.at[s], yi, yd, ydev)
    b4[xi] = b3[...].reshape(b4.shape[1:])
    exchange(3, lambda k, s: b4.at[s], lambda s: b4.at[s], xi, xd, xdev)
    o_ref[...] = b4[...]


def prow_sum(picked, top_part, xd, top):
    yd = lax.axis_size("prow") // xd
    rows, cols = picked.shape
    chunks = jnp.stack(
        [picked.reshape(xd, rows // xd, cols), top_part.reshape(xd, rows // xd, cols)], axis=1
    )
    part = 2 * rows // xd // yd
    out = pl.pallas_call(
        functools.partial(prow_kernel, xd, yd, top),
        out_shape=jax.ShapeDtypeStruct((xd, yd, part, cols), picked.dtype),
        in_specs=[pl.BlockSpec(memory_space=pltpu.VMEM)],
        out_specs=pl.BlockSpec(memory_space=pltpu.VMEM),
        scratch_shapes=[
            pltpu.VMEM(chunks.shape, picked.dtype),
            pltpu.VMEM((yd, part, cols), picked.dtype),
            pltpu.VMEM((yd, part, cols), picked.dtype),
            pltpu.VMEM((yd, part, cols), picked.dtype),
            pltpu.VMEM((xd, yd, part, cols), picked.dtype),
            pltpu.SemaphoreType.DMA((4, max(xd, yd))),
            pltpu.SemaphoreType.DMA((4, max(xd, yd))),
            pltpu.SemaphoreType.DMA((xd,)),
            pltpu.SemaphoreType.DMA((1,)),
        ],
        compiler_params=pltpu.CompilerParams(collective_id=10 + top, has_side_effects=True),
    )(chunks)
    out = out.reshape(xd, 2, rows // xd, cols)
    return out[:, 0].reshape(rows, cols), out[:, 1].reshape(rows, cols)


def pcol_kernel(nz, source, x_ref, o_ref, g, p1send, p1recv, p2send, p2recv, p3send, p3recv):
    q = lax.axis_index("pcol")
    p = lax.axis_index("prow")
    nc = lax.axis_size("pcol") // nz
    z = q // nc
    c = lax.rem(q, nc)
    zs, cs = source // nc, source % nc

    def dev(zz, cc):
        return (p, zz * nc + cc)

    barrier = pltpu.get_barrier_semaphore()
    pl.semaphore_signal(barrier, 1, device_id=dev(z, 1 - c), device_id_type=MESH)

    @pl.when(c == cs)
    def _():
        def greet(i, carry):
            pl.semaphore_signal(
                barrier, 1, device_id=dev(lax.rem(z + i, nz), cs), device_id_type=MESH
            )
            return carry

        lax.fori_loop(1, nz, greet, 0)
        pl.semaphore_wait(barrier, nz)

    @pl.when(c != cs)
    def _():
        pl.semaphore_wait(barrier, 1)

    def spread(j):
        return pltpu.make_async_remote_copy(
            src_ref=x_ref.at[j],
            dst_ref=g.at[j],
            send_sem=p1send.at[j],
            recv_sem=p1recv.at[0],
            device_id=dev(j, cs),
            device_id_type=MESH,
        )

    def ring(j, s):
        return pltpu.make_async_remote_copy(
            src_ref=g.at[s],
            dst_ref=g.at[s],
            send_sem=p2send.at[j],
            recv_sem=p2recv.at[s],
            device_id=dev(j, cs),
            device_id_type=MESH,
        )

    def partner(zz):
        return pltpu.make_async_remote_copy(
            src_ref=g,
            dst_ref=g,
            send_sem=p3send.at[0],
            recv_sem=p3recv.at[0],
            device_id=dev(zz, 1 - cs),
            device_id_type=MESH,
        )

    @pl.when(q == source)
    def _():
        def start(i, carry):
            spread(lax.rem(zs + i, nz)).start()
            return carry

        lax.fori_loop(1, nz, start, 0)
        g[zs] = x_ref[zs]

    @pl.when((c == cs) & (z != zs))
    def _():
        spread(z).wait_recv()

    @pl.when(c == cs)
    def _():
        def start(i, carry):
            ring(lax.rem(z + i, nz), z).start()
            return carry

        lax.fori_loop(1, nz, start, 0)

        def wait(i, carry):
            s = lax.rem(z + nz - i, nz)
            ring(s, s).wait_recv()
            ring(lax.rem(z + i, nz), z).wait_send()
            return carry

        lax.fori_loop(1, nz, wait, 0)
        partner(z).start()
        partner(z).wait_send()

    @pl.when(c != cs)
    def _():
        partner(z).wait_recv()

    @pl.when(q == source)
    def _():
        def sent(i, carry):
            spread(lax.rem(zs + i, nz)).wait_send()
            return carry

        lax.fori_loop(1, nz, sent, 0)

    o_ref[...] = g[...]


def pcol_bcast(x, nz, source, collective_id):
    rows, cols = x.shape
    chunks = x.reshape(nz, rows // nz, cols)
    out = pl.pallas_call(
        functools.partial(pcol_kernel, nz, source),
        out_shape=jax.ShapeDtypeStruct(chunks.shape, x.dtype),
        in_specs=[pl.BlockSpec(memory_space=pltpu.VMEM)],
        out_specs=pl.BlockSpec(memory_space=pltpu.VMEM),
        scratch_shapes=[
            pltpu.VMEM(chunks.shape, x.dtype),
            pltpu.SemaphoreType.DMA((nz,)),
            pltpu.SemaphoreType.DMA((1,)),
            pltpu.SemaphoreType.DMA((nz,)),
            pltpu.SemaphoreType.DMA((nz,)),
            pltpu.SemaphoreType.DMA((1,)),
            pltpu.SemaphoreType.DMA((1,)),
        ],
        compiler_params=pltpu.CompilerParams(collective_id=collective_id, has_side_effects=True),
    )(chunks)
    return out.reshape(rows, cols)


def update_kernel(four, rf_ref, cf_ref, a_ref, l_ref, u_ref, o_ref):
    block = l_ref.shape[1]
    for r in range(a_ref.shape[0] // block):
        rows = slice(r * block, (r + 1) * block)
        rb = rf_ref[r]
        below = (rb & 1) == 1
        in_top = (rb & 2) == 2
        lower = l_ref[rows, :]
        results = []
        for c in range(a_ref.shape[1] // block):
            cols = slice(c * block, (c + 1) * block)
            cb = cf_ref[c]
            right = (cb & 1) == 1
            in_panel = (cb & 2) == 2
            a = a_ref[rows, cols]
            upper = u_ref[:, cols]
            product = jnp.dot(lower, upper, preferred_element_type=jnp.float32)
            changed = (a.astype(jnp.float32) - product).astype(a.dtype)
            result = jnp.where(
                below & right,
                changed,
                jnp.where(in_panel & below, lower, jnp.where(in_top & right, upper, a)),
            )
            if four:
                results.append(result)
            else:
                o_ref[rows, cols] = result
        if four:
            o_ref[r] = jnp.stack(results, axis=1)


def trailing_update(a, lower, upper, row_flags, col_flags, out_shape=None):
    smem = pl.BlockSpec(memory_space=pltpu.SMEM)
    vmem = pl.BlockSpec(memory_space=pltpu.VMEM)
    return pl.pallas_call(
        functools.partial(update_kernel, out_shape is not None),
        out_shape=jax.ShapeDtypeStruct(out_shape or a.shape, a.dtype),
        in_specs=[smem, smem, vmem, vmem, vmem],
        out_specs=vmem,
    )(row_flags, col_flags, a, lower, upper)


def local(x_devices, z_chips, matrix, pivots, lower_inverse, upper_inverse):
    row_count = lax.axis_size("prow")
    col_count = lax.axis_size("pcol")
    my_row = lax.axis_index("prow")
    my_col = lax.axis_index("pcol")
    blocks_down, block, blocks_across, _ = matrix.shape
    local_rows = blocks_down * block
    local_cols = blocks_across * block
    current = matrix.reshape(local_rows, local_cols)
    row_place = jnp.arange(local_rows)
    col_place = jnp.arange(local_cols)
    global_rows = (row_place // block * row_count + my_row) * block + row_place % block
    global_cols = (col_place // block * col_count + my_col) * block + col_place % block
    for panel in range(pivots.shape[0]):
        start = panel * block
        chosen = pivots[panel]
        block_row = chosen // block
        is_mine = block_row % row_count == my_row
        local_index = block_row // row_count * block + chosen % block
        safe_index = jnp.where(is_mine, local_index, 0)
        picked = jnp.where(is_mine[:, None], current[safe_index], jnp.zeros((), jnp.bfloat16))
        top_holder = panel % row_count
        top_first = panel // row_count * block
        is_top = my_row == top_holder
        top_local = current[top_first : top_first + block]
        top_part = jnp.where(is_top, top_local, jnp.zeros((), jnp.bfloat16))
        incoming, old_top = prow_sum(picked, top_part, x_devices, top_holder)
        target = jnp.where(is_mine, local_index, local_rows)
        current = current.at[target].set(old_top, mode="drop")
        top_now = current[top_first : top_first + block]
        current = current.at[top_first : top_first + block].set(
            jnp.where(is_top, incoming, top_now)
        )
        panel_holder = panel % col_count
        panel_first = panel // col_count * block
        panel_cols = current[:, panel_first : panel_first + block]
        factor = jnp.dot(
            panel_cols, upper_inverse[panel], preferred_element_type=jnp.float32
        ).astype(jnp.bfloat16)
        is_panel = my_col == panel_holder
        factor = jnp.where(is_panel, factor, jnp.zeros((), jnp.bfloat16))
        lower = pcol_bcast(factor, z_chips, panel_holder, 20 + panel)
        upper = jnp.dot(
            lower_inverse[panel], incoming, preferred_element_type=jnp.float32
        ).astype(jnp.bfloat16)
        row_mask = global_rows >= start + block
        col_mask = global_cols >= start + block
        row_blocks = row_place[::block] // block
        col_blocks = col_place[::block] // block
        below = (row_blocks * row_count + my_row >= panel + 1).astype(jnp.int32)
        right = (col_blocks * col_count + my_col >= panel + 1).astype(jnp.int32)
        in_top = (is_top & (row_blocks == top_first // block)).astype(jnp.int32)
        in_panel = (is_panel & (col_blocks == panel_first // block)).astype(jnp.int32)
        last = panel == pivots.shape[0] - 1
        current = trailing_update(
            current, lower, upper, below + 2 * in_top, right + 2 * in_panel,
            matrix.shape if last else None,
        )
    return current.reshape(matrix.shape)


def solution(mesh):
    x_devices = len({d.coords[0] for d in mesh.devices[:, 0]})
    z_chips = len({d.coords[2] for d in mesh.devices[0, :]})
    in_specs = (P(None, "prow", None, "pcol"), P(), P(), P())
    out_specs = P(None, "prow", None, "pcol")
    return jax.shard_map(functools.partial(local, x_devices, z_chips), mesh=mesh, in_specs=in_specs, out_specs=out_specs, check_vma=False)
```
